128 devices in a mesh: rows: 16 (over y, z), grp: 8 (over x, core).
Axes of the slice: x: 4, y: 4, z: 4, core: 2. Of those that a mesh axis runs over, the one named last changes fastest.
Arguments:
- hamiltonian: float32 [13824, 13824], P(('rows', 'grp')), as said below
- current: float32 [13824, 16], P(('rows', 'grp')), may hold values from -6 to 6
- previous: float32 [13824, 16], P(('rows', 'grp')), may hold values from -6 to 6
Outputs:
- new_current: float32 [13824, 16], P(('rows', 'grp'))
- new_previous: float32 [13824, 16], P(('rows', 'grp'))
- residual_rms: float32 [16], replicated
The draws below stay inside these ranges and needn't reach their ends.
Inputs may be any that keep to these rules, and one draw needn't show every extreme that they name: hamiltonian is symmetric: hamiltonian[i, j] equals hamiltonian[j, i].
All inputs are finite; a program needn't handle non-finite values.
Results may differ from the reference program's by a relative error of at most 0.0003.
Values sent between devices are 32-bit elements; how exact they have to be, the bound alone decides.
No kernel may reach another device: no remote copies, remote signals or barrier semaphores. Data moves between devices by JAX's collectives and lax.ppermute only.
A program may use at most 64 MiB of HBM per device.

```python
import math
import jax
import jax.numpy as jnp
from jax import lax

NEIG = 16
SIGN_STEPS = 6
ORDER = 13824


def draw_hamiltonian(key, part):
    base = jax.random.fold_in(key, 11)
    key_energy, key_kernel = jax.random.split(base)
    energy = jnp.exp(jax.random.uniform(key_energy, (ORDER,), jnp.float32, 0.0, math.log(10.0)))
    coupling = 1.0
    noise = jax.random.normal(key_kernel, (ORDER, ORDER), jnp.float32)
    kernel = (noise + noise.T) * (coupling / math.sqrt(2.0 * ORDER))
    return kernel + jnp.diag(energy)


def steps_of(rng, shape, shards, smallest, largest):
    def one(position, parts):
        draws = jax.random.uniform(jax.random.fold_in(jax.random.fold_in(rng, 6), position), (parts,), jnp.float32, smallest / len(shards), largest / len(shards))
        return jnp.repeat(jnp.exp(draws), shape[position] // parts).reshape((-1,) + (1,) * (len(shape) - position - 1))

    gain = one(*shards[0])
    for cut in shards[1:]:
        gain = gain * one(*cut)
    return gain


def scatter_about(stream_key, extent, spread, bound, shards=(), kind=jnp.bfloat16):
    values = jax.random.normal(stream_key, extent, jnp.float32) * spread
    if len(shards) > 0:
        values = steps_of(stream_key, extent, shards, -0.22, 0.18) * values
    return jnp.clip(values, min=-bound, max=bound).astype(kind)


def setup_inputs(seed: int = 0) -> dict:
    streams_of = jax.random.split(jax.random.key(seed), 4)
    hamiltonian = draw_hamiltonian(jax.random.fold_in(streams_of[3], 71), 0)
    current = scatter_about(streams_of[1], (ORDER, NEIG), 1.0, 6.0, ((0, 128),), jnp.float32)
    previous = scatter_about(streams_of[2], (ORDER, NEIG), 1.0, 6.0, ((0, 128),), jnp.float32)
    return dict(hamiltonian=hamiltonian, current=current, previous=previous)


highest = lax.Precision.HIGHEST
eps_value = 1e-06

def mat_mul(left, right):
    return jnp.dot(left.astype(jnp.float32), right.astype(jnp.float32), precision=highest, preferred_element_type=jnp.float32)

def diag_of(matrix):
    mask = jnp.eye(matrix.shape[0], dtype=matrix.dtype)
    return lax.optimization_barrier(jnp.sum(matrix * mask, axis=1))

def ritz_update(stiff, mass):
    stiff_sym = 0.5 * (stiff + stiff.T)
    lower = jnp.linalg.cholesky(mass)
    half_way = jax.scipy.linalg.solve_triangular(lower, stiff_sym, lower=True)
    reduced = jax.scipy.linalg.solve_triangular(lower, half_way.T, lower=True)
    identity = jnp.eye(reduced.shape[0], dtype=reduced.dtype)
    level = jnp.max(diag_of(reduced)[:NEIG])
    signed = level * identity - reduced
    signed = signed / jnp.sqrt(jnp.sum(signed * signed))
    for sweep_index in range(SIGN_STEPS):
        signed = 1.5 * signed - 0.5 * mat_mul(signed, mat_mul(signed, signed))
    projector = 0.5 * (identity + signed)
    coeffs = jax.scipy.linalg.solve_triangular(lower, projector[:, :NEIG], trans=1, lower=True)
    return coeffs * math.sqrt(ORDER)

def reference(hamiltonian, current, previous):
    diag_vals = diag_of(hamiltonian)
    image = mat_mul(hamiltonian, current)
    ritz = mat_mul(current.T, image) / ORDER
    resid = image - mat_mul(current, ritz)
    residual_rms = jnp.sqrt(lax.optimization_barrier(jnp.sum(resid * resid, axis=0)) / ORDER + eps_value)
    shift = jnp.maximum(jnp.abs(diag_vals[:, None] - diag_of(ritz)[None, :]), 1.0)
    search = resid / (shift * residual_rms[None, :])
    basis = jnp.concatenate([current, search, previous], axis=1)
    himage = mat_mul(hamiltonian, basis)
    stiff = mat_mul(basis.T, himage)
    mass = mat_mul(basis.T, basis)
    coeffs = ritz_update(stiff, mass)
    new_current = mat_mul(basis, coeffs)
    new_previous = mat_mul(basis[:, NEIG:], coeffs[NEIG:])
    return (new_current, new_previous, residual_rms)
```

```python
import math

import jax
import jax.numpy as jnp
from jax import lax
from jax.experimental import pallas as pl
from jax.experimental.pallas import tpu as pltpu
from jax.sharding import Mesh
from jax.sharding import PartitionSpec as P

NEIG = 16
SIGN_STEPS = 6
ORDER = 13824
DEVICES = 128
ROWS = ORDER // DEVICES
CHIPS = DEVICES // 2
LANES = 128
HALF = CHIPS * LANES
TALL = 112
CHUNKS = 4
EPS = 1e-06
ROWS_GRP = ("rows_0", "rows_1", "grp_0", "grp_1")
CHIP_AXES = ("rows_0", "rows_1", "grp_0")
F32, BF16 = jnp.float32, jnp.bfloat16
HIGHEST = lax.Precision.HIGHEST
VMEM = pl.BlockSpec(memory_space=pltpu.VMEM)
LIMIT = 24 << 20


def split3(x):
    high = x.astype(BF16)
    rest = x - high.astype(F32)
    mid = rest.astype(BF16)
    return high, mid, (rest - mid.astype(F32)).astype(BF16)


def nt(left, right):
    return lax.dot_general(left, right, (((1,), (1,)), ((), ())), preferred_element_type=F32)


def nt_exact(left, right):
    return lax.dot_general(left, right, (((1,), (1,)), ((), ())), precision=HIGHEST, preferred_element_type=F32)


def dot_exact(left, right):
    return jnp.dot(left, right, precision=HIGHEST, preferred_element_type=F32)


def fold(parts):
    rows = (parts[32:48] + parts[16:32]) + parts[0:16]
    return (rows[:, 32:48] + rows[:, 16:32]) + rows[:, 0:16]


def fold_rows(product):
    rows = (product[2 * TALL :] + product[TALL : 2 * TALL]) + product[:TALL]
    wide = jnp.concatenate([rows, jnp.zeros((TALL, LANES - 3 * NEIG), F32)], axis=1)
    turned = jnp.concatenate([wide, jnp.zeros((LANES - TALL, LANES), F32)], axis=0).T
    image = (turned[32:48] + turned[16:32]) + turned[0:16]
    lane = lax.broadcasted_iota(jnp.int32, (NEIG, LANES), 1)
    return jnp.where(lane < ROWS, image, 0.0)


def prepare_kernel(h_ref, parts_ref):
    core = lax.axis_index("grp_1")
    step = pl.program_id(0)
    for block in range(2 * CHIPS // CHUNKS):
        chip, owner = divmod(block, 2)
        half = jnp.where(core == owner, 0, 1)
        x = h_ref[:, ROWS * block : ROWS * block + ROWS]
        x = jnp.concatenate([x, jnp.zeros((ROWS, LANES - ROWS), F32)], axis=1)
        lanes = pl.ds(pl.multiple_of(step * (HALF // CHUNKS) + LANES * chip, LANES), LANES)
        for number, part in enumerate(split3(x)):
            parts_ref[half, TALL * number : TALL * number + ROWS, lanes] = part


def prepare(hamiltonian):
    width = ORDER // CHUNKS
    return pl.pallas_call(
        prepare_kernel,
        grid=(CHUNKS,),
        out_shape=jax.ShapeDtypeStruct((2, 3 * TALL, HALF), BF16),
        in_specs=[pl.BlockSpec((ROWS, width), lambda i: (0, i))],
        out_specs=VMEM,
        compiler_params=pltpu.CompilerParams(vmem_limit_bytes=LIMIT),
        cost_estimate=pl.CostEstimate(flops=20 * ROWS * ORDER, bytes_accessed=10 * ROWS * ORDER, transcendentals=0),
        name="prepare",
    )(hamiltonian)


def take_parts(block_ref, parts_ref, half):
    for chip in range(CHIPS):
        for number, part in enumerate(split3(block_ref[chip, 0:NEIG])):
            parts_ref[half, NEIG * number : NEIG * (number + 1), LANES * chip : LANES * (chip + 1)] = part


def image_kernel(h_ref, own_ref, other_ref, image_ref, sent_ref, parts_ref):
    take_parts(own_ref, parts_ref, 0)
    product = nt(h_ref[0], parts_ref[0])
    take_parts(other_ref, parts_ref, 1)
    image = fold_rows(product + nt(h_ref[1], parts_ref[1]))
    image_ref[...] = image
    for chip in range(CHIPS):
        sent_ref[chip] = image


def previous_kernel(h_ref, own_ref, other_ref, c_ref, image_ref, parts_ref, gram_ref):
    take_parts(own_ref, parts_ref, 0)
    take_parts(other_ref, parts_ref, 1)
    image_ref[...] = fold_rows(nt(h_ref[0], parts_ref[0]) + nt(h_ref[1], parts_ref[1]))
    gram_ref[0] = fold(nt(c_ref[0], c_ref[0]) + nt(c_ref[1], c_ref[1]))
    gram_ref[1] = fold(nt(parts_ref[0], c_ref[0]) + nt(parts_ref[1], c_ref[1]))
    gram_ref[2] = fold(nt(parts_ref[0], parts_ref[0]) + nt(parts_ref[1], parts_ref[1]))


def search_kernel(
    h_ref, own_ref, other_ref, p_own_ref, p_other_ref, c_ref, pvec_ref, pimage_ref,
    search_ref, rms_ref, cross_ref, sent_ref, i_ref, s_ref, resid_ref,
):
    chip_here = (lax.axis_index("rows_0") * 4 + lax.axis_index("rows_1")) * 4 + lax.axis_index("grp_0")
    take_parts(own_ref, i_ref, 0)
    take_parts(other_ref, i_ref, 1)
    cross_t = fold(nt(i_ref[0], c_ref[0]) + nt(i_ref[1], c_ref[1]))
    cross_ref[...] = cross_t
    ritz_t = cross_t / ORDER
    stacked = jnp.concatenate(split3(ritz_t), axis=0)
    stacked = jnp.concatenate([stacked, stacked, stacked], axis=1)
    square = jnp.zeros((NEIG, LANES), F32)
    for half, ref in ((0, own_ref), (1, other_ref)):
        moved = jnp.dot(stacked, c_ref[half], preferred_element_type=F32)
        moved = (moved[32:48] + moved[16:32]) + moved[0:16]
        part = jnp.zeros((NEIG, LANES), F32)
        for chip in range(CHIPS):
            lanes = slice(LANES * chip, LANES * (chip + 1))
            resid = ref[chip] - moved[:, lanes]
            resid_ref[half, :, lanes] = resid
            part = part + resid * resid
        square = square + part
    rms = jnp.sqrt(jnp.sum(square, axis=1, keepdims=True) / ORDER + EPS)
    rms_ref[...] = rms
    row = lax.broadcasted_iota(jnp.int32, (NEIG, NEIG), 0)
    column = lax.broadcasted_iota(jnp.int32, (NEIG, NEIG), 1)
    value = jnp.sum(jnp.where(row == column, ritz_t, 0.0), axis=1, keepdims=True)
    value = jnp.broadcast_to(value, (NEIG, LANES))
    rms = jnp.broadcast_to(rms, (NEIG, LANES))

    def scaled(resid, diag):
        diag = jnp.concatenate([diag, diag], axis=0)
        return resid / (jnp.maximum(jnp.abs(diag - value), 1.0) * rms)

    product = jnp.zeros((3 * TALL, 3 * NEIG), F32)
    for half, ref in ((0, p_own_ref), (1, p_other_ref)):
        for chip in range(CHIPS):
            lanes = slice(LANES * chip, LANES * (chip + 1))
            search = scaled(resid_ref[half, :, lanes], ref[chip, NEIG : NEIG + 8])
            for number, part in enumerate(split3(search)):
                s_ref[half, NEIG * number : NEIG * (number + 1), lanes] = part
        product = product + nt(h_ref[half], s_ref[half])
    simage = fold_rows(product)
    lanes = pl.ds(pl.multiple_of(chip_here * LANES, LANES), LANES)
    search = scaled(resid_ref[0, :, lanes], p_own_ref[chip_here, NEIG : NEIG + 8])
    search_ref[...] = search
    pvec = pvec_ref[...]
    terms = jnp.concatenate(
        [nt_exact(simage, search), nt_exact(simage, pvec), nt_exact(pimage_ref[...], pvec), jnp.zeros((NEIG, NEIG), F32)],
        axis=1,
    )
    packed = jnp.concatenate([terms[0:8], terms[8:16]], axis=1)
    for chip in range(CHIPS):
        sent_ref[chip] = packed


def factor_kernel(s_ref, c_ref, p_ref, i_ref, gram_ref, cross_ref, inverse_ref, stiff_ref):
    def gram(left, right):
        return fold(nt(left[0], right[0]) + nt(left[1], right[1]))

    empty = jnp.zeros((NEIG, NEIG), F32)
    cc, pc, pp = gram_ref[0], gram_ref[1], gram_ref[2]
    sc, ss, ps = gram(s_ref, c_ref), gram(s_ref, s_ref), gram(p_ref, s_ref)
    low = jnp.concatenate(
        [
            jnp.concatenate([0.5 * cc, empty, empty], axis=1),
            jnp.concatenate([sc, 0.5 * ss, empty], axis=1),
            jnp.concatenate([pc, ps, 0.5 * pp], axis=1),
        ],
        axis=0,
    )
    mass = low + low.T
    low = jnp.concatenate(
        [
            jnp.concatenate([0.5 * cross_ref[...], empty, empty], axis=1),
            jnp.concatenate([gram(s_ref, i_ref), empty, empty], axis=1),
            jnp.concatenate([gram(p_ref, i_ref), empty, empty], axis=1),
        ],
        axis=0,
    )
    stiff_ref[...] = low + low.T
    size = 3 * NEIG
    row = lax.broadcasted_iota(jnp.int32, (size, size), 0)
    column = lax.broadcasted_iota(jnp.int32, (size, size), 1)
    identity = jnp.where(row == column, 1.0, 0.0).astype(F32)
    work = jnp.concatenate([mass, identity], axis=1)
    below = lax.broadcasted_iota(jnp.int32, (size, 1), 0)
    for k in range(size):
        factor = jnp.where(below > k, work[:, k : k + 1] / work[k : k + 1, k : k + 1], 0.0)
        work = work - factor * work[k : k + 1, :]
    pivots = jnp.sum(work[:, :size] * identity, axis=1, keepdims=True)
    inverse_ref[...] = work[:, size:] / jnp.sqrt(pivots)


def finish_kernel(inverse_ref, stiff_ref, own_ref, other_ref, c_ref, s_ref, p_ref, current_ref, previous_ref):
    size = 3 * NEIG
    total = own_ref[0] + other_ref[0]
    for chip in range(1, CHIPS):
        total = total + (own_ref[chip] + other_ref[chip])
    terms = jnp.concatenate([total[:, 0 : 3 * NEIG], total[:, 4 * NEIG : 7 * NEIG]], axis=0)
    ss, sp, pp = terms[:, 0:16], terms[:, 16:32], terms[:, 32:48]
    empty = jnp.zeros((NEIG, NEIG), F32)
    up = jnp.concatenate(
        [
            jnp.zeros((NEIG, size), F32),
            jnp.concatenate([empty, 0.5 * ss, sp], axis=1),
            jnp.concatenate([empty, empty, 0.5 * pp], axis=1),
        ],
        axis=0,
    )
    stiff = stiff_ref[...] + (up + up.T)
    inverse = inverse_ref[...]
    reduced = nt_exact(dot_exact(inverse, stiff), inverse)
    row = lax.broadcasted_iota(jnp.int32, (size, size), 0)
    column = lax.broadcasted_iota(jnp.int32, (size, size), 1)
    identity = jnp.where(row == column, 1.0, 0.0).astype(F32)
    diagonal = jnp.sum(reduced * identity, axis=1, keepdims=True)
    level = jnp.max(diagonal[:NEIG], axis=0, keepdims=True)
    signed = level * identity - reduced
    norm = jnp.sqrt(jnp.sum(jnp.sum(signed * signed, axis=1, keepdims=True), axis=0, keepdims=True))
    signed = signed / norm
    for _ in range(SIGN_STEPS):
        signed = 1.5 * signed - 0.5 * dot_exact(signed, dot_exact(signed, signed))
    projector = 0.5 * (identity + signed)
    wanted = jnp.where(lax.broadcasted_iota(jnp.int32, (size, size), 1) < NEIG, projector, 0.0)
    tn = (((0,), (0,)), ((), ()))
    coeffs_t = lax.dot_general(wanted, inverse, tn, precision=HIGHEST, preferred_element_type=F32)[0:NEIG]
    coeffs_t = coeffs_t * math.sqrt(ORDER)
    basis = jnp.concatenate([c_ref[...], s_ref[...], p_ref[...]], axis=0)
    current_ref[...] = dot_exact(coeffs_t, basis)[:, :ROWS]
    lane = lax.broadcasted_iota(jnp.int32, (NEIG, size), 1)
    previous_ref[...] = dot_exact(jnp.where(lane < NEIG, 0.0, coeffs_t), basis)[:, :ROWS]


def kernel_call(body, outs, args, flops, name, scratch=()):
    return pl.pallas_call(
        body,
        out_shape=[jax.ShapeDtypeStruct(shape, kind) for shape, kind in outs],
        in_specs=[VMEM] * len(args),
        out_specs=[VMEM] * len(outs),
        scratch_shapes=scratch,
        compiler_params=pltpu.CompilerParams(vmem_limit_bytes=LIMIT),
        cost_estimate=pl.CostEstimate(flops=flops, bytes_accessed=4 << 20, transcendentals=0),
        name=name,
    )(*args)


def to_chips(x):
    return lax.all_to_all(x, CHIP_AXES, 0, 0, tiled=True)


def to_core(x):
    return lax.ppermute(x, "grp_1", [(0, 1), (1, 0)])


def body(hamiltonian, current, previous):
    device = lax.axis_index(ROWS_GRP)
    cvec = jnp.pad(current.T, ((0, 0), (0, LANES - ROWS)))
    c_own = to_chips(jnp.broadcast_to(cvec[None], (CHIPS, NEIG, LANES)))
    own_block = lax.dynamic_slice_in_dim(hamiltonian, device * ROWS, ROWS, 1)
    diag = jnp.sum(own_block * jnp.eye(ROWS, dtype=F32), axis=0)
    pvec = jnp.pad(previous.T, ((0, 0), (0, LANES - ROWS)))
    diag_rows = jnp.broadcast_to(jnp.pad(diag, (0, LANES - ROWS))[None], (8, LANES))
    with_diag = jnp.concatenate([pvec, diag_rows], axis=0)
    p_own = to_chips(jnp.broadcast_to(with_diag[None], (CHIPS, NEIG + 8, LANES)))
    h_parts = prepare(hamiltonian)
    c_other = to_core(c_own)
    block, parts = ((NEIG, LANES), F32), ((2, 3 * NEIG, HALF), BF16)
    image, sent, c_parts = kernel_call(
        image_kernel, [block, ((CHIPS, NEIG, LANES), F32), parts], (h_parts, c_own, c_other), 6 << 30, "image"
    )
    i_own = to_chips(sent)
    p_other = to_core(p_own)
    p_image, p_parts, grams = kernel_call(
        previous_kernel,
        [block, parts, ((3, NEIG, NEIG), F32)],
        (h_parts, p_own, p_other, c_parts),
        6 << 30,
        "previous",
    )
    i_other = to_core(i_own)
    search, rms, cross, sent, i_parts, s_parts = kernel_call(
        search_kernel,
        [block, ((NEIG, 1), F32), ((NEIG, NEIG), F32), ((CHIPS, 8, LANES), F32), parts, parts],
        (h_parts, i_own, i_other, p_own, p_other, c_parts, pvec, p_image),
        6 << 30,
        "search",
        scratch=[pltpu.VMEM((2, NEIG, HALF), F32)],
    )
    r_own = to_chips(sent)
    square = ((3 * NEIG, 3 * NEIG), F32)
    inverse, stiff = kernel_call(
        factor_kernel, [square, square], (s_parts, c_parts, p_parts, i_parts, grams, cross), 6 << 30, "factor"
    )
    r_other = to_core(r_own)
    new_current, new_previous = kernel_call(
        finish_kernel,
        [((NEIG, ROWS), F32)] * 2,
        (inverse, stiff, r_own, r_other, cvec, search, pvec),
        1 << 28,
        "finish",
    )
    return new_current.T, new_previous.T, rms.reshape(NEIG)


def solution(mesh):
    finer = Mesh(mesh.devices.reshape(4, 4, 4, 2), ROWS_GRP)
    return jax.shard_map(
        body,
        mesh=finer,
        in_specs=(P(ROWS_GRP, None), P(ROWS_GRP, None), P(ROWS_GRP, None)),
        out_specs=(P(ROWS_GRP, None), P(ROWS_GRP, None), P()),
        check_vma=False,
    )
```

```python
import math

import jax
import jax.numpy as jnp
from jax import lax
from jax.experimental import pallas as pl
from jax.experimental.pallas import tpu as pltpu
from jax.sharding import Mesh
from jax.sharding import PartitionSpec as P

NEIG = 16
SIGN_STEPS = 6
ORDER = 13824
DEVICES = 128
ROWS = ORDER // DEVICES
CHIPS = DEVICES // 2
LANES = 128
HALF = CHIPS * LANES
TALL = 112
CHUNKS = 4
EPS = 1e-06
ROWS_GRP = ("rows_0", "rows_1", "grp_0", "grp_1")
CHIP_AXES = ("rows_0", "rows_1", "grp_0")
F32, BF16 = jnp.float32, jnp.bfloat16
HIGHEST = lax.Precision.HIGHEST
VMEM = pl.BlockSpec(memory_space=pltpu.VMEM)
HBM = pl.BlockSpec(memory_space=pltpu.HBM)
LIMIT = 48 << 20
PARTS = 2
STACK = PARTS * NEIG
SPARE = ROWS


def split(x):
    high = x.astype(BF16)
    return high, (x - high.astype(F32)).astype(BF16)


def split3(x):
    high = x.astype(BF16)
    rest = x - high.astype(F32)
    mid = rest.astype(BF16)
    return high, mid, (rest - mid.astype(F32)).astype(BF16)


def nt(left, right):
    return lax.dot_general(left, right, (((1,), (1,)), ((), ())), preferred_element_type=F32)


def nt_exact(left, right):
    return lax.dot_general(left, right, (((1,), (1,)), ((), ())), precision=HIGHEST, preferred_element_type=F32)


def dot_exact(left, right):
    return jnp.dot(left, right, precision=HIGHEST, preferred_element_type=F32)


def fold(parts):
    rows = parts[16:32] + parts[0:16]
    return rows[:, 16:32] + rows[:, 0:16]


def fold_rows(product):
    rows = product[TALL:] + product[:TALL]
    wide = jnp.concatenate([rows, jnp.zeros((TALL, LANES - STACK), F32)], axis=1)
    turned = jnp.concatenate([wide, jnp.zeros((LANES - TALL, LANES), F32)], axis=0).T
    return real_lanes(turned[16:32] + turned[0:16])


def real_lanes(tile):
    lane = lax.broadcasted_iota(jnp.int32, tile.shape, 1)
    return jnp.where(lane < ROWS, tile, 0.0)


def padded(tile):
    return jnp.concatenate([tile, jnp.zeros((tile.shape[0], LANES - ROWS), F32)], axis=1)


def prepare_kernel(h_ref, parts_ref):
    core = lax.axis_index("grp_1")
    for block in range(2 * CHIPS // CHUNKS):
        chip, owner = divmod(block, 2)
        half = jnp.where(core == owner, 0, 1)
        x = padded(h_ref[:, ROWS * block : ROWS * block + ROWS])
        for number, part in enumerate(split(x)):
            parts_ref[half, TALL * number : TALL * number + ROWS, LANES * chip : LANES * (chip + 1)] = part


def prepare(hamiltonian):
    width, out = ORDER // CHUNKS, HALF // CHUNKS
    return pl.pallas_call(
        prepare_kernel,
        grid=(CHUNKS,),
        out_shape=jax.ShapeDtypeStruct((2, PARTS * TALL, HALF), BF16),
        in_specs=[pl.BlockSpec((ROWS, width), lambda i: (0, i))],
        out_specs=pl.BlockSpec((2, PARTS * TALL, out), lambda i: (0, 0, i)),
        compiler_params=pltpu.CompilerParams(vmem_limit_bytes=58 << 20),
        cost_estimate=pl.CostEstimate(flops=20 * ROWS * ORDER, bytes_accessed=10 * ROWS * ORDER, transcendentals=0),
        name="prepare",
    )(hamiltonian)


def take_parts(tile_of, parts_ref):
    for chip in range(CHIPS):
        for number, part in enumerate(split(tile_of(chip))):
            parts_ref[NEIG * number : NEIG * (number + 1), LANES * chip : LANES * (chip + 1)] = part


def image_own_kernel(h_ref, own_ref, product_ref, own_out, h_vmem, parts, sems):
    copy = pltpu.make_async_copy(h_ref.at[0], h_vmem, sems.at[0])
    copy.start()
    keep = pltpu.make_async_copy(own_ref, own_out, sems.at[1])
    keep.start()
    take_parts(lambda chip: padded(own_ref[chip, 0:NEIG]), parts)
    copy.wait()
    product_ref[...] = nt(h_vmem[...], parts[...])
    keep.wait()


def image_other_kernel(h_ref, other_ref, product_ref, tile_ref, image_ref, sent_ref, other_out, h_vmem, parts, sems):
    copy = pltpu.make_async_copy(h_ref.at[1], h_vmem, sems.at[0])
    copy.start()
    keep = pltpu.make_async_copy(other_ref, other_out, sems.at[1])
    keep.start()
    take_parts(lambda chip: padded(other_ref[chip, 0:NEIG]), parts)
    copy.wait()
    image = fold_rows(product_ref[...] + nt(h_vmem[...], parts[...]))
    image_ref[...] = image
    sent = image + tile_ref[...]
    for chip in range(CHIPS):
        sent_ref[chip] = sent
    keep.wait()


def previous_kernel(h_ref, own_ref, other_ref, image_ref, c_out, p_out, gram_ref, h_vmem, c_ref, p_ref, sems):
    copy = pltpu.make_async_copy(h_ref, h_vmem, sems.at[0])
    copy.start()
    for half, ref in ((0, own_ref), (1, other_ref)):
        take_parts(lambda chip: padded(ref[chip, 0:NEIG]), c_ref.at[half])
        take_parts(lambda chip: padded(ref[chip, NEIG : 2 * NEIG]), p_ref.at[half])
    out_c = pltpu.make_async_copy(c_ref, c_out, sems.at[1])
    out_p = pltpu.make_async_copy(p_ref, p_out, sems.at[2])
    out_c.start()
    out_p.start()
    gram_ref[0] = fold(nt(c_ref[0], c_ref[0]) + nt(c_ref[1], c_ref[1]))
    gram_ref[1] = fold(nt(p_ref[0], c_ref[0]) + nt(p_ref[1], c_ref[1]))
    gram_ref[2] = fold(nt(p_ref[0], p_ref[0]) + nt(p_ref[1], p_ref[1]))
    copy.wait()
    image_ref[...] = fold_rows(nt(h_vmem[0], p_ref[0]) + nt(h_vmem[1], p_ref[1]))
    out_c.wait()
    out_p.wait()


def diagonal_of(tile):
    row = lax.broadcasted_iota(jnp.int32, (NEIG, LANES), 0)
    lane = lax.broadcasted_iota(jnp.int32, (NEIG, LANES), 1)
    spread = jnp.take_along_axis(tile, SPARE + lane // NEIG, axis=1)
    return jnp.sum(jnp.where(lane % NEIG == row, spread, 0.0), axis=0, keepdims=True)


def search_kernel(
    h_ref, own_ref, other_ref, c_hbm, cvec_ref, pvec_ref, pimage_ref, image_ref, tile_ref,
    search_ref, rms_ref, cross_ref, sent_ref, s_out, i_out,
    h_vmem, c_ref, i_ref, s_ref, resid_ref, sems,
):
    copy_c = pltpu.make_async_copy(c_hbm, c_ref, sems.at[0])
    copy_c.start()
    copy_h = pltpu.make_async_copy(h_ref, h_vmem, sems.at[1])
    copy_h.start()
    take_parts(lambda chip: real_lanes(own_ref[chip]), i_ref.at[0])
    take_parts(lambda chip: real_lanes(other_ref[chip]), i_ref.at[1])
    out_i = pltpu.make_async_copy(i_ref, i_out, sems.at[3])
    out_i.start()
    copy_c.wait()
    cross_t = fold(nt(i_ref[0], c_ref[0]) + nt(i_ref[1], c_ref[1]))
    cross_ref[...] = cross_t
    ritz_t = cross_t / ORDER
    stacked = jnp.concatenate(split3(ritz_t), axis=0)
    stacked = jnp.concatenate([stacked] * PARTS, axis=1)
    square = jnp.zeros((NEIG, LANES), F32)
    for half, ref in ((0, own_ref), (1, other_ref)):
        moved = jnp.dot(stacked, c_ref[half], preferred_element_type=F32)
        moved = (moved[32:48] + moved[16:32]) + moved[0:16]
        part = jnp.zeros((NEIG, LANES), F32)
        for chip in range(CHIPS):
            lanes = slice(LANES * chip, LANES * (chip + 1))
            resid = real_lanes(ref[chip]) - moved[:, lanes]
            resid_ref[half, :, lanes] = resid
            part = part + resid * resid
        square = square + part
    rms = jnp.sqrt(jnp.sum(square, axis=1, keepdims=True) / ORDER + EPS)
    rms_ref[...] = rms
    row = lax.broadcasted_iota(jnp.int32, (NEIG, NEIG), 0)
    column = lax.broadcasted_iota(jnp.int32, (NEIG, NEIG), 1)
    value = jnp.sum(jnp.where(row == column, ritz_t, 0.0), axis=1, keepdims=True)
    value = jnp.broadcast_to(value, (NEIG, LANES))
    rms = jnp.broadcast_to(rms, (NEIG, LANES))

    def scaled(resid, tile):
        return resid / (jnp.maximum(jnp.abs(diagonal_of(tile) - value), 1.0) * rms)

    resid = image_ref[...] - dot_exact(ritz_t, cvec_ref[...])
    search = scaled(resid, tile_ref[...])
    search_ref[...] = search
    for half, ref in ((0, own_ref), (1, other_ref)):
        take_parts(lambda chip: scaled(resid_ref[half, :, LANES * chip : LANES * (chip + 1)], ref[chip]), s_ref.at[half])
    out_s = pltpu.make_async_copy(s_ref, s_out, sems.at[2])
    out_s.start()
    copy_h.wait()
    simage = fold_rows(nt(h_vmem[0], s_ref[0]) + nt(h_vmem[1], s_ref[1]))
    pvec = pvec_ref[...]
    terms = jnp.concatenate(
        [nt_exact(simage, search), nt_exact(simage, pvec), nt_exact(pimage_ref[...], pvec), jnp.zeros((NEIG, NEIG), F32)],
        axis=1,
    )
    packed = jnp.concatenate([terms[0:8], terms[8:16]], axis=1)
    for chip in range(CHIPS):
        sent_ref[chip] = packed
    out_s.wait()
    out_i.wait()


def factor_kernel(
    s_hbm, c_hbm, p_hbm, i_hbm, gram_ref, cross_ref, inverse_ref, stiff_ref,
    s_ref, c_ref, p_ref, i_ref, sems,
):
    pairs = ((s_hbm, s_ref), (c_hbm, c_ref), (p_hbm, p_ref), (i_hbm, i_ref))
    copies = [pltpu.make_async_copy(a, b, sems.at[n]) for n, (a, b) in enumerate(pairs)]
    for copy in copies:
        copy.start()
    for copy in copies:
        copy.wait()

    def gram(left, right):
        return fold(nt(left[0], right[0]) + nt(left[1], right[1]))

    empty = jnp.zeros((NEIG, NEIG), F32)
    cc, pc, pp = gram_ref[0], gram_ref[1], gram_ref[2]
    sc, ss, ps = gram(s_ref, c_ref), gram(s_ref, s_ref), gram(p_ref, s_ref)
    low = jnp.concatenate(
        [
            jnp.concatenate([0.5 * cc, empty, empty], axis=1),
            jnp.concatenate([sc, 0.5 * ss, empty], axis=1),
            jnp.concatenate([pc, ps, 0.5 * pp], axis=1),
        ],
        axis=0,
    )
    mass = low + low.T
    low = jnp.concatenate(
        [
            jnp.concatenate([0.5 * cross_ref[...], empty, empty], axis=1),
            jnp.concatenate([gram(s_ref, i_ref), empty, empty], axis=1),
            jnp.concatenate([gram(p_ref, i_ref), empty, empty], axis=1),
        ],
        axis=0,
    )
    stiff_ref[...] = low + low.T
    size = 3 * NEIG
    row = lax.broadcasted_iota(jnp.int32, (size, size), 0)
    column = lax.broadcasted_iota(jnp.int32, (size, size), 1)
    identity = jnp.where(row == column, 1.0, 0.0).astype(F32)
    work = jnp.concatenate([mass, identity], axis=1)
    below = lax.broadcasted_iota(jnp.int32, (size, 1), 0)
    for k in range(size):
        factor = jnp.where(below > k, work[:, k : k + 1] / work[k : k + 1, k : k + 1], 0.0)
        work = work - factor * work[k : k + 1, :]
    pivots = jnp.sum(work[:, :size] * identity, axis=1, keepdims=True)
    inverse_ref[...] = work[:, size:] / jnp.sqrt(pivots)


def finish_kernel(inverse_ref, stiff_ref, own_ref, other_ref, c_ref, s_ref, p_ref, current_ref, previous_ref):
    size = 3 * NEIG
    total = own_ref[0] + other_ref[0]
    for chip in range(1, CHIPS):
        total = total + (own_ref[chip] + other_ref[chip])
    terms = jnp.concatenate([total[:, 0 : 3 * NEIG], total[:, 4 * NEIG : 7 * NEIG]], axis=0)
    ss, sp, pp = terms[:, 0:16], terms[:, 16:32], terms[:, 32:48]
    empty = jnp.zeros((NEIG, NEIG), F32)
    up = jnp.concatenate(
        [
            jnp.zeros((NEIG, size), F32),
            jnp.concatenate([empty, 0.5 * ss, sp], axis=1),
            jnp.concatenate([empty, empty, 0.5 * pp], axis=1),
        ],
        axis=0,
    )
    stiff = stiff_ref[...] + (up + up.T)
    inverse = inverse_ref[...]
    reduced = nt_exact(dot_exact(inverse, stiff), inverse)
    row = lax.broadcasted_iota(jnp.int32, (size, size), 0)
    column = lax.broadcasted_iota(jnp.int32, (size, size), 1)
    identity = jnp.where(row == column, 1.0, 0.0).astype(F32)
    diagonal = jnp.sum(reduced * identity, axis=1, keepdims=True)
    level = jnp.max(diagonal[:NEIG], axis=0, keepdims=True)
    signed = level * identity - reduced
    norm = jnp.sqrt(jnp.sum(jnp.sum(signed * signed, axis=1, keepdims=True), axis=0, keepdims=True))
    signed = signed / norm
    for _ in range(SIGN_STEPS):
        signed = 1.5 * signed - 0.5 * dot_exact(signed, dot_exact(signed, signed))
    projector = 0.5 * (identity + signed)
    wanted = jnp.where(lax.broadcasted_iota(jnp.int32, (size, size), 1) < NEIG, projector, 0.0)
    tn = (((0,), (0,)), ((), ()))
    coeffs_t = lax.dot_general(wanted, inverse, tn, precision=HIGHEST, preferred_element_type=F32)[0:NEIG]
    coeffs_t = coeffs_t * math.sqrt(ORDER)
    basis = jnp.concatenate([c_ref[...], s_ref[...], p_ref[...]], axis=0)
    current_ref[...] = dot_exact(coeffs_t, basis)[:, :ROWS]
    lane = lax.broadcasted_iota(jnp.int32, (NEIG, size), 1)
    previous_ref[...] = dot_exact(jnp.where(lane < NEIG, 0.0, coeffs_t), basis)[:, :ROWS]


def kernel_call(body, outs, args, flops, name, scratch=(), in_hbm=(), out_hbm=(), limit=LIMIT):
    return pl.pallas_call(
        body,
        out_shape=[jax.ShapeDtypeStruct(shape, kind) for shape, kind in outs],
        in_specs=[HBM if n in in_hbm else VMEM for n in range(len(args))],
        out_specs=[HBM if n in out_hbm else VMEM for n in range(len(outs))],
        scratch_shapes=scratch,
        compiler_params=pltpu.CompilerParams(vmem_limit_bytes=limit),
        cost_estimate=pl.CostEstimate(flops=flops, bytes_accessed=4 << 20, transcendentals=0),
        name=name,
    )(*args)


def to_chips(x):
    return lax.all_to_all(x, CHIP_AXES, 0, 0, tiled=True)


def to_core(x):
    return lax.ppermute(x, "grp_1", [(0, 1), (1, 0)])


def diagonal_tile(hamiltonian):
    device = lax.axis_index(ROWS_GRP)
    own_block = lax.dynamic_slice_in_dim(hamiltonian, device * ROWS, ROWS, 1)
    index = jnp.arange(ROWS)
    diag = jnp.sum(jnp.where(index[:, None] == index[None, :], own_block, 0.0), axis=0)
    rows = jnp.where(index[None, :] % NEIG == jnp.arange(NEIG)[:, None], diag[None, :], 0.0)
    lanes = (jnp.arange(LANES)[None, :] == SPARE + index[:, None] // NEIG).astype(F32)
    return dot_exact(rows, lanes)


def body(hamiltonian, current, previous):
    both = jnp.concatenate([current.T, previous.T], axis=0)
    v_own = to_chips(jnp.broadcast_to(both[None], (CHIPS, 2 * NEIG, ROWS)))
    tile = diagonal_tile(hamiltonian)
    cvec = jnp.pad(current.T, ((0, 0), (0, LANES - ROWS)))
    pvec = jnp.pad(previous.T, ((0, 0), (0, LANES - ROWS)))
    h_parts = prepare(hamiltonian)
    v_own, h_parts, tile = lax.optimization_barrier((v_own, h_parts, tile))
    v_other = to_core(v_own)
    block, parts = ((NEIG, LANES), F32), ((2, STACK, HALF), BF16)
    parts_vmem, h_half = pltpu.VMEM(*parts), pltpu.VMEM((PARTS * TALL, HALF), BF16)
    h_vmem = pltpu.VMEM((2, PARTS * TALL, HALF), BF16)
    half_vmem = pltpu.VMEM((STACK, HALF), BF16)
    whole = ((CHIPS, 2 * NEIG, ROWS), F32)
    product, v_own = kernel_call(
        image_own_kernel, [((PARTS * TALL, STACK), F32), whole], (h_parts, v_own), 1 << 30, "image_own",
        [h_half, half_vmem, pltpu.SemaphoreType.DMA((2,))], (0,), (1,),
    )
    image, sent, v_other = kernel_call(
        image_other_kernel, [block, ((CHIPS, NEIG, LANES), F32), whole], (h_parts, v_other, product, tile), 1 << 30, "image_other",
        [h_half, half_vmem, pltpu.SemaphoreType.DMA((2,))], (0,), (2,),
    )
    i_own = to_chips(sent)
    p_image, c_parts, p_parts, grams = kernel_call(
        previous_kernel,
        [block, parts, parts, ((3, NEIG, NEIG), F32)],
        (h_parts, v_own, v_other),
        6 << 30,
        "previous",
        [h_vmem, parts_vmem, parts_vmem, pltpu.SemaphoreType.DMA((3,))], (0,), (1, 2),
    )
    i_own, p_image, c_parts = lax.optimization_barrier((i_own, p_image, c_parts))
    i_other = to_core(i_own)
    search, rms, cross, sent, s_parts, i_parts = kernel_call(
        search_kernel,
        [block, ((NEIG, 1), F32), ((NEIG, NEIG), F32), ((CHIPS, 8, LANES), F32), parts, parts],
        (h_parts, i_own, i_other, c_parts, cvec, pvec, p_image, image, tile),
        6 << 30,
        "search",
        [h_vmem, parts_vmem, parts_vmem, parts_vmem, pltpu.VMEM((2, NEIG, HALF), F32), pltpu.SemaphoreType.DMA((4,))],
        (0, 3), (4, 5),
    )
    r_own = to_chips(sent)
    square = ((3 * NEIG, 3 * NEIG), F32)
    inverse, stiff = kernel_call(
        factor_kernel, [square, square], (s_parts, c_parts, p_parts, i_parts, grams, cross), 6 << 30, "factor",
        [parts_vmem] * 4 + [pltpu.SemaphoreType.DMA((4,))], (0, 1, 2, 3),
    )
    r_own, inverse = lax.optimization_barrier((r_own, inverse))
    r_other = to_core(r_own)
    new_current, new_previous = kernel_call(
        finish_kernel,
        [((NEIG, ROWS), F32)] * 2,
        (inverse, stiff, r_own, r_other, cvec, search, pvec),
        1 << 28,
        "finish",
        limit=8 << 20,
    )
    return new_current.T, new_previous.T, rms[:, 0]


def solution(mesh):
    finer = Mesh(mesh.devices.reshape(4, 4, 4, 2), ROWS_GRP)
    return jax.shard_map(
        body,
        mesh=finer,
        in_specs=(P(ROWS_GRP, None), P(ROWS_GRP, None), P(ROWS_GRP, None)),
        out_specs=(P(ROWS_GRP, None), P(ROWS_GRP, None), P()),
        check_vma=False,
    )
```

```python
import math

import jax
import jax.numpy as jnp
from jax import lax
from jax.experimental import pallas as pl
from jax.experimental.pallas import tpu as pltpu
from jax.sharding import Mesh
from jax.sharding import PartitionSpec as P

NEIG = 16
SIGN_STEPS = 6
ORDER = 13824
DEVICES = 128
ROWS = ORDER // DEVICES
CHIPS = DEVICES // 2
LANES = 128
HALF = CHIPS * LANES
TALL = 112
CHUNKS = 4
CHUNK = HALF // CHUNKS
EPS = 1e-06
AXIS = "device"
CHIP_ORDER = [[2 * chip + core for chip in reversed(range(CHIPS))] for core in range(2)]
F32, BF16 = jnp.float32, jnp.bfloat16
HIGHEST = lax.Precision.HIGHEST
VMEM = pl.BlockSpec(memory_space=pltpu.VMEM)
HBM = pl.BlockSpec(memory_space=pltpu.HBM)
LIMIT = 53 << 20
LIMIT_IMAGE = 48 << 20
LIMIT_SEARCH = 52 << 20
PARTS = 2
STACK = PARTS * NEIG
SPARE = ROWS


def split(x):
    high = x.astype(BF16)
    return high, (x - high.astype(F32)).astype(BF16)


def split3(x):
    high = x.astype(BF16)
    rest = x - high.astype(F32)
    mid = rest.astype(BF16)
    return high, mid, (rest - mid.astype(F32)).astype(BF16)


def nt(left, right):
    return lax.dot_general(left, right, (((1,), (1,)), ((), ())), preferred_element_type=F32)


def nt_exact(left, right):
    return lax.dot_general(left, right, (((1,), (1,)), ((), ())), precision=HIGHEST, preferred_element_type=F32)


def dot_exact(left, right):
    return jnp.dot(left, right, precision=HIGHEST, preferred_element_type=F32)


def fold(parts):
    rows = parts[16:32] + parts[0:16]
    return rows[:, 16:32] + rows[:, 0:16]


def fold_rows(product):
    rows = product[TALL:] + product[:TALL]
    wide = jnp.concatenate([rows, jnp.zeros((TALL, LANES - STACK), F32)], axis=1)
    turned = jnp.concatenate([wide, jnp.zeros((LANES - TALL, LANES), F32)], axis=0).T
    return real_lanes(turned[16:32] + turned[0:16])


def real_lanes(tile):
    lane = lax.broadcasted_iota(jnp.int32, tile.shape, 1)
    return jnp.where(lane < ROWS, tile, 0.0)


def padded(tile):
    return jnp.concatenate([tile, jnp.zeros((tile.shape[0], LANES - ROWS), F32)], axis=1)


def prepare_kernel(h_ref, parts_ref):
    core = lax.rem(lax.axis_index(AXIS), 2)
    for block in range(2 * CHIPS // CHUNKS):
        chip, owner = divmod(block, 2)
        place = CHIPS // CHUNKS - 1 - chip
        half = jnp.where(core == owner, 0, 1)
        x = padded(h_ref[:, ROWS * block : ROWS * block + ROWS])
        for number, part in enumerate(split(x)):
            parts_ref[half, 0, TALL * number : TALL * number + ROWS, LANES * place : LANES * (place + 1)] = part


def prepare(hamiltonian):
    return pl.pallas_call(
        prepare_kernel,
        grid=(CHUNKS,),
        out_shape=jax.ShapeDtypeStruct((2, CHUNKS, PARTS * TALL, CHUNK), BF16),
        in_specs=[pl.BlockSpec((ROWS, ORDER // CHUNKS), lambda i: (0, i))],
        out_specs=pl.BlockSpec((2, 1, PARTS * TALL, CHUNK), lambda i: (0, CHUNKS - 1 - i, 0, 0)),
        compiler_params=pltpu.CompilerParams(vmem_limit_bytes=58 << 20),
        cost_estimate=pl.CostEstimate(flops=20 * ROWS * ORDER, bytes_accessed=10 * ROWS * ORDER, transcendentals=0),
        name="prepare",
    )(hamiltonian)


def half_copies(h_ref, h_vmem, half, sems):
    copies = [pltpu.make_async_copy(h_ref.at[half, n], h_vmem.at[n], sems.at[n]) for n in range(CHUNKS)]
    for copy in copies:
        copy.start()
    return copies


def times(h_vmem, parts, copies):
    product = None
    for n, copy in enumerate(copies):
        copy.wait()
        term = nt(h_vmem[n], parts[:, CHUNK * n : CHUNK * (n + 1)])
        product = term if product is None else product + term
    return product


def take_parts(tile_of, parts_ref):
    for chip in range(CHIPS):
        for number, part in enumerate(split(tile_of(chip))):
            parts_ref[NEIG * number : NEIG * (number + 1), LANES * chip : LANES * (chip + 1)] = part


def image_own_kernel(h_ref, own_ref, product_ref, h_vmem, parts, sems):
    copies = half_copies(h_ref, h_vmem, 0, sems)
    take_parts(lambda chip: padded(own_ref[chip, 0:NEIG]), parts)
    product_ref[...] = times(h_vmem, parts, copies)


def image_other_kernel(h_ref, other_ref, product_ref, tile_ref, image_ref, sent_ref, h_vmem, parts, sems):
    copies = half_copies(h_ref, h_vmem, 1, sems)
    take_parts(lambda chip: padded(other_ref[chip, 0:NEIG]), parts)
    image = fold_rows(product_ref[...] + times(h_vmem, parts, copies))
    image_ref[...] = image
    sent = image + tile_ref[...]
    for chip in range(CHIPS):
        sent_ref[chip] = sent


def previous_kernel(h_ref, own_ref, other_ref, image_ref, c_out, p_out, gram_ref, h_vmem, c_ref, p_ref, sems, h_sems):
    copies = [half_copies(h_ref, h_vmem.at[half], half, h_sems.at[half]) for half in range(2)]
    for half, ref in ((0, own_ref), (1, other_ref)):
        take_parts(lambda chip: padded(ref[chip, 0:NEIG]), c_ref.at[half])
        take_parts(lambda chip: padded(ref[chip, NEIG : 2 * NEIG]), p_ref.at[half])
    out_c = pltpu.make_async_copy(c_ref, c_out, sems.at[0])
    out_p = pltpu.make_async_copy(p_ref, p_out, sems.at[1])
    out_c.start()
    out_p.start()
    gram_ref[0] = fold(nt(c_ref[0], c_ref[0]) + nt(c_ref[1], c_ref[1]))
    gram_ref[1] = fold(nt(p_ref[0], c_ref[0]) + nt(p_ref[1], c_ref[1]))
    gram_ref[2] = fold(nt(p_ref[0], p_ref[0]) + nt(p_ref[1], p_ref[1]))
    image_ref[...] = fold_rows(times(h_vmem.at[0], p_ref[0], copies[0]) + times(h_vmem.at[1], p_ref[1], copies[1]))
    out_c.wait()
    out_p.wait()


def diagonal_of(tile):
    row = lax.broadcasted_iota(jnp.int32, (NEIG, LANES), 0)
    lane = lax.broadcasted_iota(jnp.int32, (NEIG, LANES), 1)
    spread = jnp.take_along_axis(tile, SPARE + lane // NEIG, axis=1)
    return jnp.sum(jnp.where(lane % NEIG == row, spread, 0.0), axis=0, keepdims=True)


def search_kernel(
    h_ref, own_ref, other_ref, c_hbm, cvec_ref, pvec_ref, pimage_ref, image_ref, tile_ref,
    search_ref, rms_ref, cross_ref, sent_ref, s_out, i_out,
    h_vmem, c_ref, i_ref, s_ref, resid_ref, sems, h_sems,
):
    copy_c = pltpu.make_async_copy(c_hbm, c_ref, sems.at[0])
    copy_c.start()
    copies = [half_copies(h_ref, h_vmem.at[half], half, h_sems.at[half]) for half in range(2)]
    take_parts(lambda chip: real_lanes(own_ref[chip]), i_ref.at[0])
    take_parts(lambda chip: real_lanes(other_ref[chip]), i_ref.at[1])
    out_i = pltpu.make_async_copy(i_ref, i_out, sems.at[1])
    out_i.start()
    copy_c.wait()
    cross_t = fold(nt(i_ref[0], c_ref[0]) + nt(i_ref[1], c_ref[1]))
    cross_ref[...] = cross_t
    ritz_t = cross_t / ORDER
    stacked = jnp.concatenate(split3(ritz_t), axis=0)
    stacked = jnp.concatenate([stacked] * PARTS, axis=1)
    square = jnp.zeros((NEIG, LANES), F32)
    for half, ref in ((0, own_ref), (1, other_ref)):
        moved = jnp.dot(stacked, c_ref[half], preferred_element_type=F32)
        moved = (moved[32:48] + moved[16:32]) + moved[0:16]
        part = jnp.zeros((NEIG, LANES), F32)
        for chip in range(CHIPS):
            lanes = slice(LANES * chip, LANES * (chip + 1))
            resid = real_lanes(ref[chip]) - moved[:, lanes]
            resid_ref[half, :, lanes] = resid
            part = part + resid * resid
        square = square + part
    rms = jnp.sqrt(jnp.sum(square, axis=1, keepdims=True) / ORDER + EPS)
    rms_ref[...] = rms
    row = lax.broadcasted_iota(jnp.int32, (NEIG, NEIG), 0)
    column = lax.broadcasted_iota(jnp.int32, (NEIG, NEIG), 1)
    value = jnp.sum(jnp.where(row == column, ritz_t, 0.0), axis=1, keepdims=True)
    value = jnp.broadcast_to(value, (NEIG, LANES))
    rms = jnp.broadcast_to(rms, (NEIG, LANES))

    def scaled(resid, tile):
        return resid / (jnp.maximum(jnp.abs(diagonal_of(tile) - value), 1.0) * rms)

    resid = image_ref[...] - dot_exact(ritz_t, cvec_ref[...])
    search = scaled(resid, tile_ref[...])
    search_ref[...] = search
    for half, ref in ((0, own_ref), (1, other_ref)):
        take_parts(lambda chip: scaled(resid_ref[half, :, LANES * chip : LANES * (chip + 1)], ref[chip]), s_ref.at[half])
    out_s = pltpu.make_async_copy(s_ref, s_out, sems.at[2])
    out_s.start()
    simage = fold_rows(times(h_vmem.at[0], s_ref[0], copies[0]) + times(h_vmem.at[1], s_ref[1], copies[1]))
    pvec = pvec_ref[...]
    terms = jnp.concatenate(
        [nt_exact(simage, search), nt_exact(simage, pvec), nt_exact(pimage_ref[...], pvec), jnp.zeros((NEIG, NEIG), F32)],
        axis=1,
    )
    packed = jnp.concatenate([terms[0:8], terms[8:16]], axis=1)
    for chip in range(CHIPS):
        sent_ref[chip] = packed
    out_s.wait()
    out_i.wait()


def factor_kernel(
    s_hbm, c_hbm, p_hbm, i_hbm, gram_ref, cross_ref, inverse_ref, stiff_ref,
    s_ref, c_ref, p_ref, i_ref, sems,
):
    pairs = ((s_hbm, s_ref), (c_hbm, c_ref), (p_hbm, p_ref), (i_hbm, i_ref))
    copies = [pltpu.make_async_copy(a, b, sems.at[n]) for n, (a, b) in enumerate(pairs)]
    for copy in copies:
        copy.start()
    for copy in copies:
        copy.wait()

    def gram(left, right):
        return fold(nt(left[0], right[0]) + nt(left[1], right[1]))

    empty = jnp.zeros((NEIG, NEIG), F32)
    cc, pc, pp = gram_ref[0], gram_ref[1], gram_ref[2]
    sc, ss, ps = gram(s_ref, c_ref), gram(s_ref, s_ref), gram(p_ref, s_ref)
    low = jnp.concatenate(
        [
            jnp.concatenate([0.5 * cc, empty, empty], axis=1),
            jnp.concatenate([sc, 0.5 * ss, empty], axis=1),
            jnp.concatenate([pc, ps, 0.5 * pp], axis=1),
        ],
        axis=0,
    )
    mass = low + low.T
    low = jnp.concatenate(
        [
            jnp.concatenate([0.5 * cross_ref[...], empty, empty], axis=1),
            jnp.concatenate([gram(s_ref, i_ref), empty, empty], axis=1),
            jnp.concatenate([gram(p_ref, i_ref), empty, empty], axis=1),
        ],
        axis=0,
    )
    stiff_ref[...] = low + low.T
    size = 3 * NEIG
    row = lax.broadcasted_iota(jnp.int32, (size, size), 0)
    column = lax.broadcasted_iota(jnp.int32, (size, size), 1)
    identity = jnp.where(row == column, 1.0, 0.0).astype(F32)
    work = jnp.concatenate([mass, identity], axis=1)
    below = lax.broadcasted_iota(jnp.int32, (size, 1), 0)
    for k in range(size):
        factor = jnp.where(below > k, work[:, k : k + 1] / work[k : k + 1, k : k + 1], 0.0)
        work = work - factor * work[k : k + 1, :]
    pivots = jnp.sum(work[:, :size] * identity, axis=1, keepdims=True)
    inverse_ref[...] = work[:, size:] / jnp.sqrt(pivots)


def finish_kernel(inverse_ref, stiff_ref, own_ref, other_ref, c_ref, s_ref, p_ref, current_ref, previous_ref):
    size = 3 * NEIG
    total = own_ref[0] + other_ref[0]
    for chip in range(1, CHIPS):
        total = total + (own_ref[chip] + other_ref[chip])
    terms = jnp.concatenate([total[:, 0 : 3 * NEIG], total[:, 4 * NEIG : 7 * NEIG]], axis=0)
    ss, sp, pp = terms[:, 0:16], terms[:, 16:32], terms[:, 32:48]
    empty = jnp.zeros((NEIG, NEIG), F32)
    up = jnp.concatenate(
        [
            jnp.zeros((NEIG, size), F32),
            jnp.concatenate([empty, 0.5 * ss, sp], axis=1),
            jnp.concatenate([empty, empty, 0.5 * pp], axis=1),
        ],
        axis=0,
    )
    stiff = stiff_ref[...] + (up + up.T)
    inverse = inverse_ref[...]
    reduced = nt_exact(dot_exact(inverse, stiff), inverse)
    row = lax.broadcasted_iota(jnp.int32, (size, size), 0)
    column = lax.broadcasted_iota(jnp.int32, (size, size), 1)
    identity = jnp.where(row == column, 1.0, 0.0).astype(F32)
    diagonal = jnp.sum(reduced * identity, axis=1, keepdims=True)
    level = jnp.max(diagonal[:NEIG], axis=0, keepdims=True)
    signed = level * identity - reduced
    square = dot_exact(signed, signed)
    total = jnp.sum(jnp.sum(signed * signed, axis=1, keepdims=True), axis=0, keepdims=True)
    square = square / total
    signed = signed / jnp.sqrt(total)
    for step in range(SIGN_STEPS):
        if step > 0:
            square = dot_exact(signed, signed)
        signed = dot_exact(signed, 1.5 * identity - 0.5 * square)
    projector = 0.5 * (identity + signed)
    wanted = jnp.where(lax.broadcasted_iota(jnp.int32, (size, size), 1) < NEIG, projector, 0.0)
    tn = (((0,), (0,)), ((), ()))
    coeffs_t = lax.dot_general(wanted, inverse, tn, precision=HIGHEST, preferred_element_type=F32)[0:NEIG]
    coeffs_t = coeffs_t * math.sqrt(ORDER)
    basis = jnp.concatenate([c_ref[...], s_ref[...], p_ref[...]], axis=0)
    current_ref[...] = dot_exact(coeffs_t, basis)[:, :ROWS]
    lane = lax.broadcasted_iota(jnp.int32, (NEIG, size), 1)
    previous_ref[...] = dot_exact(jnp.where(lane < NEIG, 0.0, coeffs_t), basis)[:, :ROWS]


def kernel_call(body, outs, args, flops, name, scratch=(), in_hbm=(), out_hbm=(), limit=LIMIT):
    return pl.pallas_call(
        body,
        out_shape=[jax.ShapeDtypeStruct(shape, kind) for shape, kind in outs],
        in_specs=[HBM if n in in_hbm else VMEM for n in range(len(args))],
        out_specs=[HBM if n in out_hbm else VMEM for n in range(len(outs))],
        scratch_shapes=scratch,
        compiler_params=pltpu.CompilerParams(vmem_limit_bytes=limit),
        cost_estimate=pl.CostEstimate(flops=flops, bytes_accessed=4 << 20, transcendentals=0),
        name=name,
    )(*args)


def to_chips(x):
    return lax.all_to_all(x, AXIS, 0, 0, axis_index_groups=CHIP_ORDER, tiled=True)


def to_core(x):
    return lax.ppermute(x, AXIS, [(device, device ^ 1) for device in range(DEVICES)])


def diagonal_tile(hamiltonian):
    device = lax.axis_index(AXIS)
    own_block = lax.dynamic_slice_in_dim(hamiltonian, device * ROWS, ROWS, 1)
    index = jnp.arange(ROWS)
    diag = jnp.sum(jnp.where(index[:, None] == index[None, :], own_block, 0.0), axis=0)
    rows = jnp.where(index[None, :] % NEIG == jnp.arange(NEIG)[:, None], diag[None, :], 0.0)
    lanes = (jnp.arange(LANES)[None, :] == SPARE + index[:, None] // NEIG).astype(F32)
    return dot_exact(rows, lanes)


def body(hamiltonian, current, previous):
    both = jnp.concatenate([current.T, previous.T], axis=0)
    v_own = to_chips(jnp.broadcast_to(both[None], (CHIPS, 2 * NEIG, ROWS)))
    tile = diagonal_tile(hamiltonian)
    cvec = jnp.pad(current.T, ((0, 0), (0, LANES - ROWS)))
    pvec = jnp.pad(previous.T, ((0, 0), (0, LANES - ROWS)))
    h_parts = prepare(hamiltonian)
    v_own, h_parts, tile = lax.optimization_barrier((v_own, h_parts, tile))
    v_other = to_core(v_own)
    block, parts = ((NEIG, LANES), F32), ((2, STACK, HALF), BF16)
    parts_vmem, half_vmem = pltpu.VMEM(*parts), pltpu.VMEM((STACK, HALF), BF16)
    h_vmem = pltpu.VMEM((2, CHUNKS, PARTS * TALL, CHUNK), BF16)
    h_half = pltpu.VMEM((CHUNKS, PARTS * TALL, CHUNK), BF16)
    dma = pltpu.SemaphoreType.DMA
    (product,) = kernel_call(
        image_own_kernel, [((PARTS * TALL, STACK), F32)], (h_parts, v_own), 1 << 30, "image_own",
        [h_half, half_vmem, dma((CHUNKS,))], (0,), limit=LIMIT_IMAGE,
    )
    image, sent = kernel_call(
        image_other_kernel, [block, ((CHIPS, NEIG, LANES), F32)], (h_parts, v_other, product, tile), 1 << 30, "image_other",
        [h_half, half_vmem, dma((CHUNKS,))], (0,), limit=LIMIT_IMAGE,
    )
    i_own = to_chips(sent)
    p_image, c_parts, p_parts, grams = kernel_call(
        previous_kernel,
        [block, parts, parts, ((3, NEIG, NEIG), F32)],
        (h_parts, v_own, v_other),
        6 << 30,
        "previous",
        [h_vmem, parts_vmem, parts_vmem, dma((2,)), dma((2, CHUNKS))], (0,), (1, 2),
    )
    i_own, p_image, c_parts = lax.optimization_barrier((i_own, p_image, c_parts))
    i_other = to_core(i_own)
    search, rms, cross, sent, s_parts, i_parts = kernel_call(
        search_kernel,
        [block, ((NEIG, 1), F32), ((NEIG, NEIG), F32), ((CHIPS, 8, LANES), F32), parts, parts],
        (h_parts, i_own, i_other, c_parts, cvec, pvec, p_image, image, tile),
        6 << 30,
        "search",
        [h_vmem, parts_vmem, parts_vmem, parts_vmem, pltpu.VMEM((2, NEIG, HALF), F32), dma((3,)), dma((2, CHUNKS))],
        (0, 3), (4, 5), limit=LIMIT_SEARCH,
    )
    r_own = to_chips(sent)
    square = ((3 * NEIG, 3 * NEIG), F32)
    inverse, stiff = kernel_call(
        factor_kernel, [square, square], (s_parts, c_parts, p_parts, i_parts, grams, cross), 6 << 30, "factor",
        [parts_vmem] * 4 + [dma((4,))], (0, 1, 2, 3),
    )
    r_own, inverse, rms = lax.optimization_barrier((r_own, inverse, rms[:, 0]))
    r_other = to_core(r_own)
    new_current, new_previous = kernel_call(
        finish_kernel,
        [((NEIG, ROWS), F32)] * 2,
        (inverse, stiff, r_own, r_other, cvec, search, pvec),
        1 << 28,
        "finish",
        limit=8 << 20,
    )
    return new_current.T, new_previous.T, rms


def solution(mesh):
    line = Mesh(mesh.devices.reshape(DEVICES), (AXIS,))
    return jax.shard_map(
        body,
        mesh=line,
        in_specs=(P(AXIS, None), P(AXIS, None), P(AXIS, None)),
        out_specs=(P(AXIS, None), P(AXIS, None), P()),
        check_vma=False,
    )
```

```python
import math

import jax
import jax.numpy as jnp
from jax import lax
from jax.experimental import pallas as pl
from jax.experimental.pallas import tpu as pltpu
from jax.sharding import Mesh
from jax.sharding import PartitionSpec as P

NEIG = 16
SIGN_STEPS = 6
ORDER = 13824
DEVICES = 128
ROWS = ORDER // DEVICES
CHIPS = DEVICES // 2
LANES = 128
HALF = CHIPS * LANES
TALL = 112
CHUNKS = 4
CHUNK = HALF // CHUNKS
EPS = 1e-06
AXIS = "device"
FORWARD = [[2 * chip + core for chip in range(CHIPS)] for core in range(2)]
BACKWARD = [[2 * chip + core for chip in reversed(range(CHIPS))] for core in range(2)]
F32, BF16 = jnp.float32, jnp.bfloat16
HIGHEST = lax.Precision.HIGHEST
VMEM = pl.BlockSpec(memory_space=pltpu.VMEM)
HBM = pl.BlockSpec(memory_space=pltpu.HBM)
LIMIT = 53 << 20
LIMIT_IMAGE = 48 << 20
LIMIT_SEARCH = 52 << 20
LIMIT_OWN = 52 << 20
PARTS = 2
STACK = PARTS * NEIG
SPARE = ROWS


def split(x):
    high = x.astype(BF16)
    return high, (x - high.astype(F32)).astype(BF16)


def split3(x):
    high = x.astype(BF16)
    rest = x - high.astype(F32)
    mid = rest.astype(BF16)
    return high, mid, (rest - mid.astype(F32)).astype(BF16)


def nt(left, right):
    return lax.dot_general(left, right, (((1,), (1,)), ((), ())), preferred_element_type=F32)


def nt_exact(left, right):
    return lax.dot_general(left, right, (((1,), (1,)), ((), ())), precision=HIGHEST, preferred_element_type=F32)


def dot_exact(left, right):
    return jnp.dot(left, right, precision=HIGHEST, preferred_element_type=F32)


def fold(parts):
    rows = parts[16:32] + parts[0:16]
    return rows[:, 16:32] + rows[:, 0:16]


def fold_rows(product):
    rows = product[TALL:] + product[:TALL]
    wide = jnp.concatenate([rows, jnp.zeros((TALL, LANES - STACK), F32)], axis=1)
    turned = jnp.concatenate([wide, jnp.zeros((LANES - TALL, LANES), F32)], axis=0).T
    return real_lanes(turned[16:32] + turned[0:16])


def real_lanes(tile):
    lane = lax.broadcasted_iota(jnp.int32, tile.shape, 1)
    return jnp.where(lane < ROWS, tile, 0.0)


def padded(tile):
    return jnp.concatenate([tile, jnp.zeros((tile.shape[0], LANES - ROWS), F32)], axis=1)


def prepare_kernel(h_ref, parts_ref):
    core = lax.rem(lax.axis_index(AXIS), 2)
    for block in range(2 * CHIPS // CHUNKS):
        chip, owner = divmod(block, 2)
        half = jnp.where(core == owner, 0, 1)
        x = padded(h_ref[:, ROWS * block : ROWS * block + ROWS])
        for number, part in enumerate(split(x)):
            parts_ref[half, TALL * number : TALL * number + ROWS, LANES * chip : LANES * (chip + 1)] = part


def prepare(hamiltonian):
    return pl.pallas_call(
        prepare_kernel,
        grid=(CHUNKS,),
        out_shape=jax.ShapeDtypeStruct((2, PARTS * TALL, HALF), BF16),
        in_specs=[pl.BlockSpec((ROWS, ORDER // CHUNKS), lambda i: (0, i))],
        out_specs=pl.BlockSpec((2, PARTS * TALL, CHUNK), lambda i: (0, 0, i)),
        compiler_params=pltpu.CompilerParams(vmem_limit_bytes=58 << 20),
        cost_estimate=pl.CostEstimate(flops=20 * ROWS * ORDER, bytes_accessed=10 * ROWS * ORDER, transcendentals=0),
        name="prepare",
    )(hamiltonian)


def started(source, target, sem):
    copy = pltpu.make_async_copy(source, target, sem)
    copy.start()
    return copy


def take_parts(tile_of, parts_ref):
    for chip in range(CHIPS):
        for number, part in enumerate(split(tile_of(chip))):
            parts_ref[NEIG * number : NEIG * (number + 1), LANES * chip : LANES * (chip + 1)] = part


def image_own_kernel(h_ref, own_ref, product_ref, h_vmem, parts, sem):
    copy = started(h_ref.at[0], h_vmem, sem)
    take_parts(lambda chip: padded(own_ref[CHIPS - 1 - chip, 0:NEIG]), parts)
    copy.wait()
    product_ref[...] = nt(h_vmem[...], parts[...])


def image_other_kernel(h_ref, other_ref, product_ref, tile_ref, image_ref, sent_ref, h_vmem, parts, sem):
    copy = started(h_ref.at[1], h_vmem, sem)
    take_parts(lambda chip: padded(other_ref[CHIPS - 1 - chip, 0:NEIG]), parts)
    copy.wait()
    image = fold_rows(product_ref[...] + nt(h_vmem[...], parts[...]))
    image_ref[...] = image
    sent = image + tile_ref[...]
    for chip in range(CHIPS):
        sent_ref[chip] = sent


def previous_kernel(h_ref, own_ref, other_ref, image_ref, c_out, p_out, gram_ref, h_vmem, c_ref, p_ref, sems):
    copy = started(h_ref, h_vmem, sems.at[0])
    for half, ref in ((0, own_ref), (1, other_ref)):
        take_parts(lambda chip: padded(ref[CHIPS - 1 - chip, 0:NEIG]), c_ref.at[half])
        take_parts(lambda chip: padded(ref[CHIPS - 1 - chip, NEIG : 2 * NEIG]), p_ref.at[half])
    out_c = started(c_ref, c_out, sems.at[1])
    out_p = started(p_ref, p_out, sems.at[2])
    gram_ref[0] = fold(nt(c_ref[0], c_ref[0]) + nt(c_ref[1], c_ref[1]))
    gram_ref[1] = fold(nt(p_ref[0], c_ref[0]) + nt(p_ref[1], c_ref[1]))
    gram_ref[2] = fold(nt(p_ref[0], p_ref[0]) + nt(p_ref[1], p_ref[1]))
    copy.wait()
    image_ref[...] = fold_rows(nt(h_vmem[0], p_ref[0]) + nt(h_vmem[1], p_ref[1]))
    out_c.wait()
    out_p.wait()


def diagonal_of(tile):
    row = lax.broadcasted_iota(jnp.int32, (NEIG, LANES), 0)
    lane = lax.broadcasted_iota(jnp.int32, (NEIG, LANES), 1)
    spread = jnp.take_along_axis(tile, SPARE + lane // NEIG, axis=1)
    return jnp.sum(jnp.where(lane % NEIG == row, spread, 0.0), axis=0, keepdims=True)


def own_kernel(own_ref, c_hbm, i_ref, cross_ref, diag_ref, c_ref, sem):
    copy = started(c_hbm.at[0], c_ref, sem)
    take_parts(lambda chip: real_lanes(own_ref[chip]), i_ref)
    for chip in range(CHIPS):
        diag_ref[chip : chip + 1, :] = diagonal_of(own_ref[chip])
    copy.wait()
    cross_ref[...] = nt(i_ref[...], c_ref[...])


def search_kernel(
    h_ref, own_ref, other_ref, c_hbm, i_own_ref, half_cross_ref, diag_ref, cvec_ref, pvec_ref, pimage_ref, image_ref, tile_ref,
    search_ref, rms_ref, cross_ref, sent_ref, kept_ref,
    h_vmem, c_ref, i_ref, s_ref, resid_ref, other_diag_ref, sems,
):
    copy_c = started(c_hbm, c_ref, sems.at[3])
    take_parts(lambda chip: real_lanes(other_ref[chip]), i_ref)
    for chip in range(CHIPS):
        other_diag_ref[chip : chip + 1, :] = diagonal_of(other_ref[chip])
    copy_c.wait()
    copy_h = started(h_ref, h_vmem, sems.at[0])
    kept = [started(i_own_ref, kept_ref.at[2], sems.at[1]), started(i_ref, kept_ref.at[3], sems.at[2])]
    cross_t = fold(half_cross_ref[...] + nt(i_ref[...], c_ref[1]))
    cross_ref[...] = cross_t
    ritz_t = cross_t / ORDER
    stacked = jnp.concatenate(split3(ritz_t), axis=0)
    stacked = jnp.concatenate([stacked] * PARTS, axis=1)
    square = jnp.zeros((NEIG, LANES), F32)
    for half, ref in ((0, own_ref), (1, other_ref)):
        moved = jnp.dot(stacked, c_ref[half], preferred_element_type=F32)
        moved = (moved[32:48] + moved[16:32]) + moved[0:16]
        part = jnp.zeros((NEIG, LANES), F32)
        for chip in range(CHIPS):
            lanes = slice(LANES * chip, LANES * (chip + 1))
            resid = real_lanes(ref[chip]) - moved[:, lanes]
            resid_ref[half, :, lanes] = resid
            part = part + resid * resid
        square = square + part
    rms = jnp.sqrt(jnp.sum(square, axis=1, keepdims=True) / ORDER + EPS)
    rms_ref[...] = rms
    row = lax.broadcasted_iota(jnp.int32, (NEIG, NEIG), 0)
    column = lax.broadcasted_iota(jnp.int32, (NEIG, NEIG), 1)
    value = jnp.sum(jnp.where(row == column, ritz_t, 0.0), axis=1, keepdims=True)
    value = jnp.broadcast_to(value, (NEIG, LANES))
    rms = jnp.broadcast_to(rms, (NEIG, LANES))

    def scaled(resid, diag):
        return resid / (jnp.maximum(jnp.abs(diag - value), 1.0) * rms)

    resid = image_ref[...] - dot_exact(ritz_t, cvec_ref[...])
    search = scaled(resid, diagonal_of(tile_ref[...]))
    search_ref[...] = search
    for half, diag in ((0, diag_ref), (1, other_diag_ref)):
        take_parts(
            lambda chip: scaled(resid_ref[half, :, LANES * chip : LANES * (chip + 1)], diag[chip : chip + 1, :]),
            s_ref.at[half],
        )
    kept.append(started(s_ref, kept_ref.at[pl.ds(0, 2)], sems.at[4]))
    copy_h.wait()
    simage = fold_rows(nt(h_vmem[0], s_ref[0]) + nt(h_vmem[1], s_ref[1]))
    pvec = pvec_ref[...]
    terms = jnp.concatenate(
        [nt_exact(simage, search), nt_exact(simage, pvec), nt_exact(pimage_ref[...], pvec), jnp.zeros((NEIG, NEIG), F32)],
        axis=1,
    )
    packed = jnp.concatenate([terms[0:8], terms[8:16]], axis=1)
    for chip in range(CHIPS):
        sent_ref[chip] = packed
    for copy in kept:
        copy.wait()


def factor_kernel(
    kept_hbm, c_hbm, p_hbm, gram_ref, cross_ref, inverse_ref, stiff_ref, kept_ref, c_ref, p_ref, sems,
):
    pairs = ((kept_hbm, kept_ref), (c_hbm, c_ref), (p_hbm, p_ref))
    s_ref, i_ref = kept_ref.at[pl.ds(0, 2)], kept_ref.at[pl.ds(2, 2)]
    for copy in [started(a, b, sems.at[n]) for n, (a, b) in enumerate(pairs)]:
        copy.wait()

    def gram(left, right):
        return fold(nt(left[0], right[0]) + nt(left[1], right[1]))

    empty = jnp.zeros((NEIG, NEIG), F32)
    cc, pc, pp = gram_ref[0], gram_ref[1], gram_ref[2]
    sc, ss, ps = gram(s_ref, c_ref), gram(s_ref, s_ref), gram(p_ref, s_ref)
    low = jnp.concatenate(
        [
            jnp.concatenate([0.5 * cc, empty, empty], axis=1),
            jnp.concatenate([sc, 0.5 * ss, empty], axis=1),
            jnp.concatenate([pc, ps, 0.5 * pp], axis=1),
        ],
        axis=0,
    )
    mass = low + low.T
    low = jnp.concatenate(
        [
            jnp.concatenate([0.5 * cross_ref[...], empty, empty], axis=1),
            jnp.concatenate([gram(s_ref, i_ref), empty, empty], axis=1),
            jnp.concatenate([gram(p_ref, i_ref), empty, empty], axis=1),
        ],
        axis=0,
    )
    stiff_ref[...] = low + low.T
    size = 3 * NEIG
    row = lax.broadcasted_iota(jnp.int32, (size, size), 0)
    column = lax.broadcasted_iota(jnp.int32, (size, size), 1)
    identity = jnp.where(row == column, 1.0, 0.0).astype(F32)
    work = jnp.concatenate([mass, identity], axis=1)
    below = lax.broadcasted_iota(jnp.int32, (size, 1), 0)
    for k in range(size):
        factor = jnp.where(below > k, work[:, k : k + 1] / work[k : k + 1, k : k + 1], 0.0)
        work = work - factor * work[k : k + 1, :]
    pivots = jnp.sum(work[:, :size] * identity, axis=1, keepdims=True)
    inverse_ref[...] = work[:, size:] / jnp.sqrt(pivots)


def finish_kernel(inverse_ref, stiff_ref, own_ref, other_ref, c_ref, s_ref, p_ref, current_ref, previous_ref):
    size = 3 * NEIG
    total = own_ref[0] + other_ref[0]
    for chip in range(1, CHIPS):
        total = total + (own_ref[chip] + other_ref[chip])
    terms = jnp.concatenate([total[:, 0 : 3 * NEIG], total[:, 4 * NEIG : 7 * NEIG]], axis=0)
    ss, sp, pp = terms[:, 0:16], terms[:, 16:32], terms[:, 32:48]
    empty = jnp.zeros((NEIG, NEIG), F32)
    up = jnp.concatenate(
        [
            jnp.zeros((NEIG, size), F32),
            jnp.concatenate([empty, 0.5 * ss, sp], axis=1),
            jnp.concatenate([empty, empty, 0.5 * pp], axis=1),
        ],
        axis=0,
    )
    stiff = stiff_ref[...] + (up + up.T)
    inverse = inverse_ref[...]
    reduced = nt_exact(dot_exact(inverse, stiff), inverse)
    row = lax.broadcasted_iota(jnp.int32, (size, size), 0)
    column = lax.broadcasted_iota(jnp.int32, (size, size), 1)
    identity = jnp.where(row == column, 1.0, 0.0).astype(F32)
    diagonal = jnp.sum(reduced * identity, axis=1, keepdims=True)
    level = jnp.max(diagonal[:NEIG], axis=0, keepdims=True)
    signed = level * identity - reduced
    square = dot_exact(signed, signed)
    total = jnp.sum(jnp.sum(signed * signed, axis=1, keepdims=True), axis=0, keepdims=True)
    square = square / total
    signed = signed / jnp.sqrt(total)
    for step in range(SIGN_STEPS):
        if step > 0:
            square = dot_exact(signed, signed)
        signed = dot_exact(signed, 1.5 * identity - 0.5 * square)
    projector = 0.5 * (identity + signed)
    wanted = jnp.where(lax.broadcasted_iota(jnp.int32, (size, size), 1) < NEIG, projector, 0.0)
    tn = (((0,), (0,)), ((), ()))
    coeffs_t = lax.dot_general(wanted, inverse, tn, precision=HIGHEST, preferred_element_type=F32)[0:NEIG]
    coeffs_t = coeffs_t * math.sqrt(ORDER)
    basis = jnp.concatenate([c_ref[...], s_ref[...], p_ref[...]], axis=0)
    current_ref[...] = dot_exact(coeffs_t, basis)[:, :ROWS]
    lane = lax.broadcasted_iota(jnp.int32, (NEIG, size), 1)
    previous_ref[...] = dot_exact(jnp.where(lane < NEIG, 0.0, coeffs_t), basis)[:, :ROWS]


def kernel_call(body, outs, args, flops, name, scratch=(), in_hbm=(), out_hbm=(), limit=LIMIT):
    return pl.pallas_call(
        body,
        out_shape=[jax.ShapeDtypeStruct(shape, kind) for shape, kind in outs],
        in_specs=[HBM if n in in_hbm else VMEM for n in range(len(args))],
        out_specs=[HBM if n in out_hbm else VMEM for n in range(len(outs))],
        scratch_shapes=scratch,
        compiler_params=pltpu.CompilerParams(vmem_limit_bytes=limit),
        cost_estimate=pl.CostEstimate(flops=flops, bytes_accessed=4 << 20, transcendentals=0),
        name=name,
    )(*args)


def to_chips(x, groups):
    return lax.all_to_all(x, AXIS, 0, 0, axis_index_groups=groups, tiled=True)


def to_core(x):
    return lax.ppermute(x, AXIS, [(device, device ^ 1) for device in range(DEVICES)])


def diagonal_tile(hamiltonian):
    device = lax.axis_index(AXIS)
    own_block = lax.dynamic_slice_in_dim(hamiltonian, device * ROWS, ROWS, 1)
    index = jnp.arange(ROWS)
    diag = jnp.sum(jnp.where(index[:, None] == index[None, :], own_block, 0.0), axis=0)
    rows = jnp.where(index[None, :] % NEIG == jnp.arange(NEIG)[:, None], diag[None, :], 0.0)
    lanes = (jnp.arange(LANES)[None, :] == SPARE + index[:, None] // NEIG).astype(F32)
    return dot_exact(rows, lanes)


def body(hamiltonian, current, previous):
    both = jnp.concatenate([current.T, previous.T], axis=0)
    v_own = to_chips(jnp.broadcast_to(both[None], (CHIPS, 2 * NEIG, ROWS)), BACKWARD)
    tile = diagonal_tile(hamiltonian)
    cvec = jnp.pad(current.T, ((0, 0), (0, LANES - ROWS)))
    pvec = jnp.pad(previous.T, ((0, 0), (0, LANES - ROWS)))
    h_parts = prepare(hamiltonian)
    v_own, h_parts, tile = lax.optimization_barrier((v_own, h_parts, tile))
    v_other = to_core(v_own)
    block, parts, half = ((NEIG, LANES), F32), ((2, STACK, HALF), BF16), ((STACK, HALF), BF16)
    parts_vmem, half_vmem = pltpu.VMEM(*parts), pltpu.VMEM(*half)
    h_vmem = pltpu.VMEM((2, PARTS * TALL, HALF), BF16)
    h_half = pltpu.VMEM((PARTS * TALL, HALF), BF16)
    dma = pltpu.SemaphoreType.DMA
    (product,) = kernel_call(
        image_own_kernel, [((PARTS * TALL, STACK), F32)], (h_parts, v_own), 1 << 30, "image_own",
        [h_half, half_vmem, dma(())], (0,), limit=LIMIT_IMAGE,
    )
    image, sent = kernel_call(
        image_other_kernel, [block, ((CHIPS, NEIG, LANES), F32)], (h_parts, v_other, product, tile), 1 << 30, "image_other",
        [h_half, half_vmem, dma(())], (0,), limit=LIMIT_IMAGE,
    )
    i_own = to_chips(sent, FORWARD)
    p_image, c_parts, p_parts, grams = kernel_call(
        previous_kernel,
        [block, parts, parts, ((3, NEIG, NEIG), F32)],
        (h_parts, v_own, v_other),
        6 << 30,
        "previous",
        [h_vmem, parts_vmem, parts_vmem, dma((3,))], (0,), (1, 2),
    )
    i_own, p_image, c_parts = lax.optimization_barrier((i_own, p_image, c_parts))
    i_other = to_core(i_own)
    i_own_parts, half_cross, diag = kernel_call(
        own_kernel,
        [half, ((STACK, STACK), F32), ((CHIPS, LANES), F32)],
        (i_own, c_parts),
        1 << 30,
        "own",
        [half_vmem, dma(())], (1,), limit=LIMIT_OWN,
    )
    search, rms, cross, sent, kept = kernel_call(
        search_kernel,
        [block, ((NEIG, 1), F32), ((NEIG, NEIG), F32), ((CHIPS, 8, LANES), F32), ((4, STACK, HALF), BF16)],
        (h_parts, i_own, i_other, c_parts, i_own_parts, half_cross, diag, cvec, pvec, p_image, image, tile),
        6 << 30,
        "search",
        [h_vmem, parts_vmem, half_vmem, parts_vmem, pltpu.VMEM((2, NEIG, HALF), F32), pltpu.VMEM((CHIPS, LANES), F32), dma((5,))],
        (0, 3), (4,), limit=LIMIT_SEARCH,
    )
    r_own = to_chips(sent, FORWARD)
    square = ((3 * NEIG, 3 * NEIG), F32)
    inverse, stiff = kernel_call(
        factor_kernel, [square, square], (kept, c_parts, p_parts, grams, cross), 6 << 30, "factor",
        [pltpu.VMEM((4, STACK, HALF), BF16), parts_vmem, parts_vmem, dma((3,))], (0, 1, 2),
    )
    r_own, inverse, rms = lax.optimization_barrier((r_own, inverse, rms[:, 0]))
    r_other = to_core(r_own)
    new_current, new_previous = kernel_call(
        finish_kernel,
        [((NEIG, ROWS), F32)] * 2,
        (inverse, stiff, r_own, r_other, cvec, search, pvec),
        1 << 28,
        "finish",
        limit=8 << 20,
    )
    return new_current.T, new_previous.T, rms


def solution(mesh):
    line = Mesh(mesh.devices.reshape(DEVICES), (AXIS,))
    return jax.shard_map(
        body,
        mesh=line,
        in_specs=(P(AXIS, None), P(AXIS, None), P(AXIS, None)),
        out_specs=(P(AXIS, None), P(AXIS, None), P()),
        check_vma=False,
    )
```

```python
import math

import jax
import jax.numpy as jnp
from jax import lax
from jax.experimental import pallas as pl
from jax.experimental.pallas import tpu as pltpu
from jax.sharding import Mesh
from jax.sharding import PartitionSpec as P

NEIG = 16
SIGN_STEPS = 6
ORDER = 13824
DEVICES = 128
ROWS = ORDER // DEVICES
CHIPS = DEVICES // 2
LANES = 128
FORWARD = list(range(CHIPS))
BACKWARD = FORWARD[::-1]
ORDERS = (BACKWARD, BACKWARD, FORWARD)
SLOTS = [[order.index(chip) for chip in range(CHIPS)] for order in ORDERS]
HALF = CHIPS * LANES
TALL = 112
CHUNKS = 4
CHUNK = HALF // CHUNKS
EPS = 1e-06
AXIS = "device"

F32, BF16 = jnp.float32, jnp.bfloat16
HIGHEST = lax.Precision.HIGHEST
VMEM = pl.BlockSpec(memory_space=pltpu.VMEM)
HBM = pl.BlockSpec(memory_space=pltpu.HBM)
LIMIT = 53 << 20
LIMIT_IMAGE = 48 << 20
LIMIT_SEARCH = 52 << 20
LIMIT_OWN = 52 << 20
PARTS = 2
STACK = PARTS * NEIG
SPARE = ROWS


def split(x):
    high = x.astype(BF16)
    return high, (x - high.astype(F32)).astype(BF16)


def split3(x):
    high = x.astype(BF16)
    rest = x - high.astype(F32)
    mid = rest.astype(BF16)
    return high, mid, (rest - mid.astype(F32)).astype(BF16)


def nt(left, right):
    return lax.dot_general(left, right, (((1,), (1,)), ((), ())), preferred_element_type=F32)


def nt_exact(left, right):
    return lax.dot_general(left, right, (((1,), (1,)), ((), ())), precision=HIGHEST, preferred_element_type=F32)


def dot_exact(left, right):
    return jnp.dot(left, right, precision=HIGHEST, preferred_element_type=F32)


def fold(parts):
    rows = parts[16:32] + parts[0:16]
    return rows[:, 16:32] + rows[:, 0:16]


def fold_rows(product):
    rows = product[TALL:] + product[:TALL]
    wide = jnp.concatenate([rows, jnp.zeros((TALL, LANES - STACK), F32)], axis=1)
    turned = jnp.concatenate([wide, jnp.zeros((LANES - TALL, LANES), F32)], axis=0).T
    return real_lanes(turned[16:32] + turned[0:16])


def real_lanes(tile):
    lane = lax.broadcasted_iota(jnp.int32, tile.shape, 1)
    return jnp.where(lane < ROWS, tile, 0.0)


def padded(tile):
    return jnp.concatenate([tile, jnp.zeros((tile.shape[0], LANES - ROWS), F32)], axis=1)


def prepare_kernel(h_ref, parts_ref):
    core = lax.rem(lax.axis_index(AXIS), 2)
    for block in range(2 * CHIPS // CHUNKS):
        chip, owner = divmod(block, 2)
        half = jnp.where(core == owner, 0, 1)
        x = padded(h_ref[:, ROWS * block : ROWS * block + ROWS])
        for number, part in enumerate(split(x)):
            parts_ref[half, TALL * number : TALL * number + ROWS, LANES * chip : LANES * (chip + 1)] = part


def prepare(hamiltonian):
    return pl.pallas_call(
        prepare_kernel,
        grid=(CHUNKS,),
        out_shape=jax.ShapeDtypeStruct((2, PARTS * TALL, HALF), BF16),
        in_specs=[pl.BlockSpec((ROWS, ORDER // CHUNKS), lambda i: (0, i))],
        out_specs=pl.BlockSpec((2, PARTS * TALL, CHUNK), lambda i: (0, 0, i)),
        compiler_params=pltpu.CompilerParams(vmem_limit_bytes=58 << 20),
        cost_estimate=pl.CostEstimate(flops=20 * ROWS * ORDER, bytes_accessed=10 * ROWS * ORDER, transcendentals=0),
        name="prepare",
    )(hamiltonian)


def started(source, target, sem):
    copy = pltpu.make_async_copy(source, target, sem)
    copy.start()
    return copy


def take_parts(tile_of, parts_ref):
    for chip in range(CHIPS):
        for number, part in enumerate(split(tile_of(chip))):
            parts_ref[NEIG * number : NEIG * (number + 1), LANES * chip : LANES * (chip + 1)] = part


def image_own_kernel(h_ref, own_ref, product_ref, next_ref, h_vmem, parts, sems):
    copy = started(h_ref.at[0], h_vmem, sems.at[0])
    following = started(h_ref.at[1], next_ref, sems.at[1])
    take_parts(lambda chip: padded(own_ref[SLOTS[0][chip], 0:NEIG]), parts)
    copy.wait()
    product_ref[...] = nt(h_vmem[...], parts[...])
    following.wait()


def image_other_kernel(h_ref, other_ref, product_ref, tile_ref, image_ref, sent_ref, parts):
    take_parts(lambda chip: padded(other_ref[SLOTS[0][chip], 0:NEIG]), parts)
    image = fold_rows(product_ref[...] + nt(h_ref[...], parts[...]))
    image_ref[...] = image
    sent = image + tile_ref[...]
    for chip in range(CHIPS):
        sent_ref[chip] = sent


def previous_kernel(h_ref, own_ref, other_ref, image_ref, c_out, p_out, gram_ref, h_vmem, c_ref, p_ref, sems):
    copy = started(h_ref, h_vmem, sems.at[0])
    for half, ref in ((0, own_ref), (1, other_ref)):
        take_parts(lambda chip: padded(ref[SLOTS[0][chip], 0:NEIG]), c_ref.at[half])
        take_parts(lambda chip: padded(ref[SLOTS[0][chip], NEIG : 2 * NEIG]), p_ref.at[half])
    out_c = started(c_ref, c_out, sems.at[1])
    out_p = started(p_ref, p_out, sems.at[2])
    gram_ref[0] = fold(nt(c_ref[0], c_ref[0]) + nt(c_ref[1], c_ref[1]))
    gram_ref[1] = fold(nt(p_ref[0], c_ref[0]) + nt(p_ref[1], c_ref[1]))
    gram_ref[2] = fold(nt(p_ref[0], p_ref[0]) + nt(p_ref[1], p_ref[1]))
    copy.wait()
    image_ref[...] = fold_rows(nt(h_vmem[0], p_ref[0]) + nt(h_vmem[1], p_ref[1]))
    out_c.wait()
    out_p.wait()


def diagonal_of(tile):
    row = lax.broadcasted_iota(jnp.int32, (NEIG, LANES), 0)
    lane = lax.broadcasted_iota(jnp.int32, (NEIG, LANES), 1)
    spread = jnp.take_along_axis(tile, SPARE + lane // NEIG, axis=1)
    return jnp.sum(jnp.where(lane % NEIG == row, spread, 0.0), axis=0, keepdims=True)


def own_kernel(own_ref, c_hbm, i_ref, cross_ref, diag_ref, c_ref, sem):
    copy = started(c_hbm.at[0], c_ref, sem)
    take_parts(lambda chip: real_lanes(own_ref[SLOTS[1][chip]]), i_ref)
    for chip in range(CHIPS):
        diag_ref[chip : chip + 1, :] = diagonal_of(own_ref[SLOTS[1][chip]])
    copy.wait()
    cross_ref[...] = nt(i_ref[...], c_ref[...])


def search_kernel(
    h_ref, own_ref, other_ref, c_hbm, i_own_ref, half_cross_ref, diag_ref, cvec_ref, pvec_ref, pimage_ref, image_ref, tile_ref,
    search_ref, rms_ref, cross_ref, sent_ref, kept_ref,
    h_vmem, c_ref, i_ref, s_ref, resid_ref, other_diag_ref, sems, h_sems,
):
    copy_c = started(c_hbm, c_ref, sems.at[3])
    copies = [started(h_ref.at[half], h_vmem.at[half], h_sems.at[half]) for half in range(2)]
    take_parts(lambda chip: real_lanes(other_ref[SLOTS[1][chip]]), i_ref)
    for chip in range(CHIPS):
        other_diag_ref[chip : chip + 1, :] = diagonal_of(other_ref[SLOTS[1][chip]])
    copy_c.wait()
    kept = [started(i_own_ref, kept_ref.at[2], sems.at[1]), started(i_ref, kept_ref.at[3], sems.at[2])]
    cross_t = fold(half_cross_ref[...] + nt(i_ref[...], c_ref[1]))
    cross_ref[...] = cross_t
    ritz_t = cross_t / ORDER
    stacked = jnp.concatenate(split3(ritz_t), axis=0)
    stacked = jnp.concatenate([stacked] * PARTS, axis=1)
    square = jnp.zeros((NEIG, LANES), F32)
    for half, ref in ((0, own_ref), (1, other_ref)):
        moved = jnp.dot(stacked, c_ref[half], preferred_element_type=F32)
        moved = (moved[32:48] + moved[16:32]) + moved[0:16]
        part = jnp.zeros((NEIG, LANES), F32)
        for chip in range(CHIPS):
            lanes = slice(LANES * chip, LANES * (chip + 1))
            resid = real_lanes(ref[SLOTS[1][chip]]) - moved[:, lanes]
            resid_ref[half, :, lanes] = resid
            part = part + resid * resid
        square = square + part
    rms = jnp.sqrt(jnp.sum(square, axis=1, keepdims=True) / ORDER + EPS)
    rms_ref[...] = rms
    row = lax.broadcasted_iota(jnp.int32, (NEIG, NEIG), 0)
    column = lax.broadcasted_iota(jnp.int32, (NEIG, NEIG), 1)
    value = jnp.sum(jnp.where(row == column, ritz_t, 0.0), axis=1, keepdims=True)
    value = jnp.broadcast_to(value, (NEIG, LANES))
    rms = jnp.broadcast_to(rms, (NEIG, LANES))

    def scaled(resid, diag):
        return resid / (jnp.maximum(jnp.abs(diag - value), 1.0) * rms)

    resid = image_ref[...] - dot_exact(ritz_t, cvec_ref[...])
    search = scaled(resid, diagonal_of(tile_ref[...]))
    search_ref[...] = search
    for half, diag in ((0, diag_ref), (1, other_diag_ref)):
        take_parts(
            lambda chip: scaled(resid_ref[half, :, LANES * chip : LANES * (chip + 1)], diag[chip : chip + 1, :]),
            s_ref.at[half],
        )
    kept.append(started(s_ref, kept_ref.at[pl.ds(0, 2)], sems.at[0]))
    copies[0].wait()
    product = nt(h_vmem[0], s_ref[0])
    copies[1].wait()
    simage = fold_rows(product + nt(h_vmem[1], s_ref[1]))
    pvec = pvec_ref[...]
    terms = jnp.concatenate(
        [nt_exact(simage, search), nt_exact(simage, pvec), nt_exact(pimage_ref[...], pvec), jnp.zeros((NEIG, NEIG), F32)],
        axis=1,
    )
    packed = jnp.concatenate([terms[0:8], terms[8:16]], axis=1)
    for chip in range(CHIPS):
        sent_ref[chip] = packed
    for copy in kept:
        copy.wait()


def factor_kernel(
    kept_hbm, c_hbm, p_hbm, gram_ref, cross_ref, inverse_ref, stiff_ref, kept_ref, c_ref, p_ref, sems,
):
    pairs = ((kept_hbm, kept_ref), (c_hbm, c_ref), (p_hbm, p_ref))
    s_ref, i_ref = kept_ref.at[pl.ds(0, 2)], kept_ref.at[pl.ds(2, 2)]
    for copy in [started(a, b, sems.at[n]) for n, (a, b) in enumerate(pairs)]:
        copy.wait()

    def gram(left, right):
        return fold(nt(left[0], right[0]) + nt(left[1], right[1]))

    empty = jnp.zeros((NEIG, NEIG), F32)
    cc, pc, pp = gram_ref[0], gram_ref[1], gram_ref[2]
    sc, ss, ps = gram(s_ref, c_ref), gram(s_ref, s_ref), gram(p_ref, s_ref)
    low = jnp.concatenate(
        [
            jnp.concatenate([0.5 * cc, empty, empty], axis=1),
            jnp.concatenate([sc, 0.5 * ss, empty], axis=1),
            jnp.concatenate([pc, ps, 0.5 * pp], axis=1),
        ],
        axis=0,
    )
    mass = low + low.T
    low = jnp.concatenate(
        [
            jnp.concatenate([0.5 * cross_ref[...], empty, empty], axis=1),
            jnp.concatenate([gram(s_ref, i_ref), empty, empty], axis=1),
            jnp.concatenate([gram(p_ref, i_ref), empty, empty], axis=1),
        ],
        axis=0,
    )
    stiff_ref[...] = low + low.T
    size = 3 * NEIG
    row = lax.broadcasted_iota(jnp.int32, (size, size), 0)
    column = lax.broadcasted_iota(jnp.int32, (size, size), 1)
    identity = jnp.where(row == column, 1.0, 0.0).astype(F32)
    work = jnp.concatenate([mass, identity], axis=1)
    below = lax.broadcasted_iota(jnp.int32, (size, 1), 0)
    for k in range(size):
        factor = jnp.where(below > k, work[:, k : k + 1] / work[k : k + 1, k : k + 1], 0.0)
        work = work - factor * work[k : k + 1, :]
    pivots = jnp.sum(work[:, :size] * identity, axis=1, keepdims=True)
    inverse_ref[...] = work[:, size:] / jnp.sqrt(pivots)


def finish_kernel(inverse_ref, stiff_ref, own_ref, other_ref, c_ref, s_ref, p_ref, current_ref, previous_ref):
    size = 3 * NEIG
    total = own_ref[0] + other_ref[0]
    for chip in range(1, CHIPS):
        total = total + (own_ref[chip] + other_ref[chip])
    terms = jnp.concatenate([total[:, 0 : 3 * NEIG], total[:, 4 * NEIG : 7 * NEIG]], axis=0)
    ss, sp, pp = terms[:, 0:16], terms[:, 16:32], terms[:, 32:48]
    empty = jnp.zeros((NEIG, NEIG), F32)
    up = jnp.concatenate(
        [
            jnp.zeros((NEIG, size), F32),
            jnp.concatenate([empty, 0.5 * ss, sp], axis=1),
            jnp.concatenate([empty, empty, 0.5 * pp], axis=1),
        ],
        axis=0,
    )
    stiff = stiff_ref[...] + (up + up.T)
    inverse = inverse_ref[...]
    reduced = nt_exact(dot_exact(inverse, stiff), inverse)
    row = lax.broadcasted_iota(jnp.int32, (size, size), 0)
    column = lax.broadcasted_iota(jnp.int32, (size, size), 1)
    identity = jnp.where(row == column, 1.0, 0.0).astype(F32)
    diagonal = jnp.sum(reduced * identity, axis=1, keepdims=True)
    level = jnp.max(diagonal[:NEIG], axis=0, keepdims=True)
    signed = level * identity - reduced
    square = dot_exact(signed, signed)
    total = jnp.sum(jnp.sum(signed * signed, axis=1, keepdims=True), axis=0, keepdims=True)
    square = square / total
    signed = signed / jnp.sqrt(total)
    for step in range(SIGN_STEPS):
        if step > 0:
            square = dot_exact(signed, signed)
        signed = dot_exact(signed, 1.5 * identity - 0.5 * square)
    projector = 0.5 * (identity + signed)
    wanted = jnp.where(lax.broadcasted_iota(jnp.int32, (size, size), 1) < NEIG, projector, 0.0)
    tn = (((0,), (0,)), ((), ()))
    coeffs_t = lax.dot_general(wanted, inverse, tn, precision=HIGHEST, preferred_element_type=F32)[0:NEIG]
    coeffs_t = coeffs_t * math.sqrt(ORDER)
    basis = jnp.concatenate([c_ref[...], s_ref[...], p_ref[...]], axis=0)
    current_ref[...] = dot_exact(coeffs_t, basis)[:, :ROWS]
    lane = lax.broadcasted_iota(jnp.int32, (NEIG, size), 1)
    previous_ref[...] = dot_exact(jnp.where(lane < NEIG, 0.0, coeffs_t), basis)[:, :ROWS]


def kernel_call(body, outs, args, flops, name, scratch=(), in_hbm=(), out_hbm=(), limit=LIMIT):
    return pl.pallas_call(
        body,
        out_shape=[jax.ShapeDtypeStruct(shape, kind) for shape, kind in outs],
        in_specs=[HBM if n in in_hbm else VMEM for n in range(len(args))],
        out_specs=[HBM if n in out_hbm else VMEM for n in range(len(outs))],
        scratch_shapes=scratch,
        compiler_params=pltpu.CompilerParams(vmem_limit_bytes=limit),
        cost_estimate=pl.CostEstimate(flops=flops, bytes_accessed=4 << 20, transcendentals=0),
        name=name,
    )(*args)


def to_chips(x, number):
    groups = [[2 * chip + core for chip in ORDERS[number]] for core in range(2)]
    return lax.all_to_all(x, AXIS, 0, 0, axis_index_groups=groups, tiled=True)


def to_core(x):
    return lax.ppermute(x, AXIS, [(device, device ^ 1) for device in range(DEVICES)])


def diagonal_tile(hamiltonian):
    device = lax.axis_index(AXIS)
    own_block = lax.dynamic_slice_in_dim(hamiltonian, device * ROWS, ROWS, 1)
    index = jnp.arange(ROWS)
    diag = jnp.sum(jnp.where(index[:, None] == index[None, :], own_block, 0.0), axis=0)
    rows = jnp.where(index[None, :] % NEIG == jnp.arange(NEIG)[:, None], diag[None, :], 0.0)
    lanes = (jnp.arange(LANES)[None, :] == SPARE + index[:, None] // NEIG).astype(F32)
    return dot_exact(rows, lanes)


def body(hamiltonian, current, previous):
    both = jnp.concatenate([current.T, previous.T], axis=0)
    v_own = to_chips(jnp.broadcast_to(both[None], (CHIPS, 2 * NEIG, ROWS)), 0)
    tile = diagonal_tile(hamiltonian)
    cvec = jnp.pad(current.T, ((0, 0), (0, LANES - ROWS)))
    pvec = jnp.pad(previous.T, ((0, 0), (0, LANES - ROWS)))
    h_parts = prepare(hamiltonian)
    v_own, h_parts, tile = lax.optimization_barrier((v_own, h_parts, tile))
    v_other = to_core(v_own)
    block, parts, half = ((NEIG, LANES), F32), ((2, STACK, HALF), BF16), ((STACK, HALF), BF16)
    parts_vmem, half_vmem = pltpu.VMEM(*parts), pltpu.VMEM(*half)
    h_vmem = pltpu.VMEM((2, PARTS * TALL, HALF), BF16)
    h_half = pltpu.VMEM((PARTS * TALL, HALF), BF16)
    dma = pltpu.SemaphoreType.DMA
    product, h_next = kernel_call(
        image_own_kernel,
        [((PARTS * TALL, STACK), F32), ((PARTS * TALL, HALF), BF16)],
        (h_parts, v_own),
        1 << 30,
        "image_own",
        [h_half, half_vmem, dma((2,))], (0,), limit=LIMIT_IMAGE,
    )
    image, sent = kernel_call(
        image_other_kernel, [block, ((CHIPS, NEIG, LANES), F32)], (h_next, v_other, product, tile), 1 << 30, "image_other",
        [half_vmem], limit=LIMIT_IMAGE,
    )
    i_own = to_chips(sent, 1)
    p_image, c_parts, p_parts, grams = kernel_call(
        previous_kernel,
        [block, parts, parts, ((3, NEIG, NEIG), F32)],
        (h_parts, v_own, v_other),
        6 << 30,
        "previous",
        [h_vmem, parts_vmem, parts_vmem, dma((3,))], (0,), (1, 2),
    )
    i_own, p_image, c_parts = lax.optimization_barrier((i_own, p_image, c_parts))
    i_other = to_core(i_own)
    i_own_parts, half_cross, diag = kernel_call(
        own_kernel,
        [half, ((STACK, STACK), F32), ((CHIPS, LANES), F32)],
        (i_own, c_parts),
        1 << 30,
        "own",
        [half_vmem, dma(())], (1,), limit=LIMIT_OWN,
    )
    search, rms, cross, sent, kept = kernel_call(
        search_kernel,
        [block, ((NEIG, 1), F32), ((NEIG, NEIG), F32), ((CHIPS, 8, LANES), F32), ((4, STACK, HALF), BF16)],
        (h_parts, i_own, i_other, c_parts, i_own_parts, half_cross, diag, cvec, pvec, p_image, image, tile),
        6 << 30,
        "search",
        [h_vmem, parts_vmem, half_vmem, parts_vmem, pltpu.VMEM((2, NEIG, HALF), F32), pltpu.VMEM((CHIPS, LANES), F32), dma((4,)), dma((2,))],
        (0, 3), (4,), limit=LIMIT_SEARCH,
    )
    r_own = to_chips(sent, 2)
    square = ((3 * NEIG, 3 * NEIG), F32)
    inverse, stiff = kernel_call(
        factor_kernel, [square, square], (kept, c_parts, p_parts, grams, cross), 6 << 30, "factor",
        [pltpu.VMEM((4, STACK, HALF), BF16), parts_vmem, parts_vmem, dma((3,))], (0, 1, 2),
    )
    r_own, inverse, rms = lax.optimization_barrier((r_own, inverse, rms[:, 0]))
    r_other = to_core(r_own)
    new_current, new_previous = kernel_call(
        finish_kernel,
        [((NEIG, ROWS), F32)] * 2,
        (inverse, stiff, r_own, r_other, cvec, search, pvec),
        1 << 28,
        "finish",
        limit=8 << 20,
    )
    return new_current.T, new_previous.T, rms


def solution(mesh):
    line = Mesh(mesh.devices.reshape(DEVICES), (AXIS,))
    return jax.shard_map(
        body,
        mesh=line,
        in_specs=(P(AXIS, None), P(AXIS, None), P(AXIS, None)),
        out_specs=(P(AXIS, None), P(AXIS, None), P()),
        check_vma=False,
    )
```

```python
import math

import jax
import jax.numpy as jnp
from jax import lax
from jax.experimental import pallas as pl
from jax.experimental.pallas import tpu as pltpu
from jax.sharding import Mesh
from jax.sharding import PartitionSpec as P

NEIG = 16
SIGN_STEPS = 6
ORDER = 13824
DEVICES = 128
ROWS = ORDER // DEVICES
CHIPS = DEVICES // 2
LANES = 128
FORWARD = list(range(CHIPS))
BACKWARD = FORWARD[::-1]
ORDERS = (BACKWARD, BACKWARD, FORWARD)
SLOTS = [[order.index(chip) for chip in range(CHIPS)] for order in ORDERS]
HALF = CHIPS * LANES
TALL = 112
CHUNKS = 4
CHUNK = HALF // CHUNKS
EPS = 1e-06
AXIS = "device"

F32, BF16 = jnp.float32, jnp.bfloat16
HIGHEST = lax.Precision.HIGHEST
VMEM = pl.BlockSpec(memory_space=pltpu.VMEM)
HBM = pl.BlockSpec(memory_space=pltpu.HBM)
LIMIT = 53 << 20
LIMIT_IMAGE = 48 << 20
LIMIT_SEARCH = 52 << 20
LIMIT_OWN = 52 << 20
PARTS = 2
STACK = PARTS * NEIG
SPARE = ROWS


def split(x):
    high = x.astype(BF16)
    return high, (x - high.astype(F32)).astype(BF16)


def split3(x):
    high = x.astype(BF16)
    rest = x - high.astype(F32)
    mid = rest.astype(BF16)
    return high, mid, (rest - mid.astype(F32)).astype(BF16)


def nt(left, right):
    return lax.dot_general(left, right, (((1,), (1,)), ((), ())), preferred_element_type=F32)


def nt_exact(left, right):
    return lax.dot_general(left, right, (((1,), (1,)), ((), ())), precision=HIGHEST, preferred_element_type=F32)


def dot_exact(left, right):
    return jnp.dot(left, right, precision=HIGHEST, preferred_element_type=F32)


def fold(parts):
    rows = parts[16:32] + parts[0:16]
    return rows[:, 16:32] + rows[:, 0:16]


def fold_rows(product):
    rows = product[TALL:] + product[:TALL]
    wide = jnp.concatenate([rows, jnp.zeros((TALL, LANES - STACK), F32)], axis=1)
    turned = jnp.concatenate([wide, jnp.zeros((LANES - TALL, LANES), F32)], axis=0).T
    return real_lanes(turned[16:32] + turned[0:16])


def real_lanes(tile):
    lane = lax.broadcasted_iota(jnp.int32, tile.shape, 1)
    return jnp.where(lane < ROWS, tile, 0.0)


def padded(tile):
    return jnp.concatenate([tile, jnp.zeros((tile.shape[0], LANES - ROWS), F32)], axis=1)


def prepare_kernel(h_ref, parts_ref):
    core = lax.rem(lax.axis_index(AXIS), 2)
    for block in range(2 * CHIPS // CHUNKS):
        chip, owner = divmod(block, 2)
        half = jnp.where(core == owner, 0, 1)
        x = padded(h_ref[:, ROWS * block : ROWS * block + ROWS])
        for number, part in enumerate(split(x)):
            parts_ref[half, TALL * number : TALL * number + ROWS, LANES * chip : LANES * (chip + 1)] = part


def prepare(hamiltonian):
    return pl.pallas_call(
        prepare_kernel,
        grid=(CHUNKS,),
        out_shape=jax.ShapeDtypeStruct((2, PARTS * TALL, HALF), BF16),
        in_specs=[pl.BlockSpec((ROWS, ORDER // CHUNKS), lambda i: (0, i))],
        out_specs=pl.BlockSpec((2, PARTS * TALL, CHUNK), lambda i: (0, 0, i)),
        compiler_params=pltpu.CompilerParams(vmem_limit_bytes=58 << 20),
        cost_estimate=pl.CostEstimate(flops=20 * ROWS * ORDER, bytes_accessed=10 * ROWS * ORDER, transcendentals=0),
        name="prepare",
    )(hamiltonian)


def started(source, target, sem):
    copy = pltpu.make_async_copy(source, target, sem)
    copy.start()
    return copy


def take_parts(tile_of, parts_ref):
    for chip in range(CHIPS):
        for number, part in enumerate(split(tile_of(chip))):
            parts_ref[NEIG * number : NEIG * (number + 1), LANES * chip : LANES * (chip + 1)] = part


def take_both(tile_of, parts_ref):
    for chip in range(CHIPS):
        lanes = slice(LANES * chip, LANES * (chip + 1))
        for number, part in enumerate(split(tile_of(chip))):
            parts_ref[NEIG * number : NEIG * (number + 1), lanes] = part[:NEIG]
            parts_ref[STACK + NEIG * number : STACK + NEIG * (number + 1), lanes] = part[NEIG:]


def image_own_kernel(h_ref, own_ref, product_ref, next_ref, h_vmem, parts, sems):
    copy = started(h_ref.at[0], h_vmem, sems.at[0])
    following = started(h_ref.at[1], next_ref, sems.at[1])
    take_both(lambda chip: padded(own_ref[SLOTS[0][chip]]), parts)
    copy.wait()
    product_ref[...] = nt(h_vmem[...], parts[...])
    following.wait()


def image_other_kernel(h_ref, other_ref, product_ref, tile_ref, image_ref, sent_ref, parts):
    take_parts(lambda chip: padded(other_ref[SLOTS[0][chip], 0:NEIG]), parts)
    image = fold_rows(product_ref[:, 0:STACK] + nt(h_ref[...], parts[...]))
    image_ref[...] = image
    sent = image + tile_ref[...]
    for chip in range(CHIPS):
        sent_ref[chip] = sent


def previous_kernel(h_ref, own_ref, other_ref, product_ref, image_ref, both_out, gram_ref, h_vmem, both_ref, sems):
    copy = started(h_ref.at[1], h_vmem, sems.at[0])
    take_both(lambda chip: padded(own_ref[SLOTS[0][chip]]), both_ref.at[0])
    take_both(lambda chip: padded(other_ref[SLOTS[0][chip]]), both_ref.at[1])
    out = started(both_ref, both_out, sems.at[1])
    product = nt(both_ref[0], both_ref[0]) + nt(both_ref[1], both_ref[1])
    gram_ref[0] = fold(product[:STACK, :STACK])
    gram_ref[1] = fold(product[STACK:, :STACK])
    gram_ref[2] = fold(product[STACK:, STACK:])
    copy.wait()
    image_ref[...] = fold_rows(product_ref[:, STACK:] + nt(h_vmem[...], both_ref[1, STACK:]))
    out.wait()


def diagonal_of(tile):
    row = lax.broadcasted_iota(jnp.int32, (NEIG, LANES), 0)
    lane = lax.broadcasted_iota(jnp.int32, (NEIG, LANES), 1)
    spread = jnp.take_along_axis(tile, SPARE + lane // NEIG, axis=1)
    return jnp.sum(jnp.where(lane % NEIG == row, spread, 0.0), axis=0, keepdims=True)


def own_kernel(own_ref, both_hbm, i_ref, cross_ref, diag_ref, c_ref, sem):
    copy = started(both_hbm.at[0, pl.ds(0, STACK)], c_ref, sem)
    take_parts(lambda chip: real_lanes(own_ref[SLOTS[1][chip]]), i_ref)
    for chip in range(CHIPS):
        diag_ref[chip : chip + 1, :] = diagonal_of(own_ref[SLOTS[1][chip]])
    copy.wait()
    cross_ref[...] = nt(i_ref[...], c_ref[...])


def search_kernel(
    h_ref, own_ref, other_ref, both_hbm, i_own_ref, half_cross_ref, diag_ref, cvec_ref, pvec_ref, pimage_ref, image_ref, tile_ref,
    search_ref, rms_ref, cross_ref, sent_ref, kept_ref,
    h_vmem, c_ref, i_ref, s_ref, resid_ref, other_diag_ref, sems, h_sems,
):
    copy_c = started(both_hbm.at[:, pl.ds(0, STACK)], c_ref, sems.at[3])
    copies = [started(h_ref.at[half], h_vmem.at[half], h_sems.at[half]) for half in range(2)]
    take_parts(lambda chip: real_lanes(other_ref[SLOTS[1][chip]]), i_ref)
    for chip in range(CHIPS):
        other_diag_ref[chip : chip + 1, :] = diagonal_of(other_ref[SLOTS[1][chip]])
    copy_c.wait()
    kept = [started(i_own_ref, kept_ref.at[2], sems.at[1]), started(i_ref, kept_ref.at[3], sems.at[2])]
    cross_t = fold(half_cross_ref[...] + nt(i_ref[...], c_ref[1]))
    cross_ref[...] = cross_t
    ritz_t = cross_t / ORDER
    stacked = jnp.concatenate(split3(ritz_t), axis=0)
    stacked = jnp.concatenate([stacked] * PARTS, axis=1)
    square = jnp.zeros((NEIG, LANES), F32)
    for half, ref in ((0, own_ref), (1, other_ref)):
        moved = jnp.dot(stacked, c_ref[half], preferred_element_type=F32)
        moved = (moved[32:48] + moved[16:32]) + moved[0:16]
        part = jnp.zeros((NEIG, LANES), F32)
        for chip in range(CHIPS):
            lanes = slice(LANES * chip, LANES * (chip + 1))
            resid = real_lanes(ref[SLOTS[1][chip]]) - moved[:, lanes]
            resid_ref[half, :, lanes] = resid
            part = part + resid * resid
        square = square + part
    rms = jnp.sqrt(jnp.sum(square, axis=1, keepdims=True) / ORDER + EPS)
    rms_ref[...] = rms
    row = lax.broadcasted_iota(jnp.int32, (NEIG, NEIG), 0)
    column = lax.broadcasted_iota(jnp.int32, (NEIG, NEIG), 1)
    value = jnp.sum(jnp.where(row == column, ritz_t, 0.0), axis=1, keepdims=True)
    value = jnp.broadcast_to(value, (NEIG, LANES))
    rms = jnp.broadcast_to(rms, (NEIG, LANES))

    def scaled(resid, diag):
        return resid / (jnp.maximum(jnp.abs(diag - value), 1.0) * rms)

    resid = image_ref[...] - dot_exact(ritz_t, cvec_ref[...])
    search = scaled(resid, diagonal_of(tile_ref[...]))
    search_ref[...] = search
    for half, diag in ((0, diag_ref), (1, other_diag_ref)):
        take_parts(
            lambda chip: scaled(resid_ref[half, :, LANES * chip : LANES * (chip + 1)], diag[chip : chip + 1, :]),
            s_ref.at[half],
        )
    kept.append(started(s_ref, kept_ref.at[pl.ds(0, 2)], sems.at[0]))
    copies[0].wait()
    product = nt(h_vmem[0], s_ref[0])
    copies[1].wait()
    simage = fold_rows(product + nt(h_vmem[1], s_ref[1]))
    pvec = pvec_ref[...]
    terms = jnp.concatenate(
        [nt_exact(simage, search), nt_exact(simage, pvec), nt_exact(pimage_ref[...], pvec), jnp.zeros((NEIG, NEIG), F32)],
        axis=1,
    )
    packed = jnp.concatenate([terms[0:8], terms[8:16]], axis=1)
    for chip in range(CHIPS):
        sent_ref[chip] = packed
    for copy in kept:
        copy.wait()


def factor_kernel(kept_hbm, both_hbm, gram_ref, cross_ref, inverse_ref, stiff_ref, all_ref, sems):
    copies = []
    for half in range(2):
        places = (
            (kept_hbm.at[half], pl.ds(0, STACK)),
            (kept_hbm.at[2 + half], pl.ds(STACK, STACK)),
            (both_hbm.at[half], pl.ds(2 * STACK, 2 * STACK)),
        )
        for number, (source, rows) in enumerate(places):
            copies.append(started(source, all_ref.at[half, rows], sems.at[half, number]))
    for copy in copies:
        copy.wait()
    with_search = nt(all_ref[0], all_ref[0, :STACK]) + nt(all_ref[1], all_ref[1, :STACK])
    ss, i_s, cs, ps = [fold(with_search[STACK * n : STACK * (n + 1)]) for n in range(4)]
    p_image = fold(
        nt(all_ref[0, 3 * STACK :], all_ref[0, STACK : 2 * STACK]) + nt(all_ref[1, 3 * STACK :], all_ref[1, STACK : 2 * STACK])
    )
    empty = jnp.zeros((NEIG, NEIG), F32)
    cc, pc, pp = gram_ref[0], gram_ref[1], gram_ref[2]
    low = jnp.concatenate(
        [
            jnp.concatenate([0.5 * cc, cs, empty], axis=1),
            jnp.concatenate([empty, 0.5 * ss, empty], axis=1),
            jnp.concatenate([pc, ps, 0.5 * pp], axis=1),
        ],
        axis=0,
    )
    mass = low + low.T
    low = jnp.concatenate(
        [
            jnp.concatenate([0.5 * cross_ref[...], i_s, empty], axis=1),
            jnp.concatenate([empty, empty, empty], axis=1),
            jnp.concatenate([p_image, empty, empty], axis=1),
        ],
        axis=0,
    )
    stiff_ref[...] = low + low.T
    size = 3 * NEIG
    row = lax.broadcasted_iota(jnp.int32, (size, size), 0)
    column = lax.broadcasted_iota(jnp.int32, (size, size), 1)
    identity = jnp.where(row == column, 1.0, 0.0).astype(F32)
    work = jnp.concatenate([mass, identity], axis=1)
    below = lax.broadcasted_iota(jnp.int32, (size, 1), 0)
    for k in range(size):
        factor = jnp.where(below > k, work[:, k : k + 1] / work[k : k + 1, k : k + 1], 0.0)
        work = work - factor * work[k : k + 1, :]
    pivots = jnp.sum(work[:, :size] * identity, axis=1, keepdims=True)
    inverse_ref[...] = work[:, size:] / jnp.sqrt(pivots)


def finish_kernel(inverse_ref, stiff_ref, own_ref, other_ref, c_ref, s_ref, p_ref, current_ref, previous_ref):
    size = 3 * NEIG
    total = own_ref[0] + other_ref[0]
    for chip in range(1, CHIPS):
        total = total + (own_ref[chip] + other_ref[chip])
    terms = jnp.concatenate([total[:, 0 : 3 * NEIG], total[:, 4 * NEIG : 7 * NEIG]], axis=0)
    ss, sp, pp = terms[:, 0:16], terms[:, 16:32], terms[:, 32:48]
    empty = jnp.zeros((NEIG, NEIG), F32)
    up = jnp.concatenate(
        [
            jnp.zeros((NEIG, size), F32),
            jnp.concatenate([empty, 0.5 * ss, sp], axis=1),
            jnp.concatenate([empty, empty, 0.5 * pp], axis=1),
        ],
        axis=0,
    )
    stiff = stiff_ref[...] + (up + up.T)
    inverse = inverse_ref[...]
    reduced = nt_exact(dot_exact(inverse, stiff), inverse)
    row = lax.broadcasted_iota(jnp.int32, (size, size), 0)
    column = lax.broadcasted_iota(jnp.int32, (size, size), 1)
    identity = jnp.where(row == column, 1.0, 0.0).astype(F32)
    diagonal = jnp.sum(reduced * identity, axis=1, keepdims=True)
    level = jnp.max(diagonal[:NEIG], axis=0, keepdims=True)
    signed = level * identity - reduced
    square = dot_exact(signed, signed)
    total = jnp.sum(jnp.sum(signed * signed, axis=1, keepdims=True), axis=0, keepdims=True)
    square = square / total
    signed = signed / jnp.sqrt(total)
    for step in range(SIGN_STEPS):
        if step > 0:
            square = dot_exact(signed, signed)
        signed = dot_exact(signed, 1.5 * identity - 0.5 * square)
    projector = 0.5 * (identity + signed)
    wanted = jnp.where(lax.broadcasted_iota(jnp.int32, (size, size), 1) < NEIG, projector, 0.0)
    tn = (((0,), (0,)), ((), ()))
    coeffs_t = lax.dot_general(wanted, inverse, tn, precision=HIGHEST, preferred_element_type=F32)[0:NEIG]
    coeffs_t = coeffs_t * math.sqrt(ORDER)
    basis = jnp.concatenate([c_ref[...], s_ref[...], p_ref[...]], axis=0)
    current_ref[...] = dot_exact(coeffs_t, basis)[:, :ROWS]
    lane = lax.broadcasted_iota(jnp.int32, (NEIG, size), 1)
    previous_ref[...] = dot_exact(jnp.where(lane < NEIG, 0.0, coeffs_t), basis)[:, :ROWS]


def kernel_call(body, outs, args, flops, name, scratch=(), in_hbm=(), out_hbm=(), limit=LIMIT):
    return pl.pallas_call(
        body,
        out_shape=[jax.ShapeDtypeStruct(shape, kind) for shape, kind in outs],
        in_specs=[HBM if n in in_hbm else VMEM for n in range(len(args))],
        out_specs=[HBM if n in out_hbm else VMEM for n in range(len(outs))],
        scratch_shapes=scratch,
        compiler_params=pltpu.CompilerParams(vmem_limit_bytes=limit),
        cost_estimate=pl.CostEstimate(flops=flops, bytes_accessed=4 << 20, transcendentals=0),
        name=name,
    )(*args)


def to_chips(x, number):
    groups = [[2 * chip + core for chip in ORDERS[number]] for core in range(2)]
    return lax.all_to_all(x, AXIS, 0, 0, axis_index_groups=groups, tiled=True)


def to_core(x):
    return lax.ppermute(x, AXIS, [(device, device ^ 1) for device in range(DEVICES)])


def diagonal_tile(hamiltonian):
    device = lax.axis_index(AXIS)
    own_block = lax.dynamic_slice_in_dim(hamiltonian, device * ROWS, ROWS, 1)
    index = jnp.arange(ROWS)
    diag = jnp.sum(jnp.where(index[:, None] == index[None, :], own_block, 0.0), axis=0)
    rows = jnp.where(index[None, :] % NEIG == jnp.arange(NEIG)[:, None], diag[None, :], 0.0)
    lanes = (jnp.arange(LANES)[None, :] == SPARE + index[:, None] // NEIG).astype(F32)
    return dot_exact(rows, lanes)


def body(hamiltonian, current, previous):
    both = jnp.concatenate([current.T, previous.T], axis=0)
    v_own = to_chips(jnp.broadcast_to(both[None], (CHIPS, 2 * NEIG, ROWS)), 0)
    tile = diagonal_tile(hamiltonian)
    cvec = jnp.pad(current.T, ((0, 0), (0, LANES - ROWS)))
    pvec = jnp.pad(previous.T, ((0, 0), (0, LANES - ROWS)))
    h_parts = prepare(hamiltonian)
    v_own, h_parts, tile = lax.optimization_barrier((v_own, h_parts, tile))
    v_other = to_core(v_own)
    block, half, both_parts = ((NEIG, LANES), F32), ((STACK, HALF), BF16), ((2, 2 * STACK, HALF), BF16)
    half_vmem, parts_vmem = pltpu.VMEM(*half), pltpu.VMEM((2, STACK, HALF), BF16)
    h_vmem = pltpu.VMEM((2, PARTS * TALL, HALF), BF16)
    h_half = pltpu.VMEM((PARTS * TALL, HALF), BF16)
    dma = pltpu.SemaphoreType.DMA
    product, h_next = kernel_call(
        image_own_kernel,
        [((PARTS * TALL, 2 * STACK), F32), ((PARTS * TALL, HALF), BF16)],
        (h_parts, v_own),
        1 << 30,
        "image_own",
        [h_half, pltpu.VMEM((2 * STACK, HALF), BF16), dma((2,))], (0,), limit=LIMIT_IMAGE,
    )
    image, sent = kernel_call(
        image_other_kernel, [block, ((CHIPS, NEIG, LANES), F32)], (h_next, v_other, product, tile), 1 << 30, "image_other",
        [half_vmem], limit=LIMIT_IMAGE,
    )
    i_own = to_chips(sent, 1)
    p_image, both_parts, grams = kernel_call(
        previous_kernel,
        [block, both_parts, ((3, NEIG, NEIG), F32)],
        (h_parts, v_own, v_other, product),
        6 << 30,
        "previous",
        [h_half, pltpu.VMEM(*both_parts), dma((2,))], (0,), (1,),
    )
    i_own, p_image, both_parts = lax.optimization_barrier((i_own, p_image, both_parts))
    i_other = to_core(i_own)
    i_own_parts, half_cross, diag = kernel_call(
        own_kernel,
        [half, ((STACK, STACK), F32), ((CHIPS, LANES), F32)],
        (i_own, both_parts),
        1 << 30,
        "own",
        [half_vmem, dma(())], (1,), limit=LIMIT_OWN,
    )
    search, rms, cross, sent, kept = kernel_call(
        search_kernel,
        [block, ((NEIG, 1), F32), ((NEIG, NEIG), F32), ((CHIPS, 8, LANES), F32), ((4, STACK, HALF), BF16)],
        (h_parts, i_own, i_other, both_parts, i_own_parts, half_cross, diag, cvec, pvec, p_image, image, tile),
        6 << 30,
        "search",
        [h_vmem, parts_vmem, half_vmem, parts_vmem, pltpu.VMEM((2, NEIG, HALF), F32), pltpu.VMEM((CHIPS, LANES), F32), dma((4,)), dma((2,))],
        (0, 3), (4,), limit=LIMIT_SEARCH,
    )
    r_own = to_chips(sent, 2)
    square = ((3 * NEIG, 3 * NEIG), F32)
    inverse, stiff = kernel_call(
        factor_kernel, [square, square], (kept, both_parts, grams, cross), 6 << 30, "factor",
        [pltpu.VMEM((2, 4 * STACK, HALF), BF16), dma((2, 3))], (0, 1),
    )
    r_own, inverse, rms = lax.optimization_barrier((r_own, inverse, rms[:, 0]))
    r_other = to_core(r_own)
    new_current, new_previous = kernel_call(
        finish_kernel,
        [((NEIG, ROWS), F32)] * 2,
        (inverse, stiff, r_own, r_other, cvec, search, pvec),
        1 << 28,
        "finish",
        limit=8 << 20,
    )
    return new_current.T, new_previous.T, rms


def solution(mesh):
    line = Mesh(mesh.devices.reshape(DEVICES), (AXIS,))
    return jax.shard_map(
        body,
        mesh=line,
        in_specs=(P(AXIS, None), P(AXIS, None), P(AXIS, None)),
        out_specs=(P(AXIS, None), P(AXIS, None), P()),
        check_vma=False,
    )
```

```python
import math

import jax
import jax.numpy as jnp
from jax import lax
from jax.experimental import pallas as pl
from jax.experimental.pallas import tpu as pltpu
from jax.sharding import Mesh
from jax.sharding import PartitionSpec as P

NEIG = 16
SIGN_STEPS = 6
ORDER = 13824
DEVICES = 128
ROWS = ORDER // DEVICES
CHIPS = DEVICES // 2
LANES = 128
FORWARD = list(range(CHIPS))
BACKWARD = FORWARD[::-1]
ORDERS = (BACKWARD, BACKWARD, FORWARD)
SLOTS = [[order.index(chip) for chip in range(CHIPS)] for order in ORDERS]
HALF = CHIPS * LANES
TALL = 112
CHUNKS = 4
CHUNK = HALF // CHUNKS
EPS = 1e-06
AXIS = "device"

F32, BF16 = jnp.float32, jnp.bfloat16
HIGHEST = lax.Precision.HIGHEST
VMEM = pl.BlockSpec(memory_space=pltpu.VMEM)
HBM = pl.BlockSpec(memory_space=pltpu.HBM)
LIMIT = 53 << 20
LIMIT_IMAGE = 48 << 20
LIMIT_SEARCH = 52 << 20
LIMIT_OWN = 52 << 20
PARTS = 2
STACK = PARTS * NEIG
SPARE = ROWS


def split(x):
    high = x.astype(BF16)
    return high, (x - high.astype(F32)).astype(BF16)


def split3(x):
    high = x.astype(BF16)
    rest = x - high.astype(F32)
    mid = rest.astype(BF16)
    return high, mid, (rest - mid.astype(F32)).astype(BF16)


def nt(left, right):
    return lax.dot_general(left, right, (((1,), (1,)), ((), ())), preferred_element_type=F32)


def nt_exact(left, right):
    return lax.dot_general(left, right, (((1,), (1,)), ((), ())), precision=HIGHEST, preferred_element_type=F32)


def dot_exact(left, right):
    return jnp.dot(left, right, precision=HIGHEST, preferred_element_type=F32)


def fold(parts):
    rows = parts[16:32] + parts[0:16]
    return rows[:, 16:32] + rows[:, 0:16]


def fold_rows(product):
    rows = product[TALL:] + product[:TALL]
    wide = jnp.concatenate([rows, jnp.zeros((TALL, LANES - STACK), F32)], axis=1)
    turned = jnp.concatenate([wide, jnp.zeros((LANES - TALL, LANES), F32)], axis=0).T
    return real_lanes(turned[16:32] + turned[0:16])


def real_lanes(tile):
    lane = lax.broadcasted_iota(jnp.int32, tile.shape, 1)
    return jnp.where(lane < ROWS, tile, 0.0)


def padded(tile):
    return jnp.concatenate([tile, jnp.zeros((tile.shape[0], LANES - ROWS), F32)], axis=1)


def prepare_kernel(h_ref, parts_ref):
    core = lax.rem(lax.axis_index(AXIS), 2)
    for block in range(2 * CHIPS // CHUNKS):
        chip, owner = divmod(block, 2)
        half = jnp.where(core == owner, 0, 1)
        x = padded(h_ref[:, ROWS * block : ROWS * block + ROWS])
        for number, part in enumerate(split(x)):
            parts_ref[half, TALL * number : TALL * number + ROWS, LANES * chip : LANES * (chip + 1)] = part


def prepare(hamiltonian):
    return pl.pallas_call(
        prepare_kernel,
        grid=(CHUNKS,),
        out_shape=jax.ShapeDtypeStruct((2, PARTS * TALL, HALF), BF16),
        in_specs=[pl.BlockSpec((ROWS, ORDER // CHUNKS), lambda i: (0, i))],
        out_specs=pl.BlockSpec((2, PARTS * TALL, CHUNK), lambda i: (0, 0, i)),
        compiler_params=pltpu.CompilerParams(vmem_limit_bytes=58 << 20),
        cost_estimate=pl.CostEstimate(flops=20 * ROWS * ORDER, bytes_accessed=10 * ROWS * ORDER, transcendentals=0),
        name="prepare",
    )(hamiltonian)


def started(source, target, sem):
    copy = pltpu.make_async_copy(source, target, sem)
    copy.start()
    return copy


def take_parts(tile_of, parts_ref):
    for chip in range(CHIPS):
        for number, part in enumerate(split(tile_of(chip))):
            parts_ref[NEIG * number : NEIG * (number + 1), LANES * chip : LANES * (chip + 1)] = part


def take_both(tile_of, first_ref, second_ref):
    for chip in range(CHIPS):
        lanes = slice(LANES * chip, LANES * (chip + 1))
        for number, part in enumerate(split(tile_of(chip))):
            first_ref[NEIG * number : NEIG * (number + 1), lanes] = part[:NEIG]
            second_ref[NEIG * number : NEIG * (number + 1), lanes] = part[NEIG:]


def stacked_dot(left, right):
    high, low = split(left)
    right_high, right_low = split(right)
    both = jnp.dot(jnp.concatenate([high, low], axis=0), right_high, preferred_element_type=F32)
    size = left.shape[0]
    return both[:size] + (both[size:] + jnp.dot(high, right_low, preferred_element_type=F32))


def eliminated(matrix):
    size = matrix.shape[0]
    row = lax.broadcasted_iota(jnp.int32, (size, size), 0)
    column = lax.broadcasted_iota(jnp.int32, (size, size), 1)
    identity = jnp.where(row == column, 1.0, 0.0).astype(F32)
    work = jnp.concatenate([matrix, identity], axis=1)
    below = lax.broadcasted_iota(jnp.int32, (size, 1), 0)
    for k in range(size):
        factor = jnp.where(below > k, work[:, k : k + 1] / work[k : k + 1, k : k + 1], 0.0)
        work = work - factor * work[k : k + 1, :]
    pivots = jnp.sum(work[:, :size] * identity, axis=1, keepdims=True)
    return work[:, size:] / jnp.sqrt(pivots)


def joined(blocks):
    return jnp.concatenate([jnp.concatenate(row, axis=1) for row in blocks], axis=0)


def image_own_kernel(h_ref, own_ref, product_ref, next_ref, h_vmem, parts, sems):
    copy = started(h_ref.at[0], h_vmem, sems.at[0])
    following = started(h_ref.at[1], next_ref, sems.at[1])
    take_both(lambda chip: padded(own_ref[SLOTS[0][chip]]), parts.at[pl.ds(0, STACK)], parts.at[pl.ds(STACK, STACK)])
    copy.wait()
    product_ref[...] = nt(h_vmem[...], parts[...])
    following.wait()


def image_other_kernel(h_ref, other_ref, product_ref, tile_ref, image_ref, sent_ref, parts):
    take_parts(lambda chip: padded(other_ref[SLOTS[0][chip], 0:NEIG]), parts)
    image = fold_rows(product_ref[:, 0:STACK] + nt(h_ref[...], parts[...]))
    image_ref[...] = image
    sent = image + tile_ref[...]
    for chip in range(CHIPS):
        sent_ref[chip] = sent


def previous_kernel(h_ref, own_ref, other_ref, product_ref, image_ref, c_out, p_out, inverse_ref, h_vmem, c_ref, p_ref, sems):
    copy = started(h_ref.at[1], h_vmem, sems.at[0])
    take_both(lambda chip: padded(own_ref[SLOTS[0][chip]]), c_ref.at[0], p_ref.at[0])
    take_both(lambda chip: padded(other_ref[SLOTS[0][chip]]), c_ref.at[1], p_ref.at[1])
    out_c = started(c_ref, c_out, sems.at[1])
    out_p = started(p_ref, p_out, sems.at[2])
    cc = fold(nt(c_ref[0], c_ref[0]) + nt(c_ref[1], c_ref[1]))
    pc = fold(nt(p_ref[0], c_ref[0]) + nt(p_ref[1], c_ref[1]))
    pp = fold(nt(p_ref[0], p_ref[0]) + nt(p_ref[1], p_ref[1]))
    empty = jnp.zeros((NEIG, NEIG), F32)
    low = joined([[0.5 * cc, empty], [pc, 0.5 * pp]])
    inverse_ref[...] = eliminated(low + low.T)
    copy.wait()
    image_ref[...] = fold_rows(product_ref[:, STACK:] + nt(h_vmem[...], p_ref[1]))
    out_c.wait()
    out_p.wait()


def diagonal_of(tile):
    row = lax.broadcasted_iota(jnp.int32, (NEIG, LANES), 0)
    lane = lax.broadcasted_iota(jnp.int32, (NEIG, LANES), 1)
    spread = jnp.take_along_axis(tile, SPARE + lane // NEIG, axis=1)
    return jnp.sum(jnp.where(lane % NEIG == row, spread, 0.0), axis=0, keepdims=True)


def own_kernel(own_ref, c_hbm, i_ref, cross_ref, diag_ref, c_ref, sem):
    copy = started(c_hbm.at[0], c_ref, sem)
    take_parts(lambda chip: real_lanes(own_ref[SLOTS[1][chip]]), i_ref)
    for chip in range(CHIPS):
        diag_ref[chip : chip + 1, :] = diagonal_of(own_ref[SLOTS[1][chip]])
    copy.wait()
    cross_ref[...] = nt(i_ref[...], c_ref[...])


def search_kernel(
    h_ref, own_ref, other_ref, c_hbm, i_own_ref, half_cross_ref, diag_ref, cvec_ref, pvec_ref, pimage_ref, image_ref, tile_ref,
    search_ref, rms_ref, cross_ref, sent_ref, kept_ref,
    h_vmem, c_ref, i_ref, s_ref, resid_ref, other_diag_ref, sems, h_sems, c_sem,
):
    copy_c = started(c_hbm, c_ref, c_sem)
    copies = [started(h_ref.at[half], h_vmem.at[half], h_sems.at[half]) for half in range(2)]
    take_parts(lambda chip: real_lanes(other_ref[SLOTS[1][chip]]), i_ref)
    for chip in range(CHIPS):
        other_diag_ref[chip : chip + 1, :] = diagonal_of(other_ref[SLOTS[1][chip]])
    copy_c.wait()
    kept = [started(i_own_ref, kept_ref.at[2], sems.at[1]), started(i_ref, kept_ref.at[3], sems.at[2])]
    cross_t = fold(half_cross_ref[...] + nt(i_ref[...], c_ref[1]))
    cross_ref[...] = cross_t
    ritz_t = cross_t / ORDER
    stacked = jnp.concatenate(split3(ritz_t), axis=0)
    stacked = jnp.concatenate([stacked] * PARTS, axis=1)
    square = jnp.zeros((NEIG, LANES), F32)
    for half, ref in ((0, own_ref), (1, other_ref)):
        moved = jnp.dot(stacked, c_ref[half], preferred_element_type=F32)
        moved = (moved[32:48] + moved[16:32]) + moved[0:16]
        part = jnp.zeros((NEIG, LANES), F32)
        for chip in range(CHIPS):
            lanes = slice(LANES * chip, LANES * (chip + 1))
            resid = real_lanes(ref[SLOTS[1][chip]]) - moved[:, lanes]
            resid_ref[half, :, lanes] = resid
            part = part + resid * resid
        square = square + part
    rms = jnp.sqrt(jnp.sum(square, axis=1, keepdims=True) / ORDER + EPS)
    rms_ref[...] = rms
    row = lax.broadcasted_iota(jnp.int32, (NEIG, NEIG), 0)
    column = lax.broadcasted_iota(jnp.int32, (NEIG, NEIG), 1)
    value = jnp.sum(jnp.where(row == column, ritz_t, 0.0), axis=1, keepdims=True)
    value = jnp.broadcast_to(value, (NEIG, LANES))
    rms = jnp.broadcast_to(rms, (NEIG, LANES))

    def scaled(resid, diag):
        return resid / (jnp.maximum(jnp.abs(diag - value), 1.0) * rms)

    resid = image_ref[...] - dot_exact(ritz_t, cvec_ref[...])
    search = scaled(resid, diagonal_of(tile_ref[...]))
    search_ref[...] = search
    for half, diag in ((0, diag_ref), (1, other_diag_ref)):
        take_parts(
            lambda chip: scaled(resid_ref[half, :, LANES * chip : LANES * (chip + 1)], diag[chip : chip + 1, :]),
            s_ref.at[half],
        )
    kept.append(started(s_ref, kept_ref.at[pl.ds(0, 2)], sems.at[0]))
    copies[0].wait()
    product = nt(h_vmem[0], s_ref[0])
    copies[1].wait()
    simage = fold_rows(product + nt(h_vmem[1], s_ref[1]))
    pvec = pvec_ref[...]
    terms = jnp.concatenate(
        [nt_exact(simage, search), nt_exact(simage, pvec), nt_exact(pimage_ref[...], pvec), jnp.zeros((NEIG, NEIG), F32)],
        axis=1,
    )
    packed = jnp.concatenate([terms[0:8], terms[8:16]], axis=1)
    for chip in range(CHIPS):
        sent_ref[chip] = packed
    for copy in kept:
        copy.wait()


def factor_kernel(kept_hbm, c_hbm, p_hbm, first_ref, cross_ref, inverse_ref, stiff_ref, all_ref, sems):
    copies = []
    for half in range(2):
        for number, source in enumerate((kept_hbm.at[half], kept_hbm.at[2 + half], c_hbm.at[half], p_hbm.at[half])):
            copies.append(started(source, all_ref.at[half, pl.ds(STACK * number, STACK)], sems.at[half, number]))
    with_search, p_image = None, None
    for half in range(2):
        for copy in copies[4 * half : 4 * half + 4]:
            copy.wait()
        terms = nt(all_ref[half], all_ref[half, :STACK])
        with_search = terms if half == 0 else with_search + terms
        terms = nt(all_ref[half, 3 * STACK :], all_ref[half, STACK : 2 * STACK])
        p_image = terms if half == 0 else p_image + terms
    ss, i_s, cs, ps = [fold(with_search[STACK * n : STACK * (n + 1)]) for n in range(4)]
    first = first_ref[...]
    row = nt_exact(jnp.concatenate([cs.T, ps.T], axis=1), first)
    last = eliminated(ss - nt_exact(row, row))
    inverse_ref[...] = joined(
        [[first, jnp.zeros((2 * NEIG, NEIG), F32)], [-dot_exact(last, dot_exact(row, first)), last]]
    )
    empty = jnp.zeros((NEIG, NEIG), F32)
    low = joined([[0.5 * cross_ref[...], empty, i_s], [fold(p_image), empty, empty], [empty, empty, empty]])
    stiff_ref[...] = low + low.T


def finish_kernel(inverse_ref, stiff_ref, own_ref, other_ref, c_ref, s_ref, p_ref, current_ref, previous_ref):
    size = 3 * NEIG
    total = own_ref[0] + other_ref[0]
    for chip in range(1, CHIPS):
        total = total + (own_ref[chip] + other_ref[chip])
    terms = jnp.concatenate([total[:, 0 : 3 * NEIG], total[:, 4 * NEIG : 7 * NEIG]], axis=0)
    ss, sp, pp = terms[:, 0:16], terms[:, 16:32], terms[:, 32:48]
    empty = jnp.zeros((NEIG, NEIG), F32)
    low = joined([[empty, empty, empty], [empty, 0.5 * pp, empty], [empty, sp, 0.5 * ss]])
    stiff = stiff_ref[...] + (low + low.T)
    inverse = inverse_ref[...]
    reduced = nt_exact(dot_exact(inverse, stiff), inverse)
    row = lax.broadcasted_iota(jnp.int32, (size, size), 0)
    column = lax.broadcasted_iota(jnp.int32, (size, size), 1)
    identity = jnp.where(row == column, 1.0, 0.0).astype(F32)
    diagonal = jnp.sum(reduced * identity, axis=1, keepdims=True)
    level = jnp.max(diagonal[:NEIG], axis=0, keepdims=True)
    signed = level * identity - reduced
    square = stacked_dot(signed, signed)
    total = jnp.sum(jnp.sum(signed * signed, axis=1, keepdims=True), axis=0, keepdims=True)
    square = square / total
    signed = signed / jnp.sqrt(total)
    for step in range(SIGN_STEPS):
        if step > 0:
            square = stacked_dot(signed, signed)
        signed = stacked_dot(signed, 1.5 * identity - 0.5 * square)
    projector = 0.5 * (identity + signed)
    wanted = jnp.where(lax.broadcasted_iota(jnp.int32, (size, size), 1) < NEIG, projector, 0.0)
    tn = (((0,), (0,)), ((), ()))
    coeffs_t = lax.dot_general(wanted, inverse, tn, precision=HIGHEST, preferred_element_type=F32)[0:NEIG]
    coeffs_t = coeffs_t * math.sqrt(ORDER)
    basis = jnp.concatenate([c_ref[...], p_ref[...], s_ref[...]], axis=0)
    current_ref[...] = dot_exact(coeffs_t, basis)[:, :ROWS]
    lane = lax.broadcasted_iota(jnp.int32, (NEIG, size), 1)
    previous_ref[...] = dot_exact(jnp.where(lane < NEIG, 0.0, coeffs_t), basis)[:, :ROWS]


def kernel_call(body, outs, args, flops, name, scratch=(), in_hbm=(), out_hbm=(), limit=LIMIT):
    return pl.pallas_call(
        body,
        out_shape=[jax.ShapeDtypeStruct(shape, kind) for shape, kind in outs],
        in_specs=[HBM if n in in_hbm else VMEM for n in range(len(args))],
        out_specs=[HBM if n in out_hbm else VMEM for n in range(len(outs))],
        scratch_shapes=scratch,
        compiler_params=pltpu.CompilerParams(vmem_limit_bytes=limit),
        cost_estimate=pl.CostEstimate(flops=flops, bytes_accessed=4 << 20, transcendentals=0),
        name=name,
    )(*args)


def to_chips(x, number):
    groups = [[2 * chip + core for chip in ORDERS[number]] for core in range(2)]
    return lax.all_to_all(x, AXIS, 0, 0, axis_index_groups=groups, tiled=True)


def to_core(x):
    return lax.ppermute(x, AXIS, [(device, device ^ 1) for device in range(DEVICES)])


def diagonal_tile(hamiltonian):
    device = lax.axis_index(AXIS)
    own_block = lax.dynamic_slice_in_dim(hamiltonian, device * ROWS, ROWS, 1)
    index = jnp.arange(ROWS)
    diag = jnp.sum(jnp.where(index[:, None] == index[None, :], own_block, 0.0), axis=0)
    rows = jnp.where(index[None, :] % NEIG == jnp.arange(NEIG)[:, None], diag[None, :], 0.0)
    lanes = (jnp.arange(LANES)[None, :] == SPARE + index[:, None] // NEIG).astype(F32)
    return dot_exact(rows, lanes)


def body(hamiltonian, current, previous):
    both = jnp.concatenate([current.T, previous.T], axis=0)
    v_own = to_chips(jnp.broadcast_to(both[None], (CHIPS, 2 * NEIG, ROWS)), 0)
    tile = diagonal_tile(hamiltonian)
    cvec = jnp.pad(current.T, ((0, 0), (0, LANES - ROWS)))
    pvec = jnp.pad(previous.T, ((0, 0), (0, LANES - ROWS)))
    h_parts = prepare(hamiltonian)
    v_own, h_parts, tile = lax.optimization_barrier((v_own, h_parts, tile))
    v_other = to_core(v_own)
    block, half, parts = ((NEIG, LANES), F32), ((STACK, HALF), BF16), ((2, STACK, HALF), BF16)
    half_vmem, parts_vmem = pltpu.VMEM(*half), pltpu.VMEM(*parts)
    h_vmem = pltpu.VMEM((2, PARTS * TALL, HALF), BF16)
    h_half = pltpu.VMEM((PARTS * TALL, HALF), BF16)
    dma = pltpu.SemaphoreType.DMA
    product, h_next = kernel_call(
        image_own_kernel,
        [((PARTS * TALL, 2 * STACK), F32), ((PARTS * TALL, HALF), BF16)],
        (h_parts, v_own),
        1 << 30,
        "image_own",
        [h_half, pltpu.VMEM((2 * STACK, HALF), BF16), dma((2,))], (0,), limit=LIMIT_IMAGE,
    )
    image, sent = kernel_call(
        image_other_kernel, [block, ((CHIPS, NEIG, LANES), F32)], (h_next, v_other, product, tile), 1 << 30, "image_other",
        [half_vmem], limit=LIMIT_IMAGE,
    )
    i_own = to_chips(sent, 1)
    p_image, c_parts, p_parts, first = kernel_call(
        previous_kernel,
        [block, parts, parts, ((2 * NEIG, 2 * NEIG), F32)],
        (h_parts, v_own, v_other, product),
        6 << 30,
        "previous",
        [h_half, parts_vmem, parts_vmem, dma((3,))], (0,), (1, 2),
    )
    i_own, p_image, c_parts = lax.optimization_barrier((i_own, p_image, c_parts))
    i_other = to_core(i_own)
    i_own_parts, half_cross, diag = kernel_call(
        own_kernel,
        [half, ((STACK, STACK), F32), ((CHIPS, LANES), F32)],
        (i_own, c_parts),
        1 << 30,
        "own",
        [half_vmem, dma(())], (1,), limit=LIMIT_OWN,
    )
    search, rms, cross, sent, kept = kernel_call(
        search_kernel,
        [block, ((NEIG, 1), F32), ((NEIG, NEIG), F32), ((CHIPS, 8, LANES), F32), ((4, STACK, HALF), BF16)],
        (h_parts, i_own, i_other, c_parts, i_own_parts, half_cross, diag, cvec, pvec, p_image, image, tile),
        6 << 30,
        "search",
        [h_vmem, parts_vmem, half_vmem, parts_vmem, pltpu.VMEM((2, NEIG, HALF), F32), pltpu.VMEM((CHIPS, LANES), F32), dma((3,)), dma((2,)), dma(())],
        (0, 3), (4,), limit=LIMIT_SEARCH,
    )
    r_own = to_chips(sent, 2)
    square = ((3 * NEIG, 3 * NEIG), F32)
    inverse, stiff = kernel_call(
        factor_kernel, [square, square], (kept, c_parts, p_parts, first, cross), 6 << 30, "factor",
        [pltpu.VMEM((2, 4 * STACK, HALF), BF16), dma((2, 4))], (0, 1, 2),
    )
    r_own, inverse, rms = lax.optimization_barrier((r_own, inverse, rms[:, 0]))
    r_other = to_core(r_own)
    new_current, new_previous = kernel_call(
        finish_kernel,
        [((NEIG, ROWS), F32)] * 2,
        (inverse, stiff, r_own, r_other, cvec, search, pvec),
        1 << 28,
        "finish",
        limit=8 << 20,
    )
    return new_current.T, new_previous.T, rms


def solution(mesh):
    line = Mesh(mesh.devices.reshape(DEVICES), (AXIS,))
    return jax.shard_map(
        body,
        mesh=line,
        in_specs=(P(AXIS, None), P(AXIS, None), P(AXIS, None)),
        out_specs=(P(AXIS, None), P(AXIS, None), P()),
        check_vma=False,
    )
```

```python
import math

import jax
import jax.numpy as jnp
from jax import lax
from jax.experimental import pallas as pl
from jax.experimental.pallas import tpu as pltpu
from jax.sharding import Mesh
from jax.sharding import PartitionSpec as P

NEIG = 16
SIGN_STEPS = 6
ORDER = 13824
DEVICES = 128
ROWS = ORDER // DEVICES
CHIPS = DEVICES // 2
LANES = 128
FORWARD = list(range(CHIPS))
BACKWARD = FORWARD[::-1]
ORDERS = (BACKWARD, BACKWARD, BACKWARD)
SLOTS = [[order.index(chip) for chip in range(CHIPS)] for order in ORDERS]
HALF = CHIPS * LANES
TALL = 112
CHUNKS = 4
CHUNK = HALF // CHUNKS
EPS = 1e-06
AXIS = "device"

F32, BF16 = jnp.float32, jnp.bfloat16
HIGHEST = lax.Precision.HIGHEST
VMEM = pl.BlockSpec(memory_space=pltpu.VMEM)
HBM = pl.BlockSpec(memory_space=pltpu.HBM)
LIMIT = 53 << 20
LIMIT_IMAGE = 48 << 20
LIMIT_SEARCH = 52 << 20
LIMIT_OWN = 52 << 20
PARTS = 2
STACK = PARTS * NEIG
SPARE = ROWS


def split(x):
    high = x.astype(BF16)
    return high, (x - high.astype(F32)).astype(BF16)


def split3(x):
    high = x.astype(BF16)
    rest = x - high.astype(F32)
    mid = rest.astype(BF16)
    return high, mid, (rest - mid.astype(F32)).astype(BF16)


def nt(left, right):
    return lax.dot_general(left, right, (((1,), (1,)), ((), ())), preferred_element_type=F32)


def nt_exact(left, right):
    return lax.dot_general(left, right, (((1,), (1,)), ((), ())), precision=HIGHEST, preferred_element_type=F32)


def dot_exact(left, right):
    return jnp.dot(left, right, precision=HIGHEST, preferred_element_type=F32)


def fold(parts):
    rows = parts[16:32] + parts[0:16]
    return rows[:, 16:32] + rows[:, 0:16]


def fold_rows(product):
    rows = product[TALL:] + product[:TALL]
    wide = jnp.concatenate([rows, jnp.zeros((TALL, LANES - STACK), F32)], axis=1)
    turned = jnp.concatenate([wide, jnp.zeros((LANES - TALL, LANES), F32)], axis=0).T
    return real_lanes(turned[16:32] + turned[0:16])


def real_lanes(tile):
    lane = lax.broadcasted_iota(jnp.int32, tile.shape, 1)
    return jnp.where(lane < ROWS, tile, 0.0)


def padded(tile):
    return jnp.concatenate([tile, jnp.zeros((tile.shape[0], LANES - ROWS), F32)], axis=1)


def prepare_kernel(h_ref, parts_ref):
    core = lax.rem(lax.axis_index(AXIS), 2)
    for block in range(2 * CHIPS // CHUNKS):
        chip, owner = divmod(block, 2)
        half = jnp.where(core == owner, 0, 1)
        x = padded(h_ref[:, ROWS * block : ROWS * block + ROWS])
        for number, part in enumerate(split(x)):
            parts_ref[half, TALL * number : TALL * number + ROWS, LANES * chip : LANES * (chip + 1)] = part


def prepare(hamiltonian):
    return pl.pallas_call(
        prepare_kernel,
        grid=(CHUNKS,),
        out_shape=jax.ShapeDtypeStruct((2, PARTS * TALL, HALF), BF16),
        in_specs=[pl.BlockSpec((ROWS, ORDER // CHUNKS), lambda i: (0, i))],
        out_specs=pl.BlockSpec((2, PARTS * TALL, CHUNK), lambda i: (0, 0, i)),
        compiler_params=pltpu.CompilerParams(vmem_limit_bytes=58 << 20),
        cost_estimate=pl.CostEstimate(flops=20 * ROWS * ORDER, bytes_accessed=10 * ROWS * ORDER, transcendentals=0),
        name="prepare",
    )(hamiltonian)


def started(source, target, sem):
    copy = pltpu.make_async_copy(source, target, sem)
    copy.start()
    return copy


def take_parts(tile_of, parts_ref):
    for chip in range(CHIPS):
        for number, part in enumerate(split(tile_of(chip))):
            parts_ref[NEIG * number : NEIG * (number + 1), LANES * chip : LANES * (chip + 1)] = part


def take_both(tile_of, first_ref, second_ref):
    for chip in range(CHIPS):
        lanes = slice(LANES * chip, LANES * (chip + 1))
        for number, part in enumerate(split(tile_of(chip))):
            first_ref[NEIG * number : NEIG * (number + 1), lanes] = part[:NEIG]
            second_ref[NEIG * number : NEIG * (number + 1), lanes] = part[NEIG:]


def stacked_dot(left, right):
    high, low = split(left)
    right_high, right_low = split(right)
    both = jnp.dot(jnp.concatenate([high, low], axis=0), right_high, preferred_element_type=F32)
    size = left.shape[0]
    return both[:size] + (both[size:] + jnp.dot(high, right_low, preferred_element_type=F32))


def eliminated(matrix):
    size = matrix.shape[0]
    row = lax.broadcasted_iota(jnp.int32, (size, size), 0)
    column = lax.broadcasted_iota(jnp.int32, (size, size), 1)
    identity = jnp.where(row == column, 1.0, 0.0).astype(F32)
    work = jnp.concatenate([matrix, identity], axis=1)
    below = lax.broadcasted_iota(jnp.int32, (size, 1), 0)
    for k in range(size):
        factor = jnp.where(below > k, work[:, k : k + 1] / work[k : k + 1, k : k + 1], 0.0)
        work = work - factor * work[k : k + 1, :]
    pivots = jnp.sum(work[:, :size] * identity, axis=1, keepdims=True)
    return work[:, size:] / jnp.sqrt(pivots)


def joined(blocks):
    return jnp.concatenate([jnp.concatenate(row, axis=1) for row in blocks], axis=0)


def image_own_kernel(h_ref, own_ref, product_ref, next_ref, h_vmem, parts, sems):
    copy = started(h_ref.at[0], h_vmem, sems.at[0])
    following = started(h_ref.at[1], next_ref, sems.at[1])
    take_both(lambda chip: padded(own_ref[SLOTS[0][chip]]), parts.at[pl.ds(0, STACK)], parts.at[pl.ds(STACK, STACK)])
    copy.wait()
    product_ref[...] = nt(h_vmem[...], parts[...])
    following.wait()


def image_other_kernel(h_ref, other_ref, product_ref, tile_ref, image_ref, sent_ref, parts):
    take_parts(lambda chip: padded(other_ref[SLOTS[0][chip], 0:NEIG]), parts)
    image = fold_rows(product_ref[:, 0:STACK] + nt(h_ref[...], parts[...]))
    image_ref[...] = image
    sent = image + tile_ref[...]
    for chip in range(CHIPS):
        sent_ref[chip] = sent


def previous_kernel(h_ref, own_ref, other_ref, product_ref, image_ref, c_out, p_out, inverse_ref, h_vmem, c_ref, p_ref, sems):
    copy = started(h_ref.at[1], h_vmem, sems.at[0])
    take_both(lambda chip: padded(own_ref[SLOTS[0][chip]]), c_ref.at[0], p_ref.at[0])
    take_both(lambda chip: padded(other_ref[SLOTS[0][chip]]), c_ref.at[1], p_ref.at[1])
    out_c = started(c_ref, c_out, sems.at[1])
    out_p = started(p_ref, p_out, sems.at[2])
    cc = fold(nt(c_ref[0], c_ref[0]) + nt(c_ref[1], c_ref[1]))
    pc = fold(nt(p_ref[0], c_ref[0]) + nt(p_ref[1], c_ref[1]))
    pp = fold(nt(p_ref[0], p_ref[0]) + nt(p_ref[1], p_ref[1]))
    empty = jnp.zeros((NEIG, NEIG), F32)
    low = joined([[0.5 * cc, empty], [pc, 0.5 * pp]])
    copy.wait()
    image_ref[...] = fold_rows(product_ref[:, STACK:] + nt(h_vmem[...], p_ref[1]))
    inverse_ref[...] = eliminated(low + low.T)
    out_c.wait()
    out_p.wait()


def diagonal_of(tile):
    row = lax.broadcasted_iota(jnp.int32, (NEIG, LANES), 0)
    lane = lax.broadcasted_iota(jnp.int32, (NEIG, LANES), 1)
    spread = jnp.take_along_axis(tile, SPARE + lane // NEIG, axis=1)
    return jnp.sum(jnp.where(lane % NEIG == row, spread, 0.0), axis=0, keepdims=True)


def own_kernel(own_ref, c_hbm, i_ref, cross_ref, diag_ref, c_ref, sem):
    copy = started(c_hbm.at[0], c_ref, sem)
    take_parts(lambda chip: real_lanes(own_ref[SLOTS[1][chip]]), i_ref)
    for chip in range(CHIPS):
        diag_ref[chip : chip + 1, :] = diagonal_of(own_ref[SLOTS[1][chip]])
    copy.wait()
    cross_ref[...] = nt(i_ref[...], c_ref[...])


def search_kernel(
    h_ref, own_ref, other_ref, c_hbm, i_own_ref, half_cross_ref, diag_ref, cvec_ref, pvec_ref, pimage_ref, image_ref, tile_ref,
    search_ref, rms_ref, cross_ref, sent_ref, kept_ref,
    h_vmem, c_ref, i_ref, s_ref, resid_ref, other_diag_ref, sems, h_sems, c_sem,
):
    copy_c = started(c_hbm, c_ref, c_sem)
    copies = [started(h_ref.at[half], h_vmem.at[half], h_sems.at[half]) for half in range(2)]
    take_parts(lambda chip: real_lanes(other_ref[SLOTS[1][chip]]), i_ref)
    for chip in range(CHIPS):
        other_diag_ref[chip : chip + 1, :] = diagonal_of(other_ref[SLOTS[1][chip]])
    copy_c.wait()
    kept = [started(i_own_ref, kept_ref.at[2], sems.at[1]), started(i_ref, kept_ref.at[3], sems.at[2])]
    cross_t = fold(half_cross_ref[...] + nt(i_ref[...], c_ref[1]))
    cross_ref[...] = cross_t
    ritz_t = cross_t / ORDER
    stacked = jnp.concatenate(split3(ritz_t), axis=0)
    stacked = jnp.concatenate([stacked] * PARTS, axis=1)
    square = jnp.zeros((NEIG, LANES), F32)
    for half, ref in ((0, own_ref), (1, other_ref)):
        moved = jnp.dot(stacked, c_ref[half], preferred_element_type=F32)
        moved = (moved[32:48] + moved[16:32]) + moved[0:16]
        part = jnp.zeros((NEIG, LANES), F32)
        for chip in range(CHIPS):
            lanes = slice(LANES * chip, LANES * (chip + 1))
            resid = real_lanes(ref[SLOTS[1][chip]]) - moved[:, lanes]
            resid_ref[half, :, lanes] = resid
            part = part + resid * resid
        square = square + part
    rms = jnp.sqrt(jnp.sum(square, axis=1, keepdims=True) / ORDER + EPS)
    row = lax.broadcasted_iota(jnp.int32, (NEIG, NEIG), 0)
    column = lax.broadcasted_iota(jnp.int32, (NEIG, NEIG), 1)
    rms_ref[...] = jnp.sum(jnp.where(row == column, rms, 0.0), axis=0)
    value = jnp.sum(jnp.where(row == column, ritz_t, 0.0), axis=1, keepdims=True)
    value = jnp.broadcast_to(value, (NEIG, LANES))
    rms = jnp.broadcast_to(rms, (NEIG, LANES))

    def scaled(resid, diag):
        return resid / (jnp.maximum(jnp.abs(diag - value), 1.0) * rms)

    resid = image_ref[...] - dot_exact(ritz_t, cvec_ref[...])
    search = scaled(resid, diagonal_of(tile_ref[...]))
    search_ref[...] = search
    for half, diag in ((0, diag_ref), (1, other_diag_ref)):
        take_parts(
            lambda chip: scaled(resid_ref[half, :, LANES * chip : LANES * (chip + 1)], diag[chip : chip + 1, :]),
            s_ref.at[half],
        )
    kept.append(started(s_ref, kept_ref.at[pl.ds(0, 2)], sems.at[0]))
    copies[0].wait()
    product = nt(h_vmem[0], s_ref[0])
    copies[1].wait()
    simage = fold_rows(product + nt(h_vmem[1], s_ref[1]))
    pvec = pvec_ref[...]
    terms = jnp.concatenate(
        [nt_exact(simage, search), nt_exact(simage, pvec), nt_exact(pimage_ref[...], pvec), jnp.zeros((NEIG, NEIG), F32)],
        axis=1,
    )
    packed = jnp.concatenate([terms[0:8], terms[8:16]], axis=1)
    for chip in range(CHIPS):
        sent_ref[chip] = packed
    for copy in kept:
        copy.wait()


def factor_kernel(kept_hbm, c_hbm, p_hbm, first_ref, cross_ref, inverse_ref, stiff_ref, all_ref, sems):
    copies = []
    for half in range(2):
        for number, source in enumerate((kept_hbm.at[half], kept_hbm.at[2 + half], c_hbm.at[half], p_hbm.at[half])):
            copies.append(started(source, all_ref.at[half, pl.ds(STACK * number, STACK)], sems.at[half, number]))
    with_search, p_image = None, None
    for half in range(2):
        for copy in copies[4 * half : 4 * half + 4]:
            copy.wait()
        terms = nt(all_ref[half], all_ref[half, :STACK])
        with_search = terms if half == 0 else with_search + terms
        terms = nt(all_ref[half, 3 * STACK :], all_ref[half, STACK : 2 * STACK])
        p_image = terms if half == 0 else p_image + terms
    ss, i_s, cs, ps = [fold(with_search[STACK * n : STACK * (n + 1)]) for n in range(4)]
    first = first_ref[...]
    row = nt_exact(jnp.concatenate([cs.T, ps.T], axis=1), first)
    last = eliminated(ss - nt_exact(row, row))
    inverse_ref[...] = joined(
        [[first, jnp.zeros((2 * NEIG, NEIG), F32)], [-dot_exact(last, dot_exact(row, first)), last]]
    )
    empty = jnp.zeros((NEIG, NEIG), F32)
    low = joined([[0.5 * cross_ref[...], empty, i_s], [fold(p_image), empty, empty], [empty, empty, empty]])
    stiff_ref[...] = low + low.T


def finish_kernel(inverse_ref, stiff_ref, own_ref, other_ref, c_ref, s_ref, p_ref, current_ref, previous_ref):
    size = 3 * NEIG
    total = own_ref[0] + other_ref[0]
    for chip in range(1, CHIPS):
        total = total + (own_ref[chip] + other_ref[chip])
    terms = jnp.concatenate([total[:, 0 : 3 * NEIG], total[:, 4 * NEIG : 7 * NEIG]], axis=0)
    ss, sp, pp = terms[:, 0:16], terms[:, 16:32], terms[:, 32:48]
    empty = jnp.zeros((NEIG, NEIG), F32)
    low = joined([[empty, empty, empty], [empty, 0.5 * pp, empty], [empty, sp, 0.5 * ss]])
    stiff = stiff_ref[...] + (low + low.T)
    inverse = inverse_ref[...]
    basis = jnp.concatenate([c_ref[...], p_ref[...], s_ref[...]], axis=0)
    rotated = dot_exact(inverse, basis)
    rotated_rest = dot_exact(jnp.where(lax.broadcasted_iota(jnp.int32, (size, size), 1) < NEIG, 0.0, inverse), basis)
    reduced = nt_exact(dot_exact(inverse, stiff), inverse)
    row = lax.broadcasted_iota(jnp.int32, (size, size), 0)
    column = lax.broadcasted_iota(jnp.int32, (size, size), 1)
    identity = jnp.where(row == column, 1.0, 0.0).astype(F32)
    diagonal = jnp.sum(reduced * identity, axis=1, keepdims=True)
    level = jnp.max(diagonal[:NEIG], axis=0, keepdims=True)
    signed = level * identity - reduced
    square = stacked_dot(signed, signed)
    total = jnp.sum(jnp.sum(signed * signed, axis=1, keepdims=True), axis=0, keepdims=True)
    square = square / total
    signed = signed / jnp.sqrt(total)
    for step in range(SIGN_STEPS):
        if step > 0:
            square = stacked_dot(signed, signed)
        signed = stacked_dot(signed, 1.5 * identity - 0.5 * square)
    projector = 0.5 * (identity + signed)
    wanted = jnp.where(column < NEIG, projector, 0.0) * math.sqrt(ORDER)
    applied = lax.dot_general(
        wanted, jnp.concatenate([rotated, rotated_rest], axis=1), (((0,), (0,)), ((), ())), precision=HIGHEST, preferred_element_type=F32
    )
    current_ref[...] = applied[:NEIG, :ROWS]
    previous_ref[...] = applied[:NEIG, LANES : LANES + ROWS]


def kernel_call(body, outs, args, flops, name, scratch=(), in_hbm=(), out_hbm=(), limit=LIMIT):
    return pl.pallas_call(
        body,
        out_shape=[jax.ShapeDtypeStruct(shape, kind) for shape, kind in outs],
        in_specs=[HBM if n in in_hbm else VMEM for n in range(len(args))],
        out_specs=[HBM if n in out_hbm else VMEM for n in range(len(outs))],
        scratch_shapes=scratch,
        compiler_params=pltpu.CompilerParams(vmem_limit_bytes=limit),
        cost_estimate=pl.CostEstimate(flops=flops, bytes_accessed=4 << 20, transcendentals=0),
        name=name,
    )(*args)


def to_chips(x, number):
    groups = [[2 * chip + core for chip in ORDERS[number]] for core in range(2)]
    return lax.all_to_all(x, AXIS, 0, 0, axis_index_groups=groups, tiled=True)


def to_core(x):
    return lax.ppermute(x, AXIS, [(device, device ^ 1) for device in range(DEVICES)])


def diagonal_tile(hamiltonian):
    device = lax.axis_index(AXIS)
    own_block = lax.dynamic_slice_in_dim(hamiltonian, device * ROWS, ROWS, 1)
    index = jnp.arange(ROWS)
    diag = jnp.sum(jnp.where(index[:, None] == index[None, :], own_block, 0.0), axis=0)
    rows = jnp.where(index[None, :] % NEIG == jnp.arange(NEIG)[:, None], diag[None, :], 0.0)
    lanes = (jnp.arange(LANES)[None, :] == SPARE + index[:, None] // NEIG).astype(F32)
    return dot_exact(rows, lanes)


def body(hamiltonian, current, previous):
    both = jnp.concatenate([current.T, previous.T], axis=0)
    v_own = to_chips(jnp.broadcast_to(both[None], (CHIPS, 2 * NEIG, ROWS)), 0)
    tile = diagonal_tile(hamiltonian)
    cvec = jnp.pad(current.T, ((0, 0), (0, LANES - ROWS)))
    pvec = jnp.pad(previous.T, ((0, 0), (0, LANES - ROWS)))
    h_parts = prepare(hamiltonian)
    v_own, h_parts, tile = lax.optimization_barrier((v_own, h_parts, tile))
    v_other = to_core(v_own)
    block, half, parts = ((NEIG, LANES), F32), ((STACK, HALF), BF16), ((2, STACK, HALF), BF16)
    half_vmem, parts_vmem = pltpu.VMEM(*half), pltpu.VMEM(*parts)
    h_vmem = pltpu.VMEM((2, PARTS * TALL, HALF), BF16)
    h_half = pltpu.VMEM((PARTS * TALL, HALF), BF16)
    dma = pltpu.SemaphoreType.DMA
    product, h_next = kernel_call(
        image_own_kernel,
        [((PARTS * TALL, 2 * STACK), F32), ((PARTS * TALL, HALF), BF16)],
        (h_parts, v_own),
        1 << 30,
        "image_own",
        [h_half, pltpu.VMEM((2 * STACK, HALF), BF16), dma((2,))], (0,), limit=LIMIT_IMAGE,
    )
    image, sent = kernel_call(
        image_other_kernel, [block, ((CHIPS, NEIG, LANES), F32)], (h_next, v_other, product, tile), 1 << 30, "image_other",
        [half_vmem], limit=LIMIT_IMAGE,
    )
    i_own = to_chips(sent, 1)
    p_image, c_parts, p_parts, first = kernel_call(
        previous_kernel,
        [block, parts, parts, ((2 * NEIG, 2 * NEIG), F32)],
        (h_parts, v_own, v_other, product),
        6 << 30,
        "previous",
        [h_half, parts_vmem, parts_vmem, dma((3,))], (0,), (1, 2),
    )
    i_own, p_image, c_parts = lax.optimization_barrier((i_own, p_image, c_parts))
    i_other = to_core(i_own)
    i_own_parts, half_cross, diag = kernel_call(
        own_kernel,
        [half, ((STACK, STACK), F32), ((CHIPS, LANES), F32)],
        (i_own, c_parts),
        1 << 30,
        "own",
        [half_vmem, dma(())], (1,), limit=LIMIT_OWN,
    )
    search, rms, cross, sent, kept = kernel_call(
        search_kernel,
        [block, ((NEIG,), F32), ((NEIG, NEIG), F32), ((CHIPS, 8, LANES), F32), ((4, STACK, HALF), BF16)],
        (h_parts, i_own, i_other, c_parts, i_own_parts, half_cross, diag, cvec, pvec, p_image, image, tile),
        6 << 30,
        "search",
        [h_vmem, parts_vmem, half_vmem, parts_vmem, pltpu.VMEM((2, NEIG, HALF), F32), pltpu.VMEM((CHIPS, LANES), F32), dma((3,)), dma((2,)), dma(())],
        (0, 3), (4,), limit=LIMIT_SEARCH,
    )
    r_own = to_chips(sent, 2)
    square = ((3 * NEIG, 3 * NEIG), F32)
    inverse, stiff = kernel_call(
        factor_kernel, [square, square], (kept, c_parts, p_parts, first, cross), 6 << 30, "factor",
        [pltpu.VMEM((2, 4 * STACK, HALF), BF16), dma((2, 4))], (0, 1, 2),
    )
    r_own, inverse = lax.optimization_barrier((r_own, inverse))
    r_other = to_core(r_own)
    new_current, new_previous = kernel_call(
        finish_kernel,
        [((NEIG, ROWS), F32)] * 2,
        (inverse, stiff, r_own, r_other, cvec, search, pvec),
        1 << 28,
        "finish",
        limit=8 << 20,
    )
    return new_current.T, new_previous.T, rms


def solution(mesh):
    line = Mesh(mesh.devices.reshape(DEVICES), (AXIS,))
    return jax.shard_map(
        body,
        mesh=line,
        in_specs=(P(AXIS, None), P(AXIS, None), P(AXIS, None)),
        out_specs=(P(AXIS, None), P(AXIS, None), P()),
        check_vma=False,
    )
```

```python
import math

import jax
import jax.numpy as jnp
from jax import lax
from jax.experimental import pallas as pl
from jax.experimental.pallas import tpu as pltpu
from jax.sharding import Mesh
from jax.sharding import PartitionSpec as P

NEIG = 16
SIGN_STEPS = 6
ORDER = 13824
DEVICES = 128
ROWS = ORDER // DEVICES
CHIPS = DEVICES // 2
LANES = 128
FORWARD = list(range(CHIPS))
BACKWARD = FORWARD[::-1]
ORDERS = (BACKWARD, BACKWARD, BACKWARD)
SLOTS = [[order.index(chip) for chip in range(CHIPS)] for order in ORDERS]
HALF = CHIPS * ROWS
TALL = 112
CHUNKS = 2
CHUNK = HALF // CHUNKS
EPS = 1e-06
AXIS = "device"

F32, BF16 = jnp.float32, jnp.bfloat16
HIGHEST = lax.Precision.HIGHEST
VMEM = pl.BlockSpec(memory_space=pltpu.VMEM)
HBM = pl.BlockSpec(memory_space=pltpu.HBM)
LIMIT = 53 << 20
LIMIT_IMAGE = 48 << 20
LIMIT_SEARCH = 54525952
LIMIT_OWN = 54001664
PARTS = 2
STACK = PARTS * NEIG
SPARE = ROWS


def split(x):
    high = x.astype(BF16)
    return high, (x - high.astype(F32)).astype(BF16)


def split3(x):
    high = x.astype(BF16)
    rest = x - high.astype(F32)
    mid = rest.astype(BF16)
    return high, mid, (rest - mid.astype(F32)).astype(BF16)


def nt(left, right):
    return lax.dot_general(left, right, (((1,), (1,)), ((), ())), preferred_element_type=F32)


def nt_exact(left, right):
    return lax.dot_general(left, right, (((1,), (1,)), ((), ())), precision=HIGHEST, preferred_element_type=F32)


def dot_exact(left, right):
    return jnp.dot(left, right, precision=HIGHEST, preferred_element_type=F32)


def fold(parts):
    rows = parts[16:32] + parts[0:16]
    return rows[:, 16:32] + rows[:, 0:16]


def fold_rows(product):
    rows = product[TALL:] + product[:TALL]
    wide = jnp.concatenate([rows, jnp.zeros((TALL, LANES - STACK), F32)], axis=1)
    turned = jnp.concatenate([wide, jnp.zeros((LANES - TALL, LANES), F32)], axis=0).T
    return real_lanes(turned[16:32] + turned[0:16])


def real_lanes(tile):
    lane = lax.broadcasted_iota(jnp.int32, tile.shape, 1)
    return jnp.where(lane < ROWS, tile, 0.0)


def prepare_kernel(h_ref, parts_ref):
    core = lax.rem(lax.axis_index(AXIS), 2)
    for owner in range(2):
        half = jnp.where(core == owner, 0, 1)
        starts = [ROWS * (2 * chip + owner) for chip in range(CHIPS // CHUNKS)]
        x = jnp.concatenate([h_ref[:, start : start + ROWS] for start in starts], axis=1)
        for number, part in enumerate(split(x)):
            parts_ref[half, TALL * number : TALL * number + ROWS, :] = part


def prepare(hamiltonian):
    return pl.pallas_call(
        prepare_kernel,
        grid=(CHUNKS,),
        out_shape=jax.ShapeDtypeStruct((2, PARTS * TALL, HALF), BF16),
        in_specs=[pl.BlockSpec((ROWS, ORDER // CHUNKS), lambda i: (0, i))],
        out_specs=pl.BlockSpec((2, PARTS * TALL, CHUNK), lambda i: (0, 0, i)),
        compiler_params=pltpu.CompilerParams(vmem_limit_bytes=58 << 20),
        cost_estimate=pl.CostEstimate(flops=20 * ROWS * ORDER, bytes_accessed=10 * ROWS * ORDER, transcendentals=0),
        name="prepare",
    )(hamiltonian)


def started(source, target, sem):
    copy = pltpu.make_async_copy(source, target, sem)
    copy.start()
    return copy


def packed(tile_of):
    return jnp.concatenate([tile_of(chip)[:, :ROWS] for chip in range(CHIPS)], axis=1)


def store_parts(x, parts_ref):
    for number, part in enumerate(split(x)):
        parts_ref[NEIG * number : NEIG * (number + 1), :] = part


def take_parts(tile_of, parts_ref):
    store_parts(packed(tile_of), parts_ref)


def take_both(tile_of, first_ref, second_ref):
    x = packed(tile_of)
    store_parts(x[:NEIG], first_ref)
    store_parts(x[NEIG:], second_ref)


def stacked_dot(left, right):
    high, low = split(left)
    right_high, right_low = split(right)
    both = jnp.dot(jnp.concatenate([high, low], axis=0), right_high, preferred_element_type=F32)
    size = left.shape[0]
    return both[:size] + (both[size:] + jnp.dot(high, right_low, preferred_element_type=F32))


def eliminated(matrix):
    size = matrix.shape[0]
    row = lax.broadcasted_iota(jnp.int32, (size, size), 0)
    column = lax.broadcasted_iota(jnp.int32, (size, size), 1)
    identity = jnp.where(row == column, 1.0, 0.0).astype(F32)
    work = jnp.concatenate([matrix, identity], axis=1)
    below = lax.broadcasted_iota(jnp.int32, (size, 1), 0)
    for k in range(size):
        factor = jnp.where(below > k, work[:, k : k + 1] / work[k : k + 1, k : k + 1], 0.0)
        work = work - factor * work[k : k + 1, :]
    pivots = jnp.sum(work[:, :size] * identity, axis=1, keepdims=True)
    return work[:, size:] / jnp.sqrt(pivots)


def joined(blocks):
    return jnp.concatenate([jnp.concatenate(row, axis=1) for row in blocks], axis=0)


def image_own_kernel(h_ref, own_ref, product_ref, next_ref, h_vmem, parts, sems):
    copy = started(h_ref.at[0], h_vmem, sems.at[0])
    following = started(h_ref.at[1], next_ref, sems.at[1])
    take_both(lambda chip: own_ref[SLOTS[0][chip]], parts.at[pl.ds(0, STACK)], parts.at[pl.ds(STACK, STACK)])
    copy.wait()
    product_ref[...] = nt(h_vmem[...], parts[...])
    following.wait()


def image_other_kernel(h_ref, other_ref, product_ref, tile_ref, image_ref, sent_ref, parts):
    take_parts(lambda chip: other_ref[SLOTS[0][chip], 0:NEIG], parts)
    image = fold_rows(product_ref[:, 0:STACK] + nt(h_ref[...], parts[...]))
    image_ref[...] = image
    sent = image + tile_ref[...]
    for chip in range(CHIPS):
        sent_ref[chip] = sent


def previous_kernel(h_ref, own_ref, other_ref, product_ref, image_ref, c_out, p_out, inverse_ref, h_vmem, c_ref, p_ref, sems):
    copy = started(h_ref.at[1], h_vmem, sems.at[0])
    take_both(lambda chip: own_ref[SLOTS[0][chip]], c_ref.at[0], p_ref.at[0])
    take_both(lambda chip: other_ref[SLOTS[0][chip]], c_ref.at[1], p_ref.at[1])
    out_c = started(c_ref, c_out.at[pl.ds(0, 2)], sems.at[1])
    out_p = started(p_ref, p_out.at[pl.ds(0, 2)], sems.at[2])
    cc = fold(nt(c_ref[0], c_ref[0]) + nt(c_ref[1], c_ref[1]))
    pc = fold(nt(p_ref[0], c_ref[0]) + nt(p_ref[1], c_ref[1]))
    pp = fold(nt(p_ref[0], p_ref[0]) + nt(p_ref[1], p_ref[1]))
    empty = jnp.zeros((NEIG, NEIG), F32)
    low = joined([[0.5 * cc, empty], [pc, 0.5 * pp]])
    copy.wait()
    image_ref[...] = fold_rows(product_ref[:, STACK:] + nt(h_vmem[...], p_ref[1]))
    inverse_ref[...] = eliminated(low + low.T)
    out_c.wait()
    out_p.wait()


def diagonal_of(tile):
    row = lax.broadcasted_iota(jnp.int32, (NEIG, LANES), 0)
    lane = lax.broadcasted_iota(jnp.int32, (NEIG, LANES), 1)
    spread = jnp.take_along_axis(tile, SPARE + lane // NEIG, axis=1)
    return jnp.sum(jnp.where(lane % NEIG == row, spread, 0.0), axis=0, keepdims=True)


def own_kernel(own_ref, c_hbm, i_ref, x_ref, cross_ref, diag_ref, c_ref, sem):
    copy = started(c_hbm.at[0], c_ref, sem)
    x = packed(lambda chip: own_ref[SLOTS[1][chip]])
    x_ref[...] = x
    store_parts(x, i_ref)
    diag_ref[...] = packed(lambda chip: diagonal_of(own_ref[SLOTS[1][chip]]))
    copy.wait()
    cross_ref[...] = nt(i_ref[...], c_ref[...])


def search_kernel(
    h_ref, x_own_ref, other_ref, c_hbm, i_own_ref, half_cross_ref, diag_ref, cvec_ref, pvec_ref, pimage_ref, image_ref, tile_ref,
    search_ref, rms_ref, cross_ref, sent_ref, kept_ref,
    h_vmem, c_ref, i_ref, s_ref, resid_ref, other_diag_ref, sems, h_sems, c_sem,
):
    copy_c = started(c_hbm.at[pl.ds(0, 2)], c_ref, c_sem)
    copies = [started(h_ref.at[half], h_vmem.at[half], h_sems.at[half]) for half in range(2)]
    x_other = packed(lambda chip: other_ref[SLOTS[1][chip]])
    resid_ref[1] = x_other
    store_parts(x_other, i_ref)
    other_diag_ref[...] = packed(lambda chip: diagonal_of(other_ref[SLOTS[1][chip]]))
    copy_c.wait()
    kept = [started(i_own_ref, kept_ref.at[2], sems.at[1]), started(i_ref, kept_ref.at[3], sems.at[2])]
    cross_t = fold(half_cross_ref[...] + nt(i_ref[...], c_ref[1]))
    cross_ref[...] = cross_t
    ritz_t = cross_t / ORDER
    stacked = jnp.concatenate(split3(ritz_t), axis=0)
    stacked = jnp.concatenate([stacked] * PARTS, axis=1)
    square = jnp.zeros((NEIG, 1), F32)
    for half, ref in ((0, x_own_ref), (1, resid_ref.at[1])):
        moved = jnp.dot(stacked, c_ref[half], preferred_element_type=F32)
        moved = (moved[32:48] + moved[16:32]) + moved[0:16]
        resid = ref[...] - moved
        resid_ref[half] = resid
        square = square + jnp.sum(resid * resid, axis=1, keepdims=True)
    rms = jnp.sqrt(square / ORDER + EPS)
    row = lax.broadcasted_iota(jnp.int32, (NEIG, NEIG), 0)
    column = lax.broadcasted_iota(jnp.int32, (NEIG, NEIG), 1)
    rms_ref[...] = jnp.sum(jnp.where(row == column, rms, 0.0), axis=0)
    value = jnp.sum(jnp.where(row == column, ritz_t, 0.0), axis=1, keepdims=True)

    def scaled(resid, diag):
        return resid / (jnp.maximum(jnp.abs(diag - value), 1.0) * rms)

    resid = image_ref[...] - dot_exact(ritz_t, cvec_ref[...])
    search = scaled(resid, diagonal_of(tile_ref[...]))
    search_ref[...] = search
    for half, diag in ((0, diag_ref), (1, other_diag_ref)):
        store_parts(scaled(resid_ref[half], diag[...]), s_ref.at[half])
    kept.append(started(s_ref, kept_ref.at[pl.ds(0, 2)], sems.at[0]))
    copies[0].wait()
    product = nt(h_vmem[0], s_ref[0])
    copies[1].wait()
    simage = fold_rows(product + nt(h_vmem[1], s_ref[1]))
    pvec = pvec_ref[...]
    terms = jnp.concatenate(
        [nt_exact(simage, search), nt_exact(simage, pvec), nt_exact(pimage_ref[...], pvec), jnp.zeros((NEIG, NEIG), F32)],
        axis=1,
    )
    message = jnp.concatenate([terms[0:8], terms[8:16]], axis=1)
    for chip in range(CHIPS):
        sent_ref[chip] = message
    for copy in kept:
        copy.wait()


def factor_kernel(kept_hbm, c_hbm, p_hbm, first_ref, cross_ref, inverse_ref, stiff_ref, all_ref, sems):
    copies = []
    for half in range(2):
        for number, source in enumerate((kept_hbm.at[half], kept_hbm.at[2 + half], c_hbm.at[half], p_hbm.at[half])):
            copies.append(started(source, all_ref.at[half, pl.ds(STACK * number, STACK)], sems.at[half, number]))
    with_search, p_image = None, None
    for half in range(2):
        for copy in copies[4 * half : 4 * half + 4]:
            copy.wait()
        terms = nt(all_ref[half], all_ref[half, :STACK])
        with_search = terms if half == 0 else with_search + terms
        terms = nt(all_ref[half, 3 * STACK :], all_ref[half, STACK : 2 * STACK])
        p_image = terms if half == 0 else p_image + terms
    ss, i_s, cs, ps = [fold(with_search[STACK * n : STACK * (n + 1)]) for n in range(4)]
    first = first_ref[...]
    row = nt_exact(jnp.concatenate([cs.T, ps.T], axis=1), first)
    last = eliminated(ss - nt_exact(row, row))
    inverse_ref[...] = joined(
        [[first, jnp.zeros((2 * NEIG, NEIG), F32)], [-dot_exact(last, dot_exact(row, first)), last]]
    )
    empty = jnp.zeros((NEIG, NEIG), F32)
    low = joined([[0.5 * cross_ref[...], empty, i_s], [fold(p_image), empty, empty], [empty, empty, empty]])
    stiff_ref[...] = low + low.T


def finish_kernel(inverse_ref, stiff_ref, own_ref, other_ref, c_ref, s_ref, p_ref, current_ref, previous_ref):
    size = 3 * NEIG
    total = own_ref[0] + other_ref[0]
    for chip in range(1, CHIPS):
        total = total + (own_ref[chip] + other_ref[chip])
    terms = jnp.concatenate([total[:, 0 : 3 * NEIG], total[:, 4 * NEIG : 7 * NEIG]], axis=0)
    ss, sp, pp = terms[:, 0:16], terms[:, 16:32], terms[:, 32:48]
    empty = jnp.zeros((NEIG, NEIG), F32)
    low = joined([[empty, empty, empty], [empty, 0.5 * pp, empty], [empty, sp, 0.5 * ss]])
    stiff = stiff_ref[...] + (low + low.T)
    inverse = inverse_ref[...]
    basis = jnp.concatenate([c_ref[...], p_ref[...], s_ref[...]], axis=0)
    rotated = dot_exact(inverse, basis)
    rotated_rest = dot_exact(jnp.where(lax.broadcasted_iota(jnp.int32, (size, size), 1) < NEIG, 0.0, inverse), basis)
    reduced = nt_exact(dot_exact(inverse, stiff), inverse)
    row = lax.broadcasted_iota(jnp.int32, (size, size), 0)
    column = lax.broadcasted_iota(jnp.int32, (size, size), 1)
    identity = jnp.where(row == column, 1.0, 0.0).astype(F32)
    diagonal = jnp.sum(reduced * identity, axis=1, keepdims=True)
    level = jnp.max(diagonal[:NEIG], axis=0, keepdims=True)
    signed = level * identity - reduced
    square = stacked_dot(signed, signed)
    total = jnp.sum(jnp.sum(signed * signed, axis=1, keepdims=True), axis=0, keepdims=True)
    square = square / total
    signed = signed / jnp.sqrt(total)
    for step in range(SIGN_STEPS):
        if step > 0:
            square = stacked_dot(signed, signed)
        signed = stacked_dot(signed, 1.5 * identity - 0.5 * square)
    projector = 0.5 * (identity + signed)
    wanted = jnp.where(column < NEIG, projector, 0.0) * math.sqrt(ORDER)
    applied = lax.dot_general(
        wanted, jnp.concatenate([rotated, rotated_rest], axis=1), (((0,), (0,)), ((), ())), precision=HIGHEST, preferred_element_type=F32
    )
    current_ref[...] = applied[:NEIG, :ROWS]
    previous_ref[...] = applied[:NEIG, LANES : LANES + ROWS]


def kernel_call(body, outs, args, flops, name, scratch=(), in_hbm=(), out_hbm=(), limit=LIMIT):
    return pl.pallas_call(
        body,
        out_shape=[jax.ShapeDtypeStruct(shape, kind) for shape, kind in outs],
        in_specs=[HBM if n in in_hbm else VMEM for n in range(len(args))],
        out_specs=[HBM if n in out_hbm else VMEM for n in range(len(outs))],
        scratch_shapes=scratch,
        compiler_params=pltpu.CompilerParams(vmem_limit_bytes=limit),
        cost_estimate=pl.CostEstimate(flops=flops, bytes_accessed=4 << 20, transcendentals=0),
        name=name,
    )(*args)


def to_chips(x, number):
    groups = [[2 * chip + core for chip in ORDERS[number]] for core in range(2)]
    return lax.all_to_all(x, AXIS, 0, 0, axis_index_groups=groups, tiled=True)


def to_core(x):
    return lax.ppermute(x, AXIS, [(device, device ^ 1) for device in range(DEVICES)])


def diagonal_tile(hamiltonian):
    device = lax.axis_index(AXIS)
    own_block = lax.dynamic_slice_in_dim(hamiltonian, device * ROWS, ROWS, 1)
    index = jnp.arange(ROWS)
    diag = jnp.sum(jnp.where(index[:, None] == index[None, :], own_block, 0.0), axis=0)
    rows = jnp.where(index[None, :] % NEIG == jnp.arange(NEIG)[:, None], diag[None, :], 0.0)
    lanes = (jnp.arange(LANES)[None, :] == SPARE + index[:, None] // NEIG).astype(F32)
    return dot_exact(rows, lanes)


def body(hamiltonian, current, previous):
    both = jnp.concatenate([current.T, previous.T], axis=0)
    v_own = to_chips(jnp.broadcast_to(both[None], (CHIPS, 2 * NEIG, ROWS)), 0)
    tile = diagonal_tile(hamiltonian)
    cvec = jnp.pad(current.T, ((0, 0), (0, LANES - ROWS)))
    pvec = jnp.pad(previous.T, ((0, 0), (0, LANES - ROWS)))
    h_parts = prepare(hamiltonian)
    v_own, h_parts, tile = lax.optimization_barrier((v_own, h_parts, tile))
    v_other = to_core(v_own)
    block, half, parts = ((NEIG, LANES), F32), ((STACK, HALF), BF16), ((2, STACK, HALF), BF16)
    half_vmem, parts_vmem = pltpu.VMEM(*half), pltpu.VMEM(*parts)
    h_vmem = pltpu.VMEM((2, PARTS * TALL, HALF), BF16)
    h_half = pltpu.VMEM((PARTS * TALL, HALF), BF16)
    dma = pltpu.SemaphoreType.DMA
    product, h_next = kernel_call(
        image_own_kernel,
        [((PARTS * TALL, 2 * STACK), F32), ((PARTS * TALL, HALF), BF16)],
        (h_parts, v_own),
        1 << 30,
        "image_own",
        [h_half, pltpu.VMEM((2 * STACK, HALF), BF16), dma((2,))], (0,), limit=LIMIT_IMAGE,
    )
    image, sent = kernel_call(
        image_other_kernel, [block, ((CHIPS, NEIG, LANES), F32)], (h_next, v_other, product, tile), 1 << 30, "image_other",
        [half_vmem], limit=LIMIT_IMAGE,
    )
    i_own = to_chips(sent, 1)
    p_image, c_parts, p_parts, first = kernel_call(
        previous_kernel,
        [block, ((3, STACK, HALF), BF16), ((3, STACK, HALF), BF16), ((2 * NEIG, 2 * NEIG), F32)],
        (h_parts, v_own, v_other, product),
        6 << 30,
        "previous",
        [h_half, parts_vmem, parts_vmem, dma((3,))], (0,), (1, 2),
    )
    i_own, p_image, c_parts = lax.optimization_barrier((i_own, p_image, c_parts))
    i_other = to_core(i_own)
    i_own_parts, x_own, half_cross, diag = kernel_call(
        own_kernel,
        [half, ((NEIG, HALF), F32), ((STACK, STACK), F32), ((1, HALF), F32)],
        (i_own, c_parts),
        1 << 30,
        "own",
        [half_vmem, dma(())], (1,), limit=LIMIT_OWN,
    )
    search, rms, cross, sent, kept = kernel_call(
        search_kernel,
        [block, ((NEIG,), F32), ((NEIG, NEIG), F32), ((CHIPS, 8, LANES), F32), ((4, STACK, HALF), BF16)],
        (h_parts, x_own, i_other, c_parts, i_own_parts, half_cross, diag, cvec, pvec, p_image, image, tile),
        6 << 30,
        "search",
        [h_vmem, parts_vmem, half_vmem, parts_vmem, pltpu.VMEM((2, NEIG, HALF), F32), pltpu.VMEM((1, HALF), F32), dma((3,)), dma((2,)), dma(())],
        (0, 3), (4,), limit=LIMIT_SEARCH,
    )
    r_own = to_chips(sent, 2)
    square = ((3 * NEIG, 3 * NEIG), F32)
    inverse, stiff = kernel_call(
        factor_kernel, [square, square], (kept, c_parts, p_parts, first, cross), 6 << 30, "factor",
        [pltpu.VMEM((2, 4 * STACK, HALF), BF16), dma((2, 4))], (0, 1, 2),
    )
    r_own, inverse = lax.optimization_barrier((r_own, inverse))
    r_other = to_core(r_own)
    new_current, new_previous = kernel_call(
        finish_kernel,
        [((NEIG, ROWS), F32)] * 2,
        (inverse, stiff, r_own, r_other, cvec, search, pvec),
        1 << 28,
        "finish",
        limit=8 << 20,
    )
    return new_current.T, new_previous.T, rms


def solution(mesh):
    line = Mesh(mesh.devices.reshape(DEVICES), (AXIS,))
    return jax.shard_map(
        body,
        mesh=line,
        in_specs=(P(AXIS, None), P(AXIS, None), P(AXIS, None)),
        out_specs=(P(AXIS, None), P(AXIS, None), P()),
        check_vma=False,
    )
```

```python
import math

import jax
import jax.numpy as jnp
from jax import lax
from jax.experimental import pallas as pl
from jax.experimental.pallas import tpu as pltpu
from jax.sharding import Mesh
from jax.sharding import PartitionSpec as P

NEIG = 16
SIGN_STEPS = 6
ORDER = 13824
DEVICES = 128
ROWS = ORDER // DEVICES
CHIPS = DEVICES // 2
LANES = 128
FORWARD = list(range(CHIPS))
BACKWARD = FORWARD[::-1]
ORDERS = (BACKWARD, BACKWARD, BACKWARD)
SLOTS = [[order.index(chip) for chip in range(CHIPS)] for order in ORDERS]
HALF = CHIPS * ROWS
TALL = 112
CHUNKS = 2
CHUNK = HALF // CHUNKS
EPS = 1e-06
AXIS = "device"

F32, BF16 = jnp.float32, jnp.bfloat16
HIGHEST = lax.Precision.HIGHEST
VMEM = pl.BlockSpec(memory_space=pltpu.VMEM)
HBM = pl.BlockSpec(memory_space=pltpu.HBM)
LIMIT = 53 << 20
LIMIT_IMAGE = 48 << 20
LIMIT_SEARCH = 54525952
LIMIT_OWN = 54001664
PARTS = 2
STACK = PARTS * NEIG
SPARE = ROWS


def split(x):
    high = x.astype(BF16)
    return high, (x - high.astype(F32)).astype(BF16)


def split3(x):
    high = x.astype(BF16)
    rest = x - high.astype(F32)
    mid = rest.astype(BF16)
    return high, mid, (rest - mid.astype(F32)).astype(BF16)


def nt(left, right):
    return lax.dot_general(left, right, (((1,), (1,)), ((), ())), preferred_element_type=F32)


def nt_exact(left, right):
    return lax.dot_general(left, right, (((1,), (1,)), ((), ())), precision=HIGHEST, preferred_element_type=F32)


def dot_exact(left, right):
    return jnp.dot(left, right, precision=HIGHEST, preferred_element_type=F32)


def fold(parts):
    rows = parts[16:32] + parts[0:16]
    return rows[:, 16:32] + rows[:, 0:16]


def fold_rows(product):
    rows = product[TALL:] + product[:TALL]
    wide = jnp.concatenate([rows, jnp.zeros((TALL, LANES - STACK), F32)], axis=1)
    turned = jnp.concatenate([wide, jnp.zeros((LANES - TALL, LANES), F32)], axis=0).T
    return real_lanes(turned[16:32] + turned[0:16])


def real_lanes(tile):
    lane = lax.broadcasted_iota(jnp.int32, tile.shape, 1)
    return jnp.where(lane < ROWS, tile, 0.0)


def prepare_kernel(h_ref, parts_ref):
    core = lax.rem(lax.axis_index(AXIS), 2)
    for owner in range(2):
        half = jnp.where(core == owner, 0, 1)
        starts = [ROWS * (2 * chip + owner) for chip in range(CHIPS // CHUNKS)]
        x = jnp.concatenate([h_ref[:, start : start + ROWS] for start in starts], axis=1)
        for number, part in enumerate(split(x)):
            parts_ref[half, TALL * number : TALL * number + ROWS, :] = part


def prepare(hamiltonian):
    return pl.pallas_call(
        prepare_kernel,
        grid=(CHUNKS,),
        out_shape=jax.ShapeDtypeStruct((2, PARTS * TALL, HALF), BF16),
        in_specs=[pl.BlockSpec((ROWS, ORDER // CHUNKS), lambda i: (0, i))],
        out_specs=pl.BlockSpec((2, PARTS * TALL, CHUNK), lambda i: (0, 0, i)),
        compiler_params=pltpu.CompilerParams(vmem_limit_bytes=58 << 20),
        cost_estimate=pl.CostEstimate(flops=20 * ROWS * ORDER, bytes_accessed=10 * ROWS * ORDER, transcendentals=0),
        name="prepare",
    )(hamiltonian)


def started(source, target, sem):
    copy = pltpu.make_async_copy(source, target, sem)
    copy.start()
    return copy


def packed(tile_of):
    return jnp.concatenate([tile_of(chip)[:, :ROWS] for chip in range(CHIPS)], axis=1)


def store_parts(x, parts_ref):
    for number, part in enumerate(split(x)):
        parts_ref[NEIG * number : NEIG * (number + 1), :] = part


def take_parts(tile_of, parts_ref):
    store_parts(packed(tile_of), parts_ref)


def take_both(tile_of, first_ref, second_ref):
    x = packed(tile_of)
    store_parts(x[:NEIG], first_ref)
    store_parts(x[NEIG:], second_ref)


def stacked_dot(left, right):
    high, low = split(left)
    right_high, right_low = split(right)
    both = jnp.dot(jnp.concatenate([high, low], axis=0), right_high, preferred_element_type=F32)
    size = left.shape[0]
    return both[:size] + (both[size:] + jnp.dot(high, right_low, preferred_element_type=F32))


def eliminated(matrix):
    size = matrix.shape[0]
    row = lax.broadcasted_iota(jnp.int32, (size, size), 0)
    column = lax.broadcasted_iota(jnp.int32, (size, size), 1)
    identity = jnp.where(row == column, 1.0, 0.0).astype(F32)
    work = jnp.concatenate([matrix, identity], axis=1)
    below = lax.broadcasted_iota(jnp.int32, (size, 1), 0)
    for k in range(size):
        factor = jnp.where(below > k, work[:, k : k + 1] / work[k : k + 1, k : k + 1], 0.0)
        work = work - factor * work[k : k + 1, :]
    pivots = jnp.sum(work[:, :size] * identity, axis=1, keepdims=True)
    return work[:, size:] / jnp.sqrt(pivots)


def joined(blocks):
    return jnp.concatenate([jnp.concatenate(row, axis=1) for row in blocks], axis=0)


def image_own_kernel(h_ref, own_ref, product_ref, next_ref, h_vmem, parts, sems):
    copy = started(h_ref.at[0], h_vmem, sems.at[0])
    following = started(h_ref.at[1], next_ref, sems.at[1])
    take_both(lambda chip: own_ref[SLOTS[0][chip]], parts.at[pl.ds(0, STACK)], parts.at[pl.ds(STACK, STACK)])
    copy.wait()
    product_ref[...] = nt(h_vmem[...], parts[...])
    following.wait()


def image_other_kernel(h_ref, other_ref, product_ref, tile_ref, image_ref, sent_ref, parts):
    take_parts(lambda chip: other_ref[SLOTS[0][chip], 0:NEIG], parts)
    image = fold_rows(product_ref[:, 0:STACK] + nt(h_ref[...], parts[...]))
    image_ref[...] = image
    sent = image + tile_ref[...]
    for chip in range(CHIPS):
        sent_ref[chip] = sent


def previous_kernel(h_ref, own_ref, other_ref, product_ref, image_ref, c_out, p_out, inverse_ref, h_vmem, c_ref, p_ref, sems):
    copy = started(h_ref.at[1], h_vmem, sems.at[0])
    take_both(lambda chip: own_ref[SLOTS[0][chip]], c_ref.at[0], p_ref.at[0])
    take_both(lambda chip: other_ref[SLOTS[0][chip]], c_ref.at[1], p_ref.at[1])
    out_c = started(c_ref, c_out.at[pl.ds(0, 2)], sems.at[1])
    out_p = started(p_ref, p_out.at[pl.ds(0, 2)], sems.at[2])
    cc = fold(nt(c_ref[0], c_ref[0]) + nt(c_ref[1], c_ref[1]))
    pc = fold(nt(p_ref[0], c_ref[0]) + nt(p_ref[1], c_ref[1]))
    pp = fold(nt(p_ref[0], p_ref[0]) + nt(p_ref[1], p_ref[1]))
    empty = jnp.zeros((NEIG, NEIG), F32)
    low = joined([[0.5 * cc, empty], [pc, 0.5 * pp]])
    copy.wait()
    image_ref[...] = fold_rows(product_ref[:, STACK:] + nt(h_vmem[...], p_ref[1]))
    inverse_ref[...] = eliminated(low + low.T)
    out_c.wait()
    out_p.wait()


def diagonal_of(tile):
    row = lax.broadcasted_iota(jnp.int32, (NEIG, LANES), 0)
    lane = lax.broadcasted_iota(jnp.int32, (NEIG, LANES), 1)
    spread = jnp.take_along_axis(tile, SPARE + lane // NEIG, axis=1)
    return jnp.sum(jnp.where(lane % NEIG == row, spread, 0.0), axis=0, keepdims=True)


def own_kernel(own_ref, c_hbm, i_ref, x_ref, cross_ref, diag_ref, c_ref, sem):
    copy = started(c_hbm.at[0], c_ref, sem)
    x = packed(lambda chip: own_ref[SLOTS[1][chip]])
    x_ref[...] = x
    store_parts(x, i_ref)
    diag_ref[...] = packed(lambda chip: diagonal_of(own_ref[SLOTS[1][chip]]))
    copy.wait()
    cross_ref[...] = nt(i_ref[...], c_ref[...])


def search_kernel(
    h_ref, x_own_ref, other_ref, c_hbm, i_own_ref, half_cross_ref, diag_ref, cvec_ref, pvec_ref, pimage_ref, image_ref, tile_ref,
    search_ref, rms_ref, cross_ref, sent_ref, kept_ref,
    h_vmem, c_ref, i_ref, s_ref, resid_ref, other_diag_ref, sems, h_sems, c_sem,
):
    copy_c = started(c_hbm.at[pl.ds(0, 2)], c_ref, c_sem)
    copies = [started(h_ref.at[half], h_vmem.at[half], h_sems.at[half]) for half in range(2)]
    x_other = packed(lambda chip: other_ref[SLOTS[1][chip]])
    resid_ref[1] = x_other
    store_parts(x_other, i_ref)
    other_diag_ref[...] = packed(lambda chip: diagonal_of(other_ref[SLOTS[1][chip]]))
    copy_c.wait()
    kept = [started(i_own_ref, kept_ref.at[2], sems.at[1]), started(i_ref, kept_ref.at[3], sems.at[2])]
    cross_t = fold(half_cross_ref[...] + nt(i_ref[...], c_ref[1]))
    cross_ref[...] = cross_t
    ritz_t = cross_t / ORDER
    stacked = jnp.concatenate(split3(ritz_t), axis=0)
    stacked = jnp.concatenate([stacked] * PARTS, axis=1)
    square = jnp.zeros((NEIG, 1), F32)
    for half, ref in ((0, x_own_ref), (1, resid_ref.at[1])):
        moved = jnp.dot(stacked, c_ref[half], preferred_element_type=F32)
        moved = (moved[32:48] + moved[16:32]) + moved[0:16]
        resid = ref[...] - moved
        resid_ref[half] = resid
        square = square + jnp.sum(resid * resid, axis=1, keepdims=True)
    rms = jnp.sqrt(square / ORDER + EPS)
    row = lax.broadcasted_iota(jnp.int32, (NEIG, NEIG), 0)
    column = lax.broadcasted_iota(jnp.int32, (NEIG, NEIG), 1)
    rms_ref[...] = jnp.sum(jnp.where(row == column, rms, 0.0), axis=0)
    value = jnp.sum(jnp.where(row == column, ritz_t, 0.0), axis=1, keepdims=True)

    def scaled(resid, diag):
        return resid / (jnp.maximum(jnp.abs(diag - value), 1.0) * rms)

    resid = image_ref[...] - dot_exact(ritz_t, cvec_ref[...])
    search = scaled(resid, diagonal_of(tile_ref[...]))
    search_ref[...] = search
    for half, diag in ((0, diag_ref), (1, other_diag_ref)):
        store_parts(scaled(resid_ref[half], diag[...]), s_ref.at[half])
    kept.append(started(s_ref, kept_ref.at[pl.ds(0, 2)], sems.at[0]))
    copies[0].wait()
    product = nt(h_vmem[0], s_ref[0])
    copies[1].wait()
    simage = fold_rows(product + nt(h_vmem[1], s_ref[1]))
    pvec = pvec_ref[...]
    terms = jnp.concatenate(
        [
            nt_exact(simage, jnp.concatenate([search, pvec], axis=0)),
            nt_exact(pimage_ref[...], pvec),
            jnp.zeros((NEIG, NEIG), F32),
        ],
        axis=1,
    )
    message = jnp.concatenate([terms[0:8], terms[8:16]], axis=1)
    for chip in range(CHIPS):
        sent_ref[chip] = message
    for copy in kept:
        copy.wait()


def factor_kernel(kept_hbm, c_hbm, p_hbm, first_ref, cross_ref, inverse_ref, stiff_ref, all_ref, sems):
    copies = []
    for half in range(2):
        for number, source in enumerate((kept_hbm.at[half], kept_hbm.at[2 + half], c_hbm.at[half], p_hbm.at[half])):
            copies.append(started(source, all_ref.at[half, pl.ds(STACK * number, STACK)], sems.at[half, number]))
    products = None
    for half in range(2):
        for copy in copies[4 * half : 4 * half + 4]:
            copy.wait()
        terms = nt(all_ref[half], all_ref[half, : 2 * STACK])
        products = terms if half == 0 else products + terms
    with_search, p_image = products[:, :STACK], products[3 * STACK :, STACK:]
    ss, i_s, cs, ps = [fold(with_search[STACK * n : STACK * (n + 1)]) for n in range(4)]
    first = first_ref[...]
    row = nt_exact(jnp.concatenate([cs.T, ps.T], axis=1), first)
    last = eliminated(ss - nt_exact(row, row))
    inverse_ref[...] = joined(
        [[first, jnp.zeros((2 * NEIG, NEIG), F32)], [-dot_exact(last, dot_exact(row, first)), last]]
    )
    empty = jnp.zeros((NEIG, NEIG), F32)
    low = joined([[0.5 * cross_ref[...], empty, i_s], [fold(p_image), empty, empty], [empty, empty, empty]])
    stiff_ref[...] = low + low.T


def finish_kernel(inverse_ref, stiff_ref, own_ref, other_ref, c_ref, s_ref, p_ref, current_ref, previous_ref):
    size = 3 * NEIG
    total = own_ref[0] + other_ref[0]
    for chip in range(1, CHIPS):
        total = total + (own_ref[chip] + other_ref[chip])
    terms = jnp.concatenate([total[:, 0 : 3 * NEIG], total[:, 4 * NEIG : 7 * NEIG]], axis=0)
    ss, sp, pp = terms[:, 0:16], terms[:, 16:32], terms[:, 32:48]
    empty = jnp.zeros((NEIG, NEIG), F32)
    low = joined([[empty, empty, empty], [empty, 0.5 * pp, empty], [empty, sp, 0.5 * ss]])
    stiff = stiff_ref[...] + (low + low.T)
    inverse = inverse_ref[...]
    basis = jnp.concatenate([c_ref[...], p_ref[...], s_ref[...]], axis=0)
    rotated = dot_exact(inverse, basis)
    rotated_rest = dot_exact(jnp.where(lax.broadcasted_iota(jnp.int32, (size, size), 1) < NEIG, 0.0, inverse), basis)
    reduced = nt_exact(dot_exact(inverse, stiff), inverse)
    row = lax.broadcasted_iota(jnp.int32, (size, size), 0)
    column = lax.broadcasted_iota(jnp.int32, (size, size), 1)
    identity = jnp.where(row == column, 1.0, 0.0).astype(F32)
    diagonal = jnp.sum(reduced * identity, axis=1, keepdims=True)
    level = jnp.max(diagonal[:NEIG], axis=0, keepdims=True)
    signed = level * identity - reduced
    square = stacked_dot(signed, signed)
    total = jnp.sum(jnp.sum(signed * signed, axis=1, keepdims=True), axis=0, keepdims=True)
    square = square / total
    signed = signed / jnp.sqrt(total)
    for step in range(SIGN_STEPS):
        if step > 0:
            square = stacked_dot(signed, signed)
        signed = stacked_dot(signed, 1.5 * identity - 0.5 * square)
    projector = 0.5 * (identity + signed)
    wanted = jnp.where(column < NEIG, projector, 0.0) * math.sqrt(ORDER)
    applied = lax.dot_general(
        wanted, jnp.concatenate([rotated, rotated_rest], axis=1), (((0,), (0,)), ((), ())), precision=HIGHEST, preferred_element_type=F32
    )
    current_ref[...] = applied[:NEIG, :ROWS]
    previous_ref[...] = applied[:NEIG, LANES : LANES + ROWS]


def kernel_call(body, outs, args, flops, name, scratch=(), in_hbm=(), out_hbm=(), limit=LIMIT):
    return pl.pallas_call(
        body,
        out_shape=[jax.ShapeDtypeStruct(shape, kind) for shape, kind in outs],
        in_specs=[HBM if n in in_hbm else VMEM for n in range(len(args))],
        out_specs=[HBM if n in out_hbm else VMEM for n in range(len(outs))],
        scratch_shapes=scratch,
        compiler_params=pltpu.CompilerParams(vmem_limit_bytes=limit),
        cost_estimate=pl.CostEstimate(flops=flops, bytes_accessed=4 << 20, transcendentals=0),
        name=name,
    )(*args)


def to_chips(x, number):
    groups = [[2 * chip + core for chip in ORDERS[number]] for core in range(2)]
    return lax.all_to_all(x, AXIS, 0, 0, axis_index_groups=groups, tiled=True)


def to_core(x):
    return lax.ppermute(x, AXIS, [(device, device ^ 1) for device in range(DEVICES)])


def diagonal_tile(hamiltonian):
    device = lax.axis_index(AXIS)
    own_block = lax.dynamic_slice_in_dim(hamiltonian, device * ROWS, ROWS, 1)
    index = jnp.arange(ROWS)
    diag = jnp.sum(jnp.where(index[:, None] == index[None, :], own_block, 0.0), axis=0)
    rows = jnp.where(index[None, :] % NEIG == jnp.arange(NEIG)[:, None], diag[None, :], 0.0)
    lanes = (jnp.arange(LANES)[None, :] == SPARE + index[:, None] // NEIG).astype(F32)
    return dot_exact(rows, lanes)


def body(hamiltonian, current, previous):
    both = jnp.concatenate([current.T, previous.T], axis=0)
    v_own = to_chips(jnp.broadcast_to(both[None], (CHIPS, 2 * NEIG, ROWS)), 0)
    tile = diagonal_tile(hamiltonian)
    cvec = jnp.pad(current.T, ((0, 0), (0, LANES - ROWS)))
    pvec = jnp.pad(previous.T, ((0, 0), (0, LANES - ROWS)))
    h_parts = prepare(hamiltonian)
    v_own, h_parts, tile = lax.optimization_barrier((v_own, h_parts, tile))
    v_other = to_core(v_own)
    block, half, parts = ((NEIG, LANES), F32), ((STACK, HALF), BF16), ((2, STACK, HALF), BF16)
    half_vmem, parts_vmem = pltpu.VMEM(*half), pltpu.VMEM(*parts)
    h_vmem = pltpu.VMEM((2, PARTS * TALL, HALF), BF16)
    h_half = pltpu.VMEM((PARTS * TALL, HALF), BF16)
    dma = pltpu.SemaphoreType.DMA
    product, h_next = kernel_call(
        image_own_kernel,
        [((PARTS * TALL, 2 * STACK), F32), ((PARTS * TALL, HALF), BF16)],
        (h_parts, v_own),
        1 << 30,
        "image_own",
        [h_half, pltpu.VMEM((2 * STACK, HALF), BF16), dma((2,))], (0,), limit=LIMIT_IMAGE,
    )
    image, sent = kernel_call(
        image_other_kernel, [block, ((CHIPS, NEIG, LANES), F32)], (h_next, v_other, product, tile), 1 << 30, "image_other",
        [half_vmem], limit=LIMIT_IMAGE,
    )
    i_own = to_chips(sent, 1)
    p_image, c_parts, p_parts, first = kernel_call(
        previous_kernel,
        [block, ((3, STACK, HALF), BF16), ((3, STACK, HALF), BF16), ((2 * NEIG, 2 * NEIG), F32)],
        (h_parts, v_own, v_other, product),
        6 << 30,
        "previous",
        [h_half, parts_vmem, parts_vmem, dma((3,))], (0,), (1, 2),
    )
    i_own, p_image, c_parts = lax.optimization_barrier((i_own, p_image, c_parts))
    i_other = to_core(i_own)
    i_own_parts, x_own, half_cross, diag = kernel_call(
        own_kernel,
        [half, ((NEIG, HALF), F32), ((STACK, STACK), F32), ((1, HALF), F32)],
        (i_own, c_parts),
        1 << 30,
        "own",
        [half_vmem, dma(())], (1,), limit=LIMIT_OWN,
    )
    search, rms, cross, sent, kept = kernel_call(
        search_kernel,
        [block, ((NEIG,), F32), ((NEIG, NEIG), F32), ((CHIPS, 8, LANES), F32), ((4, STACK, HALF), BF16)],
        (h_parts, x_own, i_other, c_parts, i_own_parts, half_cross, diag, cvec, pvec, p_image, image, tile),
        6 << 30,
        "search",
        [h_vmem, parts_vmem, half_vmem, parts_vmem, pltpu.VMEM((2, NEIG, HALF), F32), pltpu.VMEM((1, HALF), F32), dma((3,)), dma((2,)), dma(())],
        (0, 3), (4,), limit=LIMIT_SEARCH,
    )
    r_own = to_chips(sent, 2)
    square = ((3 * NEIG, 3 * NEIG), F32)
    inverse, stiff = kernel_call(
        factor_kernel, [square, square], (kept, c_parts, p_parts, first, cross), 6 << 30, "factor",
        [pltpu.VMEM((2, 4 * STACK, HALF), BF16), dma((2, 4))], (0, 1, 2),
    )
    r_own, inverse = lax.optimization_barrier((r_own, inverse))
    r_other = to_core(r_own)
    new_current, new_previous = kernel_call(
        finish_kernel,
        [((NEIG, ROWS), F32)] * 2,
        (inverse, stiff, r_own, r_other, cvec, search, pvec),
        1 << 28,
        "finish",
        limit=8 << 20,
    )
    return new_current.T, new_previous.T, rms


def solution(mesh):
    line = Mesh(mesh.devices.reshape(DEVICES), (AXIS,))
    return jax.shard_map(
        body,
        mesh=line,
        in_specs=(P(AXIS, None), P(AXIS, None), P(AXIS, None)),
        out_specs=(P(AXIS, None), P(AXIS, None), P()),
        check_vma=False,
    )
```

```python
import math

import jax
import jax.numpy as jnp
from jax import lax
from jax.experimental import pallas as pl
from jax.experimental.pallas import tpu as pltpu
from jax.sharding import Mesh
from jax.sharding import PartitionSpec as P

NEIG = 16
SIGN_STEPS = 6
ORDER = 13824
DEVICES = 128
ROWS = ORDER // DEVICES
CHIPS = DEVICES // 2
LANES = 128
FORWARD = list(range(CHIPS))
BACKWARD = FORWARD[::-1]
ORDERS = (BACKWARD, BACKWARD, BACKWARD)
SLOTS = [[order.index(chip) for chip in range(CHIPS)] for order in ORDERS]
HALF = CHIPS * ROWS
TALL = 112
CHUNKS = 2
CHUNK = HALF // CHUNKS
EPS = 1e-06
AXIS = "device"

F32, BF16 = jnp.float32, jnp.bfloat16
HIGHEST = lax.Precision.HIGHEST
VMEM = pl.BlockSpec(memory_space=pltpu.VMEM)
HBM = pl.BlockSpec(memory_space=pltpu.HBM)
LIMIT = 53 << 20
LIMIT_IMAGE = 48 << 20
LIMIT_SEARCH = 54525952
LIMIT_OWN = 54001664
PARTS = 2
STACK = PARTS * NEIG
SPARE = ROWS


def split(x):
    high = x.astype(BF16)
    return high, (x - high.astype(F32)).astype(BF16)


def nt(left, right):
    return lax.dot_general(left, right, (((1,), (1,)), ((), ())), preferred_element_type=F32)


def nt_exact(left, right):
    return lax.dot_general(left, right, (((1,), (1,)), ((), ())), precision=HIGHEST, preferred_element_type=F32)


def dot_exact(left, right):
    return jnp.dot(left, right, precision=HIGHEST, preferred_element_type=F32)


def fold(parts):
    rows = parts[16:32] + parts[0:16]
    return rows[:, 16:32] + rows[:, 0:16]


def fold_rows(product):
    rows = product[TALL:] + product[:TALL]
    wide = jnp.concatenate([rows, jnp.zeros((TALL, LANES - STACK), F32)], axis=1)
    turned = jnp.concatenate([wide, jnp.zeros((LANES - TALL, LANES), F32)], axis=0).T
    return real_lanes(turned[16:32] + turned[0:16])


def real_lanes(tile):
    lane = lax.broadcasted_iota(jnp.int32, tile.shape, 1)
    return jnp.where(lane < ROWS, tile, 0.0)


def prepare_kernel(h_ref, parts_ref):
    core = lax.rem(lax.axis_index(AXIS), 2)
    for owner in range(2):
        half = jnp.where(core == owner, 0, 1)
        starts = [ROWS * (2 * chip + owner) for chip in range(CHIPS // CHUNKS)]
        x = jnp.concatenate([h_ref[:, start : start + ROWS] for start in starts], axis=1)
        for number, part in enumerate(split(x)):
            parts_ref[half, TALL * number : TALL * number + ROWS, :] = part


def prepare(hamiltonian):
    return pl.pallas_call(
        prepare_kernel,
        grid=(CHUNKS,),
        out_shape=jax.ShapeDtypeStruct((2, PARTS * TALL, HALF), BF16),
        in_specs=[pl.BlockSpec((ROWS, ORDER // CHUNKS), lambda i: (0, i))],
        out_specs=pl.BlockSpec((2, PARTS * TALL, CHUNK), lambda i: (0, 0, i)),
        compiler_params=pltpu.CompilerParams(vmem_limit_bytes=58 << 20),
        cost_estimate=pl.CostEstimate(flops=20 * ROWS * ORDER, bytes_accessed=10 * ROWS * ORDER, transcendentals=0),
        name="prepare",
    )(hamiltonian)


def started(source, target, sem):
    copy = pltpu.make_async_copy(source, target, sem)
    copy.start()
    return copy


def packed(tile_of):
    return jnp.concatenate([tile_of(chip)[:, :ROWS] for chip in range(CHIPS)], axis=1)


def store_parts(x, parts_ref):
    for number, part in enumerate(split(x)):
        parts_ref[NEIG * number : NEIG * (number + 1), :] = part


def take_parts(tile_of, parts_ref):
    store_parts(packed(tile_of), parts_ref)


def take_both(tile_of, first_ref, second_ref):
    x = packed(tile_of)
    store_parts(x[:NEIG], first_ref)
    store_parts(x[NEIG:], second_ref)


def stacked_dot(left, right):
    high, low = split(left)
    right_high, right_low = split(right)
    both = jnp.dot(jnp.concatenate([high, low], axis=0), right_high, preferred_element_type=F32)
    size = left.shape[0]
    return both[:size] + (both[size:] + jnp.dot(high, right_low, preferred_element_type=F32))


def eliminated(matrix):
    size = matrix.shape[0]
    row = lax.broadcasted_iota(jnp.int32, (size, size), 0)
    column = lax.broadcasted_iota(jnp.int32, (size, size), 1)
    identity = jnp.where(row == column, 1.0, 0.0).astype(F32)
    work = jnp.concatenate([matrix, identity], axis=1)
    below = lax.broadcasted_iota(jnp.int32, (size, 1), 0)
    for k in range(size):
        factor = jnp.where(below > k, work[:, k : k + 1] / work[k : k + 1, k : k + 1], 0.0)
        work = work - factor * work[k : k + 1, :]
    pivots = jnp.sum(work[:, :size] * identity, axis=1, keepdims=True)
    return work[:, size:] / jnp.sqrt(pivots)


def joined(blocks):
    return jnp.concatenate([jnp.concatenate(row, axis=1) for row in blocks], axis=0)


def image_own_kernel(h_ref, own_ref, product_ref, next_ref, h_vmem, parts, sems):
    copy = started(h_ref.at[0], h_vmem, sems.at[0])
    following = started(h_ref.at[1], next_ref, sems.at[1])
    take_both(lambda chip: own_ref[SLOTS[0][chip]], parts.at[pl.ds(0, STACK)], parts.at[pl.ds(STACK, STACK)])
    copy.wait()
    product_ref[...] = nt(h_vmem[...], parts[...])
    following.wait()


def image_other_kernel(h_ref, other_ref, product_ref, tile_ref, image_ref, sent_ref, parts):
    take_parts(lambda chip: other_ref[SLOTS[0][chip], 0:NEIG], parts)
    image = fold_rows(product_ref[:, 0:STACK] + nt(h_ref[...], parts[...]))
    image_ref[...] = image
    sent = image + tile_ref[...]
    for chip in range(CHIPS):
        sent_ref[chip] = sent


def previous_kernel(h_ref, own_ref, other_ref, product_ref, image_ref, c_out, p_out, inverse_ref, h_vmem, c_ref, p_ref, sems):
    copy = started(h_ref.at[1], h_vmem, sems.at[0])
    take_both(lambda chip: own_ref[SLOTS[0][chip]], c_ref.at[0], p_ref.at[0])
    take_both(lambda chip: other_ref[SLOTS[0][chip]], c_ref.at[1], p_ref.at[1])
    out_c = started(c_ref, c_out.at[pl.ds(0, 2)], sems.at[1])
    out_p = started(p_ref, p_out.at[pl.ds(0, 2)], sems.at[2])
    cc = fold(nt(c_ref[0], c_ref[0]) + nt(c_ref[1], c_ref[1]))
    pc = fold(nt(p_ref[0], c_ref[0]) + nt(p_ref[1], c_ref[1]))
    pp = fold(nt(p_ref[0], p_ref[0]) + nt(p_ref[1], p_ref[1]))
    empty = jnp.zeros((NEIG, NEIG), F32)
    low = joined([[0.5 * cc, empty], [pc, 0.5 * pp]])
    copy.wait()
    image_ref[...] = fold_rows(product_ref[:, STACK:] + nt(h_vmem[...], p_ref[1]))
    inverse_ref[...] = eliminated(low + low.T)
    out_c.wait()
    out_p.wait()


def diagonal_of(tile):
    row = lax.broadcasted_iota(jnp.int32, (NEIG, LANES), 0)
    lane = lax.broadcasted_iota(jnp.int32, (NEIG, LANES), 1)
    spread = jnp.take_along_axis(tile, SPARE + lane // NEIG, axis=1)
    return jnp.sum(jnp.where(lane % NEIG == row, spread, 0.0), axis=0, keepdims=True)


def own_kernel(own_ref, c_hbm, i_ref, x_ref, cross_ref, diag_ref, c_ref, sem):
    copy = started(c_hbm.at[0], c_ref, sem)
    x = packed(lambda chip: own_ref[SLOTS[1][chip]])
    x_ref[...] = x
    store_parts(x, i_ref)
    diag_ref[...] = packed(lambda chip: diagonal_of(own_ref[SLOTS[1][chip]]))
    copy.wait()
    cross_ref[...] = nt(i_ref[...], c_ref[...])


def search_kernel(
    h_ref, x_own_ref, other_ref, c_hbm, i_own_ref, half_cross_ref, diag_ref, cvec_ref, pvec_ref, pimage_ref, image_ref, tile_ref,
    search_ref, rms_ref, cross_ref, sent_ref, kept_ref,
    h_vmem, c_ref, i_ref, s_ref, resid_ref, other_diag_ref, sems, h_sems, c_sem,
):
    copy_c = started(c_hbm.at[pl.ds(0, 2)], c_ref, c_sem)
    copies = [started(h_ref.at[half], h_vmem.at[half], h_sems.at[half]) for half in range(2)]
    x_other = packed(lambda chip: other_ref[SLOTS[1][chip]])
    resid_ref[1] = x_other
    store_parts(x_other, i_ref)
    other_diag_ref[...] = packed(lambda chip: diagonal_of(other_ref[SLOTS[1][chip]]))
    copy_c.wait()
    kept = [started(i_own_ref, kept_ref.at[2], sems.at[1]), started(i_ref, kept_ref.at[3], sems.at[2])]
    cross_t = fold(half_cross_ref[...] + nt(i_ref[...], c_ref[1]))
    cross_ref[...] = cross_t
    ritz_t = cross_t / ORDER
    stacked = jnp.concatenate(split(ritz_t), axis=0)
    stacked = jnp.concatenate([stacked] * PARTS, axis=1)
    square = jnp.zeros((NEIG, 1), F32)
    for half, ref in ((0, x_own_ref), (1, resid_ref.at[1])):
        moved = jnp.dot(stacked, c_ref[half], preferred_element_type=F32)
        moved = moved[16:32] + moved[0:16]
        resid = ref[...] - moved
        resid_ref[half] = resid
        square = square + jnp.sum(resid * resid, axis=1, keepdims=True)
    rms = jnp.sqrt(square / ORDER + EPS)
    row = lax.broadcasted_iota(jnp.int32, (NEIG, NEIG), 0)
    column = lax.broadcasted_iota(jnp.int32, (NEIG, NEIG), 1)
    rms_ref[...] = jnp.sum(jnp.where(row == column, rms, 0.0), axis=0)
    value = jnp.sum(jnp.where(row == column, ritz_t, 0.0), axis=1, keepdims=True)

    def scaled(resid, diag):
        return resid / (jnp.maximum(jnp.abs(diag - value), 1.0) * rms)

    resid = image_ref[...] - dot_exact(ritz_t, cvec_ref[...])
    search = scaled(resid, diagonal_of(tile_ref[...]))
    search_ref[...] = search
    for half, diag in ((0, diag_ref), (1, other_diag_ref)):
        store_parts(scaled(resid_ref[half], diag[...]), s_ref.at[half])
    copies[0].wait()
    product = nt(h_vmem[0], s_ref[0])
    copies[1].wait()
    kept.append(started(s_ref, kept_ref.at[pl.ds(0, 2)], sems.at[0]))
    simage = fold_rows(product + nt(h_vmem[1], s_ref[1]))
    pvec = pvec_ref[...]
    terms = jnp.concatenate(
        [
            nt_exact(simage, jnp.concatenate([search, pvec], axis=0)),
            nt_exact(pimage_ref[...], pvec),
            jnp.zeros((NEIG, NEIG), F32),
        ],
        axis=1,
    )
    message = jnp.concatenate([terms[0:8], terms[8:16]], axis=1)
    for chip in range(CHIPS):
        sent_ref[chip] = message
    for copy in kept:
        copy.wait()


def factor_kernel(kept_hbm, c_hbm, p_hbm, first_ref, cross_ref, inverse_ref, stiff_ref, all_ref, sems):
    copies = []
    for half in range(2):
        for number, source in enumerate((kept_hbm.at[half], kept_hbm.at[2 + half], c_hbm.at[half], p_hbm.at[half])):
            copies.append(started(source, all_ref.at[half, pl.ds(STACK * number, STACK)], sems.at[half, number]))
    products = None
    for half in range(2):
        for copy in copies[4 * half : 4 * half + 4]:
            copy.wait()
        terms = nt(all_ref[half], all_ref[half, : 2 * STACK])
        products = terms if half == 0 else products + terms
    with_search, p_image = products[:, :STACK], products[3 * STACK :, STACK:]
    ss, i_s, cs, ps = [fold(with_search[STACK * n : STACK * (n + 1)]) for n in range(4)]
    first = first_ref[...]
    row = nt_exact(jnp.concatenate([cs.T, ps.T], axis=1), first)
    last = eliminated(ss - nt_exact(row, row))
    inverse_ref[...] = joined(
        [[first, jnp.zeros((2 * NEIG, NEIG), F32)], [-dot_exact(last, dot_exact(row, first)), last]]
    )
    empty = jnp.zeros((NEIG, NEIG), F32)
    low = joined([[0.5 * cross_ref[...], empty, i_s], [fold(p_image), empty, empty], [empty, empty, empty]])
    stiff_ref[...] = low + low.T


def finish_kernel(inverse_ref, stiff_ref, own_ref, other_ref, c_ref, s_ref, p_ref, current_ref, previous_ref):
    size = 3 * NEIG
    total = own_ref[0] + other_ref[0]
    for chip in range(1, CHIPS):
        total = total + (own_ref[chip] + other_ref[chip])
    terms = jnp.concatenate([total[:, 0 : 3 * NEIG], total[:, 4 * NEIG : 7 * NEIG]], axis=0)
    ss, sp, pp = terms[:, 0:16], terms[:, 16:32], terms[:, 32:48]
    empty = jnp.zeros((NEIG, NEIG), F32)
    low = joined([[empty, empty, empty], [empty, 0.5 * pp, empty], [empty, sp, 0.5 * ss]])
    stiff = stiff_ref[...] + (low + low.T)
    inverse = inverse_ref[...]
    basis = jnp.concatenate([c_ref[...], p_ref[...], s_ref[...]], axis=0)
    rotated = dot_exact(inverse, basis)
    rotated_rest = dot_exact(jnp.where(lax.broadcasted_iota(jnp.int32, (size, size), 1) < NEIG, 0.0, inverse), basis)
    reduced = nt_exact(dot_exact(inverse, stiff), inverse)
    row = lax.broadcasted_iota(jnp.int32, (size, size), 0)
    column = lax.broadcasted_iota(jnp.int32, (size, size), 1)
    identity = jnp.where(row == column, 1.0, 0.0).astype(F32)
    diagonal = jnp.sum(reduced * identity, axis=1, keepdims=True)
    level = jnp.max(diagonal[:NEIG], axis=0, keepdims=True)
    signed = level * identity - reduced
    square = stacked_dot(signed, signed)
    total = jnp.sum(jnp.sum(signed * signed, axis=1, keepdims=True), axis=0, keepdims=True)
    square = square / total
    signed = signed / jnp.sqrt(total)
    for step in range(SIGN_STEPS):
        if step > 0:
            square = stacked_dot(signed, signed)
        signed = stacked_dot(signed, 1.5 * identity - 0.5 * square)
    projector = 0.5 * (identity + signed)
    wanted = jnp.where(column < NEIG, projector, 0.0) * math.sqrt(ORDER)
    applied = lax.dot_general(
        wanted, jnp.concatenate([rotated, rotated_rest], axis=1), (((0,), (0,)), ((), ())), precision=HIGHEST, preferred_element_type=F32
    )
    current_ref[...] = applied[:NEIG, :ROWS]
    previous_ref[...] = applied[:NEIG, LANES : LANES + ROWS]


def kernel_call(body, outs, args, flops, name, scratch=(), in_hbm=(), out_hbm=(), limit=LIMIT):
    return pl.pallas_call(
        body,
        out_shape=[jax.ShapeDtypeStruct(shape, kind) for shape, kind in outs],
        in_specs=[HBM if n in in_hbm else VMEM for n in range(len(args))],
        out_specs=[HBM if n in out_hbm else VMEM for n in range(len(outs))],
        scratch_shapes=scratch,
        compiler_params=pltpu.CompilerParams(vmem_limit_bytes=limit),
        cost_estimate=pl.CostEstimate(flops=flops, bytes_accessed=4 << 20, transcendentals=0),
        name=name,
    )(*args)


def to_chips(x, number):
    groups = [[2 * chip + core for chip in ORDERS[number]] for core in range(2)]
    return lax.all_to_all(x, AXIS, 0, 0, axis_index_groups=groups, tiled=True)


def to_core(x):
    return lax.ppermute(x, AXIS, [(device, device ^ 1) for device in range(DEVICES)])


def diagonal_tile(hamiltonian):
    device = lax.axis_index(AXIS)
    own_block = lax.dynamic_slice_in_dim(hamiltonian, device * ROWS, ROWS, 1)
    index = jnp.arange(ROWS)
    diag = jnp.sum(jnp.where(index[:, None] == index[None, :], own_block, 0.0), axis=0)
    rows = jnp.where(index[None, :] % NEIG == jnp.arange(NEIG)[:, None], diag[None, :], 0.0)
    lanes = (jnp.arange(LANES)[None, :] == SPARE + index[:, None] // NEIG).astype(F32)
    return dot_exact(rows, lanes)


def body(hamiltonian, current, previous):
    both = jnp.concatenate([current.T, previous.T], axis=0)
    v_own = to_chips(jnp.broadcast_to(both[None], (CHIPS, 2 * NEIG, ROWS)), 0)
    tile = diagonal_tile(hamiltonian)
    cvec = jnp.pad(current.T, ((0, 0), (0, LANES - ROWS)))
    pvec = jnp.pad(previous.T, ((0, 0), (0, LANES - ROWS)))
    h_parts = prepare(hamiltonian)
    v_own, h_parts, tile = lax.optimization_barrier((v_own, h_parts, tile))
    v_other = to_core(v_own)
    block, half, parts = ((NEIG, LANES), F32), ((STACK, HALF), BF16), ((2, STACK, HALF), BF16)
    half_vmem, parts_vmem = pltpu.VMEM(*half), pltpu.VMEM(*parts)
    h_vmem = pltpu.VMEM((2, PARTS * TALL, HALF), BF16)
    h_half = pltpu.VMEM((PARTS * TALL, HALF), BF16)
    dma = pltpu.SemaphoreType.DMA
    product, h_next = kernel_call(
        image_own_kernel,
        [((PARTS * TALL, 2 * STACK), F32), ((PARTS * TALL, HALF), BF16)],
        (h_parts, v_own),
        1 << 30,
        "image_own",
        [h_half, pltpu.VMEM((2 * STACK, HALF), BF16), dma((2,))], (0,), limit=LIMIT_IMAGE,
    )
    image, sent = kernel_call(
        image_other_kernel, [block, ((CHIPS, NEIG, LANES), F32)], (h_next, v_other, product, tile), 1 << 30, "image_other",
        [half_vmem], limit=LIMIT_IMAGE,
    )
    i_own = to_chips(sent, 1)
    p_image, c_parts, p_parts, first = kernel_call(
        previous_kernel,
        [block, ((3, STACK, HALF), BF16), ((3, STACK, HALF), BF16), ((2 * NEIG, 2 * NEIG), F32)],
        (h_parts, v_own, v_other, product),
        6 << 30,
        "previous",
        [h_half, parts_vmem, parts_vmem, dma((3,))], (0,), (1, 2),
    )
    i_own, p_image, c_parts = lax.optimization_barrier((i_own, p_image, c_parts))
    i_other = to_core(i_own)
    i_own_parts, x_own, half_cross, diag = kernel_call(
        own_kernel,
        [half, ((NEIG, HALF), F32), ((STACK, STACK), F32), ((1, HALF), F32)],
        (i_own, c_parts),
        1 << 30,
        "own",
        [half_vmem, dma(())], (1,), limit=LIMIT_OWN,
    )
    search, rms, cross, sent, kept = kernel_call(
        search_kernel,
        [block, ((NEIG,), F32), ((NEIG, NEIG), F32), ((CHIPS, 8, LANES), F32), ((4, STACK, HALF), BF16)],
        (h_parts, x_own, i_other, c_parts, i_own_parts, half_cross, diag, cvec, pvec, p_image, image, tile),
        6 << 30,
        "search",
        [h_vmem, parts_vmem, half_vmem, parts_vmem, pltpu.VMEM((2, NEIG, HALF), F32), pltpu.VMEM((1, HALF), F32), dma((3,)), dma((2,)), dma(())],
        (0, 3), (4,), limit=LIMIT_SEARCH,
    )
    r_own = to_chips(sent, 2)
    square = ((3 * NEIG, 3 * NEIG), F32)
    inverse, stiff = kernel_call(
        factor_kernel, [square, square], (kept, c_parts, p_parts, first, cross), 6 << 30, "factor",
        [pltpu.VMEM((2, 4 * STACK, HALF), BF16), dma((2, 4))], (0, 1, 2),
    )
    r_own, inverse = lax.optimization_barrier((r_own, inverse))
    r_other = to_core(r_own)
    new_current, new_previous = kernel_call(
        finish_kernel,
        [((NEIG, ROWS), F32)] * 2,
        (inverse, stiff, r_own, r_other, cvec, search, pvec),
        1 << 28,
        "finish",
        limit=8 << 20,
    )
    return new_current.T, new_previous.T, rms


def solution(mesh):
    line = Mesh(mesh.devices.reshape(DEVICES), (AXIS,))
    return jax.shard_map(
        body,
        mesh=line,
        in_specs=(P(AXIS, None), P(AXIS, None), P(AXIS, None)),
        out_specs=(P(AXIS, None), P(AXIS, None), P()),
        check_vma=False,
    )
```

```python
import math

import jax
import jax.numpy as jnp
from jax import lax
from jax.experimental import pallas as pl
from jax.experimental.pallas import tpu as pltpu
from jax.sharding import Mesh
from jax.sharding import PartitionSpec as P

NEIG = 16
SIGN_STEPS = 6
ORDER = 13824
DEVICES = 128
ROWS = ORDER // DEVICES
CHIPS = DEVICES // 2
LANES = 128
FORWARD = list(range(CHIPS))
BACKWARD = [16 * (p % 4) + 4 * (p // 16) + (p // 4) % 4 for p in FORWARD[::-1]]
ORDERS = (BACKWARD, BACKWARD, BACKWARD)
SLOTS = [[order.index(chip) for chip in range(CHIPS)] for order in ORDERS]
HALF = CHIPS * ROWS
TALL = 112
CHUNKS = 2
CHUNK = HALF // CHUNKS
EPS = 1e-06
AXIS = "device"

F32, BF16 = jnp.float32, jnp.bfloat16
HIGHEST = lax.Precision.HIGHEST
VMEM = pl.BlockSpec(memory_space=pltpu.VMEM)
HBM = pl.BlockSpec(memory_space=pltpu.HBM)
LIMIT = 53 << 20
LIMIT_IMAGE = 48 << 20
LIMIT_SEARCH = 54525952
LIMIT_OWN = 54001664
PARTS = 2
STACK = PARTS * NEIG
SPARE = ROWS


def split(x):
    high = x.astype(BF16)
    return high, (x - high.astype(F32)).astype(BF16)


def split3(x):
    high = x.astype(BF16)
    rest = x - high.astype(F32)
    mid = rest.astype(BF16)
    return high, mid, (rest - mid.astype(F32)).astype(BF16)


def nt(left, right):
    return lax.dot_general(left, right, (((1,), (1,)), ((), ())), preferred_element_type=F32)


def nt_exact(left, right):
    return lax.dot_general(left, right, (((1,), (1,)), ((), ())), precision=HIGHEST, preferred_element_type=F32)


def dot_exact(left, right):
    return jnp.dot(left, right, precision=HIGHEST, preferred_element_type=F32)


def fold(parts):
    rows = parts[16:32] + parts[0:16]
    return rows[:, 16:32] + rows[:, 0:16]


def fold_rows(product):
    rows = product[TALL:] + product[:TALL]
    wide = jnp.concatenate([rows, jnp.zeros((TALL, LANES - STACK), F32)], axis=1)
    turned = jnp.concatenate([wide, jnp.zeros((LANES - TALL, LANES), F32)], axis=0).T
    return real_lanes(turned[16:32] + turned[0:16])


def real_lanes(tile):
    lane = lax.broadcasted_iota(jnp.int32, tile.shape, 1)
    return jnp.where(lane < ROWS, tile, 0.0)


def prepare_kernel(h_ref, parts_ref):
    core = lax.rem(lax.axis_index(AXIS), 2)
    for owner in range(2):
        half = jnp.where(core == owner, 0, 1)
        starts = [ROWS * (2 * chip + owner) for chip in range(CHIPS // CHUNKS)]
        x = jnp.concatenate([h_ref[:, start : start + ROWS] for start in starts], axis=1)
        for number, part in enumerate(split(x)):
            parts_ref[half, TALL * number : TALL * number + ROWS, :] = part


def prepare(hamiltonian):
    return pl.pallas_call(
        prepare_kernel,
        grid=(CHUNKS,),
        out_shape=jax.ShapeDtypeStruct((2, PARTS * TALL, HALF), BF16),
        in_specs=[pl.BlockSpec((ROWS, ORDER // CHUNKS), lambda i: (0, i))],
        out_specs=pl.BlockSpec((2, PARTS * TALL, CHUNK), lambda i: (0, 0, i)),
        compiler_params=pltpu.CompilerParams(vmem_limit_bytes=58 << 20),
        cost_estimate=pl.CostEstimate(flops=20 * ROWS * ORDER, bytes_accessed=10 * ROWS * ORDER, transcendentals=0),
        name="prepare",
    )(hamiltonian)


def started(source, target, sem):
    copy = pltpu.make_async_copy(source, target, sem)
    copy.start()
    return copy


def packed(tile_of):
    return jnp.concatenate([tile_of(chip)[:, :ROWS] for chip in range(CHIPS)], axis=1)


def store_parts(x, parts_ref):
    for number, part in enumerate(split(x)):
        parts_ref[NEIG * number : NEIG * (number + 1), :] = part


def take_parts(tile_of, parts_ref):
    store_parts(packed(tile_of), parts_ref)


def take_both(tile_of, first_ref, second_ref):
    x = packed(tile_of)
    store_parts(x[:NEIG], first_ref)
    store_parts(x[NEIG:], second_ref)


def stacked_dot(left, right):
    high, low = split(left)
    right_high, right_low = split(right)
    both = jnp.dot(jnp.concatenate([high, low], axis=0), right_high, preferred_element_type=F32)
    size = left.shape[0]
    return both[:size] + (both[size:] + jnp.dot(high, right_low, preferred_element_type=F32))


def eliminated(matrix):
    size = matrix.shape[0]
    row = lax.broadcasted_iota(jnp.int32, (size, size), 0)
    column = lax.broadcasted_iota(jnp.int32, (size, size), 1)
    identity = jnp.where(row == column, 1.0, 0.0).astype(F32)
    work = jnp.concatenate([matrix, identity], axis=1)
    below = lax.broadcasted_iota(jnp.int32, (size, 1), 0)
    for k in range(size):
        factor = jnp.where(below > k, work[:, k : k + 1] / work[k : k + 1, k : k + 1], 0.0)
        work = work - factor * work[k : k + 1, :]
    pivots = jnp.sum(work[:, :size] * identity, axis=1, keepdims=True)
    return work[:, size:] / jnp.sqrt(pivots)


def joined(blocks):
    return jnp.concatenate([jnp.concatenate(row, axis=1) for row in blocks], axis=0)


def image_own_kernel(h_ref, own_ref, product_ref, next_ref, h_vmem, parts, sems):
    copy = started(h_ref.at[0], h_vmem, sems.at[0])
    following = started(h_ref.at[1], next_ref, sems.at[1])
    take_both(lambda chip: own_ref[SLOTS[0][chip]], parts.at[pl.ds(0, STACK)], parts.at[pl.ds(STACK, STACK)])
    copy.wait()
    product_ref[...] = nt(h_vmem[...], parts[...])
    following.wait()


def image_other_kernel(h_ref, other_ref, product_ref, tile_ref, image_ref, sent_ref, parts):
    take_parts(lambda chip: other_ref[SLOTS[0][chip], 0:NEIG], parts)
    image = fold_rows(product_ref[:, 0:STACK] + nt(h_ref[...], parts[...]))
    image_ref[...] = image
    sent = image + tile_ref[...]
    for chip in range(CHIPS):
        sent_ref[chip] = sent


def previous_kernel(h_ref, own_ref, other_ref, product_ref, image_ref, c_out, p_out, inverse_ref, h_vmem, c_ref, p_ref, sems):
    copy = started(h_ref.at[1], h_vmem, sems.at[0])
    take_both(lambda chip: own_ref[SLOTS[0][chip]], c_ref.at[0], p_ref.at[0])
    take_both(lambda chip: other_ref[SLOTS[0][chip]], c_ref.at[1], p_ref.at[1])
    out_c = started(c_ref, c_out.at[pl.ds(0, 2)], sems.at[1])
    out_p = started(p_ref, p_out.at[pl.ds(0, 2)], sems.at[2])
    cc = fold(nt(c_ref[0], c_ref[0]) + nt(c_ref[1], c_ref[1]))
    pc = fold(nt(p_ref[0], c_ref[0]) + nt(p_ref[1], c_ref[1]))
    pp = fold(nt(p_ref[0], p_ref[0]) + nt(p_ref[1], p_ref[1]))
    empty = jnp.zeros((NEIG, NEIG), F32)
    low = joined([[0.5 * cc, empty], [pc, 0.5 * pp]])
    copy.wait()
    image_ref[...] = fold_rows(product_ref[:, STACK:] + nt(h_vmem[...], p_ref[1]))
    inverse_ref[...] = eliminated(low + low.T)
    out_c.wait()
    out_p.wait()


def diagonal_of(tile):
    row = lax.broadcasted_iota(jnp.int32, (NEIG, LANES), 0)
    lane = lax.broadcasted_iota(jnp.int32, (NEIG, LANES), 1)
    spread = jnp.take_along_axis(tile, SPARE + lane // NEIG, axis=1)
    return jnp.sum(jnp.where(lane % NEIG == row, spread, 0.0), axis=0, keepdims=True)


def own_kernel(own_ref, c_hbm, i_ref, x_ref, cross_ref, diag_ref, c_ref, sem):
    copy = started(c_hbm.at[0], c_ref, sem)
    x = packed(lambda chip: own_ref[SLOTS[1][chip]])
    x_ref[...] = x
    store_parts(x, i_ref)
    diag_ref[...] = packed(lambda chip: diagonal_of(own_ref[SLOTS[1][chip]]))
    copy.wait()
    cross_ref[...] = nt(i_ref[...], c_ref[...])


def search_kernel(
    h_ref, x_own_ref, other_ref, c_hbm, i_own_ref, half_cross_ref, diag_ref, cvec_ref, pvec_ref, pimage_ref, image_ref, tile_ref,
    search_ref, rms_ref, cross_ref, sent_ref, kept_ref,
    h_vmem, c_ref, i_ref, s_ref, resid_ref, other_diag_ref, sems, h_sems, c_sem,
):
    copy_c = started(c_hbm.at[pl.ds(0, 2)], c_ref, c_sem)
    copies = [started(h_ref.at[half], h_vmem.at[half], h_sems.at[half]) for half in range(2)]
    x_other = packed(lambda chip: other_ref[SLOTS[1][chip]])
    resid_ref[1] = x_other
    store_parts(x_other, i_ref)
    other_diag_ref[...] = packed(lambda chip: diagonal_of(other_ref[SLOTS[1][chip]]))
    copy_c.wait()
    kept = [started(i_own_ref, kept_ref.at[2], sems.at[1]), started(i_ref, kept_ref.at[3], sems.at[2])]
    cross_t = fold(half_cross_ref[...] + nt(i_ref[...], c_ref[1]))
    cross_ref[...] = cross_t
    ritz_t = cross_t / ORDER
    stacked = jnp.concatenate(split3(ritz_t), axis=0)
    stacked = jnp.concatenate([stacked] * PARTS, axis=1)
    square = jnp.zeros((NEIG, 1), F32)
    for half, ref in ((0, x_own_ref), (1, resid_ref.at[1])):
        moved = jnp.dot(stacked, c_ref[half], preferred_element_type=F32)
        moved = (moved[32:48] + moved[16:32]) + moved[0:16]
        resid = ref[...] - moved
        resid_ref[half] = resid
        square = square + jnp.sum(resid * resid, axis=1, keepdims=True)
    rms = jnp.sqrt(square / ORDER + EPS)
    row = lax.broadcasted_iota(jnp.int32, (NEIG, NEIG), 0)
    column = lax.broadcasted_iota(jnp.int32, (NEIG, NEIG), 1)
    rms_ref[...] = jnp.sum(jnp.where(row == column, rms, 0.0), axis=0)
    value = jnp.sum(jnp.where(row == column, ritz_t, 0.0), axis=1, keepdims=True)

    def scaled(resid, diag):
        return resid / (jnp.maximum(jnp.abs(diag - value), 1.0) * rms)

    resid = image_ref[...] - dot_exact(ritz_t, cvec_ref[...])
    search = scaled(resid, diagonal_of(tile_ref[...]))
    search_ref[...] = search
    for half, diag in ((0, diag_ref), (1, other_diag_ref)):
        store_parts(scaled(resid_ref[half], diag[...]), s_ref.at[half])
    kept.append(started(s_ref, kept_ref.at[pl.ds(0, 2)], sems.at[0]))
    copies[0].wait()
    product = nt(h_vmem[0], s_ref[0])
    copies[1].wait()
    simage = fold_rows(product + nt(h_vmem[1], s_ref[1]))
    pvec = pvec_ref[...]
    terms = jnp.concatenate(
        [
            nt_exact(simage, jnp.concatenate([search, pvec], axis=0)),
            nt_exact(pimage_ref[...], pvec),
            jnp.zeros((NEIG, NEIG), F32),
        ],
        axis=1,
    )
    message = jnp.concatenate([terms[0:8], terms[8:16]], axis=1)
    for chip in range(CHIPS):
        sent_ref[chip] = message
    for copy in kept:
        copy.wait()


def factor_kernel(kept_hbm, c_hbm, p_hbm, first_ref, cross_ref, inverse_ref, stiff_ref, all_ref, sems):
    copies = []
    for half in range(2):
        for number, source in enumerate((kept_hbm.at[half], kept_hbm.at[2 + half], c_hbm.at[half], p_hbm.at[half])):
            copies.append(started(source, all_ref.at[half, pl.ds(STACK * number, STACK)], sems.at[half, number]))
    products = None
    for half in range(2):
        for copy in copies[4 * half : 4 * half + 4]:
            copy.wait()
        terms = nt(all_ref[half], all_ref[half, : 2 * STACK])
        products = terms if half == 0 else products + terms
    with_search, p_image = products[:, :STACK], products[3 * STACK :, STACK:]
    ss, i_s, cs, ps = [fold(with_search[STACK * n : STACK * (n + 1)]) for n in range(4)]
    first = first_ref[...]
    row = nt_exact(jnp.concatenate([cs.T, ps.T], axis=1), first)
    last = eliminated(ss - nt_exact(row, row))
    inverse_ref[...] = joined(
        [[first, jnp.zeros((2 * NEIG, NEIG), F32)], [-dot_exact(last, dot_exact(row, first)), last]]
    )
    empty = jnp.zeros((NEIG, NEIG), F32)
    low = joined([[0.5 * cross_ref[...], empty, i_s], [fold(p_image), empty, empty], [empty, empty, empty]])
    stiff_ref[...] = low + low.T


def finish_kernel(inverse_ref, stiff_ref, own_ref, other_ref, c_ref, s_ref, p_ref, current_ref, previous_ref):
    size = 3 * NEIG
    total = own_ref[0] + other_ref[0]
    for chip in range(1, CHIPS):
        total = total + (own_ref[chip] + other_ref[chip])
    terms = jnp.concatenate([total[:, 0 : 3 * NEIG], total[:, 4 * NEIG : 7 * NEIG]], axis=0)
    ss, sp, pp = terms[:, 0:16], terms[:, 16:32], terms[:, 32:48]
    empty = jnp.zeros((NEIG, NEIG), F32)
    low = joined([[empty, empty, empty], [empty, 0.5 * pp, empty], [empty, sp, 0.5 * ss]])
    stiff = stiff_ref[...] + (low + low.T)
    inverse = inverse_ref[...]
    basis = jnp.concatenate([c_ref[...], p_ref[...], s_ref[...]], axis=0)
    rotated = dot_exact(inverse, basis)
    rotated_rest = dot_exact(jnp.where(lax.broadcasted_iota(jnp.int32, (size, size), 1) < NEIG, 0.0, inverse), basis)
    reduced = nt_exact(dot_exact(inverse, stiff), inverse)
    row = lax.broadcasted_iota(jnp.int32, (size, size), 0)
    column = lax.broadcasted_iota(jnp.int32, (size, size), 1)
    identity = jnp.where(row == column, 1.0, 0.0).astype(F32)
    diagonal = jnp.sum(reduced * identity, axis=1, keepdims=True)
    level = jnp.max(diagonal[:NEIG], axis=0, keepdims=True)
    signed = level * identity - reduced
    square = stacked_dot(signed, signed)
    total = jnp.sum(jnp.sum(signed * signed, axis=1, keepdims=True), axis=0, keepdims=True)
    square = square / total
    signed = signed / jnp.sqrt(total)
    for step in range(SIGN_STEPS):
        if step > 0:
            square = stacked_dot(signed, signed)
        signed = stacked_dot(signed, 1.5 * identity - 0.5 * square)
    projector = 0.5 * (identity + signed)
    wanted = jnp.where(column < NEIG, projector, 0.0) * math.sqrt(ORDER)
    applied = lax.dot_general(
        wanted, jnp.concatenate([rotated, rotated_rest], axis=1), (((0,), (0,)), ((), ())), precision=HIGHEST, preferred_element_type=F32
    )
    current_ref[...] = applied[:NEIG, :ROWS]
    previous_ref[...] = applied[:NEIG, LANES : LANES + ROWS]


def kernel_call(body, outs, args, flops, name, scratch=(), in_hbm=(), out_hbm=(), limit=LIMIT):
    return pl.pallas_call(
        body,
        out_shape=[jax.ShapeDtypeStruct(shape, kind) for shape, kind in outs],
        in_specs=[HBM if n in in_hbm else VMEM for n in range(len(args))],
        out_specs=[HBM if n in out_hbm else VMEM for n in range(len(outs))],
        scratch_shapes=scratch,
        compiler_params=pltpu.CompilerParams(vmem_limit_bytes=limit),
        cost_estimate=pl.CostEstimate(flops=flops, bytes_accessed=4 << 20, transcendentals=0),
        name=name,
    )(*args)


def to_chips(x, number):
    groups = [[2 * chip + core for chip in ORDERS[number]] for core in range(2)]
    return lax.all_to_all(x, AXIS, 0, 0, axis_index_groups=groups, tiled=True)


def to_core(x):
    return lax.ppermute(x, AXIS, [(device, device ^ 1) for device in range(DEVICES)])


def diagonal_tile(hamiltonian):
    device = lax.axis_index(AXIS)
    own_block = lax.dynamic_slice_in_dim(hamiltonian, device * ROWS, ROWS, 1)
    index = jnp.arange(ROWS)
    diag = jnp.sum(jnp.where(index[:, None] == index[None, :], own_block, 0.0), axis=0)
    rows = jnp.where(index[None, :] % NEIG == jnp.arange(NEIG)[:, None], diag[None, :], 0.0)
    lanes = (jnp.arange(LANES)[None, :] == SPARE + index[:, None] // NEIG).astype(F32)
    return dot_exact(rows, lanes)


def body(hamiltonian, current, previous):
    both = jnp.concatenate([current.T, previous.T], axis=0)
    v_own = to_chips(jnp.broadcast_to(both[None], (CHIPS, 2 * NEIG, ROWS)), 0)
    tile = diagonal_tile(hamiltonian)
    cvec = jnp.pad(current.T, ((0, 0), (0, LANES - ROWS)))
    pvec = jnp.pad(previous.T, ((0, 0), (0, LANES - ROWS)))
    h_parts = prepare(hamiltonian)
    v_own, h_parts, tile = lax.optimization_barrier((v_own, h_parts, tile))
    v_other = to_core(v_own)
    block, half, parts = ((NEIG, LANES), F32), ((STACK, HALF), BF16), ((2, STACK, HALF), BF16)
    half_vmem, parts_vmem = pltpu.VMEM(*half), pltpu.VMEM(*parts)
    h_vmem = pltpu.VMEM((2, PARTS * TALL, HALF), BF16)
    h_half = pltpu.VMEM((PARTS * TALL, HALF), BF16)
    dma = pltpu.SemaphoreType.DMA
    product, h_next = kernel_call(
        image_own_kernel,
        [((PARTS * TALL, 2 * STACK), F32), ((PARTS * TALL, HALF), BF16)],
        (h_parts, v_own),
        1 << 30,
        "image_own",
        [h_half, pltpu.VMEM((2 * STACK, HALF), BF16), dma((2,))], (0,), limit=LIMIT_IMAGE,
    )
    image, sent = kernel_call(
        image_other_kernel, [block, ((CHIPS, NEIG, LANES), F32)], (h_next, v_other, product, tile), 1 << 30, "image_other",
        [half_vmem], limit=LIMIT_IMAGE,
    )
    i_own = to_chips(sent, 1)
    p_image, c_parts, p_parts, first = kernel_call(
        previous_kernel,
        [block, ((3, STACK, HALF), BF16), ((3, STACK, HALF), BF16), ((2 * NEIG, 2 * NEIG), F32)],
        (h_parts, v_own, v_other, product),
        6 << 30,
        "previous",
        [h_half, parts_vmem, parts_vmem, dma((3,))], (0,), (1, 2),
    )
    i_own, p_image, c_parts = lax.optimization_barrier((i_own, p_image, c_parts))
    i_other = to_core(i_own)
    i_own_parts, x_own, half_cross, diag = kernel_call(
        own_kernel,
        [half, ((NEIG, HALF), F32), ((STACK, STACK), F32), ((1, HALF), F32)],
        (i_own, c_parts),
        1 << 30,
        "own",
        [half_vmem, dma(())], (1,), limit=LIMIT_OWN,
    )
    search, rms, cross, sent, kept = kernel_call(
        search_kernel,
        [block, ((NEIG,), F32), ((NEIG, NEIG), F32), ((CHIPS, 8, LANES), F32), ((4, STACK, HALF), BF16)],
        (h_parts, x_own, i_other, c_parts, i_own_parts, half_cross, diag, cvec, pvec, p_image, image, tile),
        6 << 30,
        "search",
        [h_vmem, parts_vmem, half_vmem, parts_vmem, pltpu.VMEM((2, NEIG, HALF), F32), pltpu.VMEM((1, HALF), F32), dma((3,)), dma((2,)), dma(())],
        (0, 3), (4,), limit=LIMIT_SEARCH,
    )
    r_own = to_chips(sent, 2)
    square = ((3 * NEIG, 3 * NEIG), F32)
    inverse, stiff = kernel_call(
        factor_kernel, [square, square], (kept, c_parts, p_parts, first, cross), 6 << 30, "factor",
        [pltpu.VMEM((2, 4 * STACK, HALF), BF16), dma((2, 4))], (0, 1, 2),
    )
    r_own, inverse = lax.optimization_barrier((r_own, inverse))
    r_other = to_core(r_own)
    new_current, new_previous = kernel_call(
        finish_kernel,
        [((NEIG, ROWS), F32)] * 2,
        (inverse, stiff, r_own, r_other, cvec, search, pvec),
        1 << 28,
        "finish",
        limit=8 << 20,
    )
    return new_current.T, new_previous.T, rms


def solution(mesh):
    line = Mesh(mesh.devices.reshape(DEVICES), (AXIS,))
    return jax.shard_map(
        body,
        mesh=line,
        in_specs=(P(AXIS, None), P(AXIS, None), P(AXIS, None)),
        out_specs=(P(AXIS, None), P(AXIS, None), P()),
        check_vma=False,
    )
```
